256 devices in a mesh: segment: 2 (over core), tensor: 16 (over x, z_hi), dp: 8 (over z_lo, y).
Axes of the slice: x: 4, y: 4, z: 8 (z_hi: 4, z_lo: 2; z = z_hi * 2 + z_lo), core: 2. Of those that a mesh axis runs over, the one named last changes fastest.
Arguments:
- tokens: bfloat16 [1024, 1536], P('dp', 'tensor'), may hold values from -6 to 6
- w_gate: bfloat16 [2, 1536, 12288], P('segment', None, 'tensor'), may hold values from -0.15625 to 0.15625
- w_up: bfloat16 [2, 1536, 12288], P('segment', None, 'tensor'), may hold values from -0.15625 to 0.15625
- w_down: bfloat16 [2, 12288, 1536], P('segment', 'tensor'), may hold values from -0.0546875 to 0.0546875
- cotangent: bfloat16 [1024, 1536], P('dp', 'tensor'), may hold values from -0.1796875 to 0.1796875
Outputs:
- grad_gate: float32 [2, 1536, 12288], P('segment', 'dp', 'tensor')
- grad_up: float32 [2, 1536, 12288], P('segment', 'dp', 'tensor')
- grad_down: float32 [2, 12288, 1536], P('segment', 'tensor', 'dp')
The draws below stay inside these ranges and needn't reach their ends.
All inputs are finite; a program needn't handle non-finite values.
Results may differ from the reference program's by a relative error of at most 0.023.
Values may be sent and summed in bfloat16 or wider, within the bound.
No kernel may reach another device: no remote copies, remote signals or barrier semaphores. Data moves between devices by JAX's collectives and lax.ppermute only.
A program may use at most 64 MiB of HBM per device.

```python
import jax
import jax.numpy as jnp
from jax import lax

D = 1536
FF = 12288
TOKENS = 1024
N_DP = 8


def with_spikes(array, key, source, target, parts, factor):
    owner, partner = [(jnp.arange(array.shape[dim]) // (array.shape[dim] // parts)).reshape([-1 if axis == dim else 1 for axis in range(array.ndim)]) for dim in (source, target)]
    chosen = jax.random.permutation(key, parts)[partner]
    strong = (owner == chosen) | (owner == (partner + parts // 2) % parts)
    return jnp.where(strong, factor * array, array)


def block_scale(rng, shape, shards, low, largest):
    def one(dim, shards_of):
        heights = jax.random.uniform(jax.random.fold_in(jax.random.fold_in(rng, 6), dim), (shards_of,), jnp.float32, low / len(shards), largest / len(shards))
        return jnp.repeat(jnp.exp(heights), shape[dim] // shards_of).reshape((-1,) + (1,) * (len(shape) - dim - 1))

    gain = one(*shards[0])
    for cut in shards[1:]:
        gain = gain * one(*cut)
    return gain


def normal_values(stream_key, shape, spread, bound, pieces=(), held_as=jnp.bfloat16):
    drawn = spread * jax.random.normal(stream_key, shape, jnp.float32)
    if pieces:
        drawn = drawn * block_scale(stream_key, shape, pieces, -0.22, 0.18)
    return jnp.clip(drawn, -bound, bound).astype(held_as)


def noise_with(stream_key, shape, deviation, reach, pieces, heavy, kind=jnp.bfloat16):
    entries = deviation * jax.random.normal(stream_key, shape, jnp.float32)
    if pieces:
        entries = entries * block_scale(stream_key, shape, pieces, -0.22, 0.18)
    return jnp.clip(with_spikes(entries, jax.random.fold_in(stream_key, 3), *heavy), -reach, reach).astype(kind)


def setup_inputs(seed: int = 0) -> dict:
    key_of = jax.random.split(jax.random.key(seed), 6)
    return {
        "tokens": normal_values(key_of[0], (TOKENS, D), 1.0, 6.0, ((0, 8), (1, 16))),
        "w_gate": normal_values(key_of[1], (2, D, FF), D ** -0.5, 0.15625, ((0, 2), (2, 16))),
        "w_up": normal_values(key_of[2], (2, D, FF), D ** -0.5, 0.15625, ((0, 2), (2, 16))),
        "w_down": normal_values(key_of[3], (2, FF, D), FF ** -0.5, 0.0546875, ((0, 2), (1, 16))),
        "cotangent": noise_with(key_of[4], (TOKENS, D), 0.03, 0.1796875, ((0, 8), (1, 16)), (0, 1, 16, 2.0)),
    }


def layer_forward(acts, gate_weight, up_weight, down_weight):
    gate_store = jnp.dot(acts, gate_weight, preferred_element_type=jnp.float32).astype(jnp.bfloat16)
    up_store = jnp.dot(acts, up_weight, preferred_element_type=jnp.float32).astype(jnp.bfloat16)
    gate_value = gate_store.astype(jnp.float32)
    up_value = up_store.astype(jnp.float32)
    hidden = (jax.nn.silu(gate_value) * up_value).astype(jnp.bfloat16)
    mixed_sum = jnp.dot(hidden, down_weight, preferred_element_type=jnp.float32)
    layer_out = (acts.astype(jnp.float32) + mixed_sum).astype(jnp.bfloat16)
    return layer_out, gate_value, up_value, hidden


def layer_backward(acts, gate_value, up_value, hidden, upstream, gate_weight, up_weight, down_weight):
    d_hidden = jnp.dot(upstream, down_weight.T, preferred_element_type=jnp.float32)
    sigma = jax.nn.sigmoid(gate_value)
    d_gate = (d_hidden * up_value * sigma * (1.0 + gate_value * (1.0 - sigma))).astype(jnp.bfloat16)
    d_up = (d_hidden * gate_value * sigma).astype(jnp.bfloat16)
    grad_gate = jnp.dot(acts.T, d_gate, preferred_element_type=jnp.float32)
    grad_up = jnp.dot(acts.T, d_up, preferred_element_type=jnp.float32)
    grad_down = jnp.dot(hidden.T, upstream, preferred_element_type=jnp.float32)
    inner = jnp.dot(d_gate, gate_weight.T, preferred_element_type=jnp.float32)
    inner = inner + jnp.dot(d_up, up_weight.T, preferred_element_type=jnp.float32)
    d_input = (upstream.astype(jnp.float32) + inner).astype(jnp.bfloat16)
    return d_input, grad_gate, grad_up, grad_down


def rounded(value):
    return lax.optimization_barrier(value.astype(jnp.bfloat16)).astype(jnp.float32)


def reference(tokens, w_gate, w_up, w_down, cotangent):
    per_replica = tokens.shape[0] // N_DP
    token_blocks = tokens.reshape(N_DP, per_replica, D)
    cot_blocks = cotangent.reshape(N_DP, per_replica, D)

    def replica(carry, item):
        acts, upstream = item
        middle, gate0, up0, hidden0 = layer_forward(acts, w_gate[0], w_up[0], w_down[0])
        final, gate1, up1, hidden1 = layer_forward(middle, w_gate[1], w_up[1], w_down[1])
        back1, gg1, gu1, gd1 = layer_backward(middle, gate1, up1, hidden1, upstream, w_gate[1], w_up[1], w_down[1])
        back0, gg0, gu0, gd0 = layer_backward(acts, gate0, up0, hidden0, back1, w_gate[0], w_up[0], w_down[0])
        sum_gate = carry[0] + rounded(jnp.stack([gg0, gg1]))
        sum_up = carry[1] + rounded(jnp.stack([gu0, gu1]))
        sum_down = carry[2] + rounded(jnp.stack([gd0, gd1]))
        return (sum_gate, sum_up, sum_down), None

    start = (jnp.zeros((2, D, FF), jnp.float32), jnp.zeros((2, D, FF), jnp.float32), jnp.zeros((2, FF, D), jnp.float32))
    totals, unused = lax.scan(replica, start, (token_blocks, cot_blocks))
    return totals[0], totals[1], totals[2]
```

```python
import jax
import jax.numpy as jnp
from jax import lax
from jax.sharding import PartitionSpec as P

MICRO = 1


def sent_to_all(value, axis):
    copies = jnp.broadcast_to(value, (lax.axis_size(axis), *value.shape))
    return lax.all_to_all(copies, axis, split_axis=0, concat_axis=0, tiled=True)


def joined_along(blocks, dim):
    shape = list(blocks.shape[1:])
    shape[dim] *= blocks.shape[0]
    return jnp.moveaxis(blocks, 0, dim).reshape(shape)


def gather_directly(value, axis, dim):
    blocks = sent_to_all(value, axis)
    return joined_along(blocks, dim)


def in_blocks(value, dim, peers):
    shape = value.shape
    blocks = value.reshape(*shape[:dim], peers, shape[dim] // peers, *shape[dim + 1 :])
    return jnp.moveaxis(blocks, dim, 0)


def sent_and_summed(value, axis, dim):
    peers = lax.axis_size(axis)
    blocks = lax.all_to_all(in_blocks(value, dim, peers), axis, 0, 0, tiled=True)
    return jnp.sum(blocks.astype(jnp.float32), axis=0)


def from_behind(block, axis, distance):
    devices = range(lax.axis_size(axis))
    route = [(i - distance, i) for i in devices if i - distance in devices]
    return lax.ppermute(block, axis, route)


def select_tick(stored, position):
    if 0 <= position < len(stored):
        return stored[position]
    return jnp.zeros_like(stored[0])


def inner_rows(left, right):
    return lax.dot_general(
        left, right, (((0,), (0,)), ((), ())), preferred_element_type=jnp.float32
    )


def against_cols(left, right):
    return lax.dot_general(
        left, right, (((1,), (1,)), ((), ())), preferred_element_type=jnp.float32
    )


def local(tokens, w_gate, w_up, w_down, cotangent):
    gate_weight = w_gate[0]
    up_weight = w_up[0]
    down_weight = w_down[0]
    leading = lax.axis_index("segment") == 0
    row_count = tokens.shape[0] // MICRO
    hidden_cols = gate_weight.shape[1]
    blank_rows = jnp.zeros((row_count, tokens.shape[1]), jnp.bfloat16)
    received = blank_rows
    gathers = []
    gates = []
    ups = []
    for moment in range(MICRO + 1):
        fresh_rows = (
            tokens[moment * row_count : (moment + 1) * row_count] if moment < MICRO else blank_rows
        )
        inputs = jnp.where(leading, fresh_rows, received)
        gathered = gather_directly(inputs, "tensor", 1)
        gate_store = jnp.dot(gathered, gate_weight, preferred_element_type=jnp.float32).astype(
            jnp.bfloat16
        )
        up_store = jnp.dot(gathered, up_weight, preferred_element_type=jnp.float32).astype(
            jnp.bfloat16
        )
        hidden = (
            jax.nn.silu(gate_store.astype(jnp.float32)) * up_store.astype(jnp.float32)
        ).astype(jnp.bfloat16)
        partial_value = jnp.dot(hidden, down_weight, preferred_element_type=jnp.float32)
        mixed_sum = sent_and_summed(partial_value.astype(jnp.bfloat16), "tensor", 1)
        output = (inputs.astype(jnp.float32) + mixed_sum).astype(jnp.bfloat16)
        gathers.append(gathered)
        gates.append(gate_store)
        ups.append(up_store)
        if moment < MICRO:
            received = from_behind(output, "segment", 1)
    received_back = blank_rows
    records = []
    for moment in range(MICRO + 1):
        fresh_rows = (
            cotangent[moment * row_count : (moment + 1) * row_count]
            if moment < MICRO
            else blank_rows
        )
        upstream = jnp.where(leading, received_back, fresh_rows)
        gathered = jnp.where(
            leading, select_tick(gathers, moment - 1), select_tick(gathers, moment + 1)
        )
        gate_store = jnp.where(
            leading, select_tick(gates, moment - 1), select_tick(gates, moment + 1)
        )
        up_store = jnp.where(leading, select_tick(ups, moment - 1), select_tick(ups, moment + 1))
        gate_value = gate_store.astype(jnp.float32)
        up_value = up_store.astype(jnp.float32)
        hidden = (jax.nn.silu(gate_value) * up_value).astype(jnp.bfloat16)
        cot_full = gather_directly(upstream, "tensor", 1)
        d_hidden = against_cols(cot_full, down_weight)
        sigma = jax.nn.sigmoid(gate_value)
        d_gate = (d_hidden * up_value * sigma * (1.0 + gate_value * (1.0 - sigma))).astype(
            jnp.bfloat16
        )
        d_up = (d_hidden * gate_value * sigma).astype(jnp.bfloat16)
        records.append((gathered, d_gate, d_up, cot_full, hidden))
        if moment < MICRO:
            partial_value = against_cols(d_gate, gate_weight) + against_cols(d_up, up_weight)
            summed = sent_and_summed(partial_value.astype(jnp.bfloat16), "tensor", 1)
            d_input = (upstream.astype(jnp.float32) + summed).astype(jnp.bfloat16)
            received_back = from_behind(d_input, "segment", -1)
    all_gathered = jnp.concatenate([entry[0] for entry in records], axis=0)
    all_gate = jnp.concatenate([entry[1] for entry in records], axis=0)
    all_up = jnp.concatenate([entry[2] for entry in records], axis=0)
    all_cot = jnp.concatenate([entry[3] for entry in records], axis=0)
    all_hidden = jnp.concatenate([entry[4] for entry in records], axis=0)
    reduced = lax.psum_scatter(
        jnp.concatenate(
            [
                inner_rows(all_gathered, all_gate),
                inner_rows(all_gathered, all_up),
                inner_rows(all_cot, all_hidden),
            ],
            axis=1,
        ).astype(jnp.bfloat16),
        "dp",
        scatter_dimension=0,
        tiled=True,
    ).astype(jnp.float32)
    grad_gate = reduced[:, :hidden_cols][None]
    grad_up = reduced[:, hidden_cols : 2 * hidden_cols][None]
    grad_down = reduced[:, 2 * hidden_cols :].T[None]
    return (grad_gate, grad_up, grad_down)


def solution(mesh):
    in_specs = (
        P("dp", "tensor"),
        P("segment", None, "tensor"),
        P("segment", None, "tensor"),
        P("segment", "tensor", None),
        P("dp", "tensor"),
    )
    out_specs = (
        P("segment", "dp", "tensor"),
        P("segment", "dp", "tensor"),
        P("segment", "tensor", "dp"),
    )
    return jax.shard_map(local, mesh=mesh, in_specs=in_specs, out_specs=out_specs, check_vma=False)
```

```python
import jax
import jax.numpy as jnp
from jax import lax
from jax.experimental import pallas as pl
from jax.experimental.pallas import tpu as pltpu
from jax.sharding import Mesh, PartitionSpec as P

CORES = 2
XS = 4
ZH = 4
ZL = 2
YS = 4
PEERS = ZL * YS
LANES = 128
TENSOR = ("x", "zh")
DP = ("zl", "y")
BF16 = jnp.bfloat16
F32 = jnp.float32


def shifted(value, axis, distance):
    size = lax.axis_size(axis)
    return lax.ppermute(value, axis, [(i, (i + distance) % size) for i in range(size)])


def one_way(value, source):
    return lax.ppermute(value, "segment", [(source, 1 - source)])


def exchanged(value, axes):
    return lax.all_to_all(value, axes, 0, 0, tiled=True)


def dot_tn(left, right):
    return lax.dot_general(left, right, (((0,), (0,)), ((), ())), preferred_element_type=F32)


def dot_nt(left, right):
    return lax.dot_general(left, right, (((1,), (1,)), ((), ())), preferred_element_type=F32)


def dot_nn(left, right):
    return jnp.dot(left, right, preferred_element_type=F32)


def whole(memory_space=pltpu.VMEM):
    return pl.BlockSpec(memory_space=memory_space)


def hidden_of(gate, up):
    gate = gate.astype(F32)
    return (jax.nn.silu(gate) * up.astype(F32)).astype(BF16)


def gate_grads(d_hidden, gate, up):
    gate = gate.astype(F32)
    up = up.astype(F32)
    sigma = jax.nn.sigmoid(gate)
    d_gate = (d_hidden * up * sigma * (1.0 + gate * (1.0 - sigma))).astype(BF16)
    d_up = (d_hidden * gate * sigma).astype(BF16)
    return d_gate, d_up


def limits(mebibytes):
    return pltpu.CompilerParams(vmem_limit_bytes=mebibytes * 2**20)


def columns_at(value, index, width):
    return lax.dynamic_slice_in_dim(value, index * width, width, 1)


def assemble(blocks, x):
    rows, width = blocks[0].shape

    def body(x_ref, *refs):
        out_ref = refs[-1]
        for k in range(XS):
            start = pl.multiple_of(((x_ref[0] + k) % XS) * width, LANES)
            out_ref[:, pl.ds(start, width)] = refs[k][...]

    return pl.pallas_call(
        body,
        in_specs=[whole(pltpu.SMEM)] + [whole()] * XS,
        out_specs=whole(),
        out_shape=jax.ShapeDtypeStruct((rows, width * XS), BF16),
        compiler_params=limits(2),
        name="assemble",
    )(x, *blocks)


def merge(own, other, core):
    rows, width = own.shape

    def body(core_ref, own_ref, other_ref, out_ref):
        start = pl.multiple_of(core_ref[0] * rows, 16)
        out_ref[pl.ds(start, rows), :] = own_ref[...]
        start = pl.multiple_of((1 - core_ref[0]) * rows, 16)
        out_ref[pl.ds(start, rows), :] = other_ref[...]

    return pl.pallas_call(
        body,
        in_specs=[whole(pltpu.SMEM), whole(), whole()],
        out_specs=whole(),
        out_shape=jax.ShapeDtypeStruct((rows * CORES, width), BF16),
        compiler_params=limits(2),
        name="merge",
    )(core, own, other)


def packed(choices, acts, core):
    rows, half = choices[0][1].shape
    tiles = half // LANES
    shard = acts.shape[0] // PEERS
    count = len(choices)
    height = count * tiles * rows + shard

    def body(core_ref, *refs):
        acts_ref = refs[2 * count]
        out_ref = refs[-1]
        for c in range(count):
            source = choices[c][0]

            def fill(ref, c=c):
                for t in range(tiles):
                    base = (c * tiles + t) * rows
                    out_ref[0, base : base + rows, :] = ref[:, t * LANES : (t + 1) * LANES]

            pl.when(core_ref[0] == source)(lambda: fill(refs[2 * c]))
            pl.when(core_ref[0] != source)(lambda: fill(refs[2 * c + 1]))
        out_ref[0, count * tiles * rows :, :] = acts_ref[...]

    values = [v for choice in choices for v in choice[1:]]
    return pl.pallas_call(
        body,
        grid=(PEERS,),
        in_specs=[whole(pltpu.SMEM)]
        + [pl.BlockSpec((rows, half), lambda p: (0, 0))] * (2 * count)
        + [pl.BlockSpec((shard, rows), lambda p: (p, 0))],
        out_specs=pl.BlockSpec((1, height, rows), lambda p: (p, 0, 0)),
        out_shape=jax.ShapeDtypeStruct((PEERS, height, rows), BF16),
        compiler_params=limits(8),
        name="packed",
    )(core, *values, acts)


def weight_grads(stored, d_hidden, acts, upstream, core):
    arrays = []

    def ref_of(array):
        for i, known in enumerate(arrays):
            if known is array:
                return i
        arrays.append(array)
        return len(arrays) - 1

    step = 2
    lanes = stored[0].shape[2]
    half = 3 * lanes
    shard = 192
    stored_at = ref_of(stored[0])
    grad_at = ref_of(d_hidden[0])
    plans = []
    for plan in (acts, upstream):
        if plan[0] == "own":
            plans.append((ref_of(plan[1]), plan[2], None, None))
        else:
            plans.append((ref_of(plan[2]), plan[3], plan[1], ref_of(plan[4])))

    def body(core_ref, *refs):
        ins = refs[: len(arrays)]
        out_ref, low_ref, acc_ref = refs[len(arrays) :]
        index = pl.program_id(0)

        @pl.when(index == 0)
        def _():
            acc_ref[...] = jnp.zeros_like(acc_ref)

        def wide(ref, base):
            rows = [
                jnp.concatenate(
                    [ref[r, base + t * lanes : base + (t + 1) * lanes, :] for t in range(3)],
                    axis=1,
                )
                for r in range(step)
            ]
            return jnp.concatenate(rows, axis=0)

        def features(plan):
            at, base, when, other = plan
            blocks = []
            for r in range(step):
                block = ins[at][r, base : base + shard, :]
                if other is not None:
                    block = jnp.where(core_ref[0] == when, block, ins[other][r])
                blocks.append(block)
            return jnp.concatenate(blocks, axis=1)

        gate = wide(ins[stored_at], stored[1]).astype(F32)
        up = wide(ins[stored_at], stored[1] + half).astype(F32)
        grad = wide(ins[grad_at], d_hidden[1]).astype(F32)
        sigma = jax.nn.sigmoid(gate)
        silu = gate * sigma
        d_gate = (grad * up * sigma * (1.0 + gate * (1.0 - sigma))).astype(BF16)
        d_up = (grad * silu).astype(BF16)
        acts_t = features(plans[0])
        acc_ref[0] += dot_nn(acts_t, d_gate)
        acc_ref[1] += dot_nn(acts_t, d_up)
        acc_ref[2] += dot_nn(features(plans[1]), (silu * up).astype(BF16))

        @pl.when(index == PEERS // step - 1)
        def _():
            out_ref[...] = acc_ref[...]
            low_ref[...] = acc_ref[...].astype(BF16)

    shape = (3, shard, half)
    return pl.pallas_call(
        body,
        grid=(PEERS // step,),
        in_specs=[whole(pltpu.SMEM)]
        + [pl.BlockSpec((step, *a.shape[1:]), lambda p: (p, 0, 0)) for a in arrays],
        out_specs=[
            pl.BlockSpec(shape, lambda p: (0, 0, 0)),
            pl.BlockSpec(shape, lambda p: (0, 0, 0)),
        ],
        out_shape=[jax.ShapeDtypeStruct(shape, F32), jax.ShapeDtypeStruct(shape, BF16)],
        scratch_shapes=[pltpu.VMEM(shape, F32)],
        compiler_params=limits(16),
    )(core, *arrays)


def finish(own_0, own_1, got_0, got_1, core):
    count, shard, half = own_0.shape

    def body(core_ref, own_0_ref, own_1_ref, got_0_ref, got_1_ref, *outs):
        @pl.when(core_ref[0] == 0)
        def _():
            for i in range(count):
                outs[i][:, :half] = own_0_ref[i]
                outs[i][:, half:] = got_0_ref[i].astype(F32)

        @pl.when(core_ref[0] != 0)
        def _():
            for i in range(count):
                outs[i][:, :half] = got_1_ref[i].astype(F32)
                outs[i][:, half:] = own_1_ref[i]

    shape = jax.ShapeDtypeStruct((shard, half * CORES), F32)
    return pl.pallas_call(
        body,
        in_specs=[whole(pltpu.SMEM)] + [whole()] * 4,
        out_specs=[whole()] * count,
        out_shape=[shape] * count,
        compiler_params=limits(8),
        name="finish",
    )(core, own_0, own_1, got_0, got_1)


def crossing(sent, kept, residual, source, core, x, core_id, x_id):
    received = one_way(sent.astype(BF16), source)
    mine = jnp.where(core == source, kept.astype(BF16), received)
    width = mine.shape[1] // XS
    pieces = [
        shifted(columns_at(mine, (x + k) % XS, width), "x", k) for k in range(1, XS)
    ]
    total = columns_at(mine, x, width).astype(F32)
    for piece in pieces:
        total = total + piece.astype(F32)
    summed = total.astype(BF16)
    pieces = [shifted(summed, "zh", k) for k in range(1, ZH)]
    total = summed.astype(F32)
    for piece in pieces:
        total = total + piece.astype(F32)
    half_rows = lax.dynamic_slice(
        residual, (core * sent.shape[0], x * width), (sent.shape[0], width)
    )
    out = (half_rows.astype(F32) + total).astype(BF16)
    blocks = [out] + [shifted(out, "x", XS - k) for k in range(1, XS)]
    own = assemble(blocks, x_id)
    other = shifted(own, "segment", 1)
    return merge(own, other, core_id)


def local(tokens, w_gate, w_up, w_down, cotangent):
    return step(tokens, w_gate[0], w_up[0], w_down[0], cotangent)


def step(tokens, gate_w, up_w, down_w, cotangent):
    core = lax.axis_index("segment")
    x = lax.axis_index("x")
    core_id = core.astype(jnp.int32)[None]
    x_id = x.astype(jnp.int32)[None]
    rows = tokens.shape[0]
    features, hidden = gate_w.shape
    half = hidden // CORES
    split = rows // CORES

    def split_of(value):
        return value[:, :half], value[:, half:]

    own = jnp.where(core == 0, tokens.T, cotangent.T)
    gathered = exchanged(jnp.broadcast_to(own, (XS * ZH, *own.shape)), TENSOR)
    entered = gathered.reshape(features, rows)

    gate_a = dot_tn(entered, gate_w).astype(BF16)
    up_a = dot_tn(entered, up_w).astype(BF16)
    hidden_a = hidden_of(gate_a, up_a)
    sent = dot_nn(hidden_a[split:], down_w)
    kept = dot_nn(hidden_a[:split], down_w)
    swapped = shifted(entered, "segment", 1)
    tokens_t = jnp.where(core == 0, entered, swapped)
    cot_t = jnp.where(core == 0, swapped, entered)
    middle = crossing(sent, kept, tokens_t.T, 0, core, x, core_id, x_id)

    d_hidden_a = lax.optimization_barrier(
        lax.dot_general(
            entered, down_w, (((0,), (1,)), ((), ())), preferred_element_type=F32
        ).astype(BF16)
    )
    gate_l, gate_r = split_of(gate_a)
    up_l, up_r = split_of(up_a)
    grad_l, grad_r = split_of(d_hidden_a)
    choices = [
        (0, gate_l, one_way(gate_r, 0)),
        (0, up_l, one_way(up_r, 0)),
        (1, grad_r, one_way(grad_l, 1)),
    ]
    load = packed(choices, entered, core_id)
    wide = exchanged(load, DP)

    wide_a = wide
    entered_all = wide[:, 3 * half :]
    entered_other = shifted(entered_all, "segment", 1)

    gate_b = dot_nn(middle, gate_w).astype(BF16)
    up_b = dot_nn(middle, up_w).astype(BF16)
    d_gate_b, d_up_b = gate_grads(d_hidden_a.astype(F32), gate_b, up_b)
    sent = dot_nt(d_gate_b[:split], gate_w) + dot_nt(d_up_b[:split], up_w)
    kept = dot_nt(d_gate_b[split:], gate_w) + dot_nt(d_up_b[split:], up_w)
    upstream = crossing(sent, kept, cot_t.T, 1, core, x, core_id, x_id)

    gate_l, gate_r = split_of(gate_b)
    up_l, up_r = split_of(up_b)
    choices = [(1, gate_r, one_way(gate_l, 1)), (1, up_r, one_way(up_l, 1))]
    load = packed(choices, middle.T, core_id)
    load, wide_a = lax.optimization_barrier((load, wide_a))
    wide_b = exchanged(load, DP)

    d_hidden_b = dot_nt(upstream, down_w).astype(BF16)
    grad_l, grad_r = split_of(d_hidden_b)
    choices = [(0, grad_l, one_way(grad_r, 0))]
    load = packed(choices, upstream.T, core_id)
    load, wide_b = lax.optimization_barrier((load, wide_b))
    wide_c = exchanged(load, DP)

    own_1, low_1 = weight_grads(
        (wide_b, 0),
        (wide_a, 2 * half),
        ("own", wide_b, 2 * half),
        ("pick", 1, wide_a, 3 * half, entered_other),
        core_id,
    )
    got_1 = one_way(low_1, 0)
    own_0, low_0 = weight_grads(
        (wide_a, 0),
        (wide_c, 0),
        ("pick", 0, wide_a, 3 * half, entered_other),
        ("own", wide_c, half),
        core_id,
    )
    got_0 = one_way(low_0, 1)
    grad_gate, grad_up, grad_down = finish(own_0, own_1, got_0, got_1, core_id)
    return (grad_gate[None], grad_up[None], grad_down.T[None])


def solution(mesh):
    fine = Mesh(
        mesh.devices.reshape(CORES, XS, ZH, ZL, YS), ("segment", "x", "zh", "zl", "y")
    )
    in_specs = (
        P(DP, TENSOR),
        P("segment", None, TENSOR),
        P("segment", None, TENSOR),
        P("segment", TENSOR, None),
        P(DP, TENSOR),
    )
    out_specs = (
        P("segment", DP, TENSOR),
        P("segment", DP, TENSOR),
        P("segment", TENSOR, DP),
    )
    return jax.shard_map(
        local, mesh=fine, in_specs=in_specs, out_specs=out_specs, check_vma=False
    )
```

```python
import jax
import jax.numpy as jnp
from jax import lax
from jax.experimental import pallas as pl
from jax.experimental.pallas import tpu as pltpu
from jax.sharding import Mesh, PartitionSpec as P

CORES = 2
XS = 4
ZH = 4
ZL = 2
YS = 4
PEERS = ZL * YS
LANES = 128
TENSOR = ("x", "zh")
DP = ("zl", "y")
BF16 = jnp.bfloat16
F32 = jnp.float32


def shifted(value, axis, distance):
    size = lax.axis_size(axis)
    return lax.ppermute(value, axis, [(i, (i + distance) % size) for i in range(size)])


def one_way(value, source):
    return lax.ppermute(value, "segment", [(source, 1 - source)])


def exchanged(value, axes):
    return lax.all_to_all(value, axes, 0, 0, tiled=True)


def dot_tn(left, right):
    return lax.dot_general(left, right, (((0,), (0,)), ((), ())), preferred_element_type=F32)


def dot_nt(left, right):
    return lax.dot_general(left, right, (((1,), (1,)), ((), ())), preferred_element_type=F32)


def dot_nn(left, right):
    return jnp.dot(left, right, preferred_element_type=F32)


def whole(memory_space=pltpu.VMEM):
    return pl.BlockSpec(memory_space=memory_space)


def hidden_of(gate, up):
    gate = gate.astype(F32)
    return (jax.nn.silu(gate) * up.astype(F32)).astype(BF16)


def gate_grads(d_hidden, gate, up):
    gate = gate.astype(F32)
    up = up.astype(F32)
    sigma = jax.nn.sigmoid(gate)
    d_gate = (d_hidden * up * sigma * (1.0 + gate * (1.0 - sigma))).astype(BF16)
    d_up = (d_hidden * gate * sigma).astype(BF16)
    return d_gate, d_up


def limits(mebibytes):
    return pltpu.CompilerParams(vmem_limit_bytes=mebibytes * 2**20)


def columns_at(value, index, width):
    return lax.dynamic_slice_in_dim(value, index * width, width, 1)


def assemble(blocks, x):
    rows, width = blocks[0].shape

    def body(x_ref, *refs):
        out_ref = refs[-1]
        for k in range(XS):
            start = pl.multiple_of(((x_ref[0] + k) % XS) * width, LANES)
            out_ref[:, pl.ds(start, width)] = refs[k][...]

    return pl.pallas_call(
        body,
        in_specs=[whole(pltpu.SMEM)] + [whole()] * XS,
        out_specs=whole(),
        out_shape=jax.ShapeDtypeStruct((rows, width * XS), BF16),
        compiler_params=limits(2),
        name="assemble",
    )(x, *blocks)


def merge(own, other, core):
    rows, width = own.shape

    def body(core_ref, own_ref, other_ref, out_ref):
        start = pl.multiple_of(core_ref[0] * rows, 16)
        out_ref[pl.ds(start, rows), :] = own_ref[...]
        start = pl.multiple_of((1 - core_ref[0]) * rows, 16)
        out_ref[pl.ds(start, rows), :] = other_ref[...]

    return pl.pallas_call(
        body,
        in_specs=[whole(pltpu.SMEM), whole(), whole()],
        out_specs=whole(),
        out_shape=jax.ShapeDtypeStruct((rows * CORES, width), BF16),
        compiler_params=limits(2),
        name="merge",
    )(core, own, other)


def picked(by_core, core):
    rows, width = by_core[0][0][0].shape
    half = width // CORES
    count = max(len(picks) for picks in by_core)
    values = []
    for picks in by_core:
        for value, _ in picks:
            if not any(value is known for known in values):
                values.append(value)

    def body(core_ref, *refs):
        out_ref = refs[-1]
        for c, picks in enumerate(by_core):

            @pl.when(core_ref[0] == c)
            def _(picks=picks):
                for slot in range(count):
                    value, side = picks[min(slot, len(picks) - 1)]
                    at = [value is known for known in values].index(True)
                    out_ref[slot] = refs[at][:, side * half : (side + 1) * half]

    return pl.pallas_call(
        body,
        in_specs=[whole(pltpu.SMEM)] + [whole()] * len(values),
        out_specs=whole(),
        out_shape=jax.ShapeDtypeStruct((count, rows, half), BF16),
        compiler_params=limits(4),
        name="picked",
    )(core, *values)


def packed(choices, given, acts, core):
    rows, width = choices[0][0].shape
    half = width // CORES
    tiles = half // LANES
    shard = acts.shape[0] // PEERS
    count = len(choices)
    height = count * tiles * rows + shard

    def body(core_ref, *refs):
        given_ref, acts_ref, out_ref = refs[count:]
        for c, (_, source, slot) in enumerate(choices):
            for t in range(tiles):
                base = (c * tiles + t) * rows
                first = source * half + t * LANES
                own = refs[c][:, first : first + LANES]
                other = given_ref[slot, :, t * LANES : (t + 1) * LANES]
                out_ref[0, base : base + rows, :] = jnp.where(core_ref[0] == source, own, other)
        out_ref[0, count * tiles * rows :, :] = acts_ref[...]

    return pl.pallas_call(
        body,
        grid=(PEERS,),
        in_specs=[whole(pltpu.SMEM)]
        + [pl.BlockSpec((rows, width), lambda p: (0, 0))] * count
        + [pl.BlockSpec(given.shape, lambda p: (0, 0, 0))]
        + [pl.BlockSpec((shard, rows), lambda p: (p, 0))],
        out_specs=pl.BlockSpec((1, height, rows), lambda p: (p, 0, 0)),
        out_shape=pltpu.HBM((PEERS, height, rows), BF16),
        compiler_params=limits(8),
        name="packed",
    )(core, *[choice[0] for choice in choices], given, acts)


def weight_grads(stored, d_hidden, acts, upstream, core):
    arrays = []

    def ref_of(array):
        for i, known in enumerate(arrays):
            if known is array:
                return i
        arrays.append(array)
        return len(arrays) - 1

    step = 2
    lanes = stored[0].shape[2]
    half = 3 * lanes
    shard = 192
    stored_at = ref_of(stored[0])
    grad_at = ref_of(d_hidden[0])
    plans = []
    for plan in (acts, upstream):
        if plan[0] == "own":
            plans.append((ref_of(plan[1]), plan[2], None, None))
        else:
            plans.append((ref_of(plan[2]), plan[3], plan[1], ref_of(plan[4])))

    def body(core_ref, *refs):
        ins = refs[: len(arrays)]
        out_ref, low_ref, acc_ref = refs[len(arrays) :]
        index = pl.program_id(0)

        @pl.when(index == 0)
        def _():
            acc_ref[...] = jnp.zeros_like(acc_ref)

        def wide(ref, base):
            rows = [
                jnp.concatenate(
                    [ref[r, base + t * lanes : base + (t + 1) * lanes, :] for t in range(3)],
                    axis=1,
                )
                for r in range(step)
            ]
            return jnp.concatenate(rows, axis=0)

        def features(plan):
            at, base, when, other = plan
            blocks = []
            for r in range(step):
                block = ins[at][r, base : base + shard, :]
                if other is not None:
                    block = jnp.where(core_ref[0] == when, block, ins[other][r])
                blocks.append(block)
            return jnp.concatenate(blocks, axis=1)

        gate = wide(ins[stored_at], stored[1]).astype(F32)
        up = wide(ins[stored_at], stored[1] + half).astype(F32)
        grad = wide(ins[grad_at], d_hidden[1]).astype(F32)
        sigma = jax.nn.sigmoid(gate)
        silu = gate * sigma
        d_gate = (grad * up * sigma * (1.0 + gate * (1.0 - sigma))).astype(BF16)
        d_up = (grad * silu).astype(BF16)
        acts_t = features(plans[0])
        acc_ref[0] += dot_nn(acts_t, d_gate)
        acc_ref[1] += dot_nn(acts_t, d_up)
        acc_ref[2] += dot_nn(features(plans[1]), (silu * up).astype(BF16))

        @pl.when(index == PEERS // step - 1)
        def _():
            out_ref[...] = acc_ref[...]
            low_ref[...] = acc_ref[...].astype(BF16)

    shape = (3, shard, half)
    return pl.pallas_call(
        body,
        grid=(PEERS // step,),
        in_specs=[whole(pltpu.SMEM)]
        + [pl.BlockSpec((step, *a.shape[1:]), lambda p: (p, 0, 0)) for a in arrays],
        out_specs=[
            pl.BlockSpec(shape, lambda p: (0, 0, 0)),
            pl.BlockSpec(shape, lambda p: (0, 0, 0)),
        ],
        out_shape=[jax.ShapeDtypeStruct(shape, F32), jax.ShapeDtypeStruct(shape, BF16)],
        scratch_shapes=[pltpu.VMEM(shape, F32)],
        compiler_params=limits(16),
    )(core, *arrays)


def finish(own_0, own_1, got_0, got_1, core):
    count, shard, half = own_0.shape

    def body(core_ref, own_0_ref, own_1_ref, got_0_ref, got_1_ref, *outs):
        @pl.when(core_ref[0] == 0)
        def _():
            for i in range(count):
                outs[i][:, :half] = own_0_ref[i]
                outs[i][:, half:] = got_0_ref[i].astype(F32)

        @pl.when(core_ref[0] != 0)
        def _():
            for i in range(count):
                outs[i][:, :half] = got_1_ref[i].astype(F32)
                outs[i][:, half:] = own_1_ref[i]

    shape = jax.ShapeDtypeStruct((shard, half * CORES), F32)
    return pl.pallas_call(
        body,
        in_specs=[whole(pltpu.SMEM)] + [whole()] * 4,
        out_specs=[whole()] * count,
        out_shape=[shape] * count,
        compiler_params=limits(8),
        name="finish",
    )(core, own_0, own_1, got_0, got_1)


def crossing(partial, residual, source, core, x, core_id, x_id):
    split = partial.shape[0] // CORES
    halves = [partial[:split], partial[split:]]
    received = one_way(halves[1 - source], source)
    mine = jnp.where(core == source, halves[source], received)
    width = mine.shape[1] // XS
    pieces = [
        shifted(columns_at(mine, (x + k) % XS, width), "x", k) for k in range(1, XS)
    ]
    total = columns_at(mine, x, width).astype(F32)
    for piece in pieces:
        total = total + piece.astype(F32)
    summed = total.astype(BF16)
    pieces = [shifted(summed, "zh", k) for k in range(1, ZH)]
    total = summed.astype(F32)
    for piece in pieces:
        total = total + piece.astype(F32)
    half_rows = lax.dynamic_slice(residual, (core * split, x * width), (split, width))
    out = (half_rows.astype(F32) + total).astype(BF16)
    blocks = [out] + [shifted(out, "x", XS - k) for k in range(1, XS)]
    own = assemble(blocks, x_id)
    other = shifted(own, "segment", 1)
    return merge(own, other, core_id)


def local(tokens, w_gate, w_up, w_down, cotangent):
    return step(tokens, w_gate[0], w_up[0], w_down[0], cotangent)


def step(tokens, gate_w, up_w, down_w, cotangent):
    core = lax.axis_index("segment")
    x = lax.axis_index("x")
    core_id = core.astype(jnp.int32)[None]
    x_id = x.astype(jnp.int32)[None]
    rows = tokens.shape[0]
    features, hidden = gate_w.shape
    half = hidden // CORES

    own = jnp.where(core == 0, tokens.T, cotangent.T)
    gathered = exchanged(jnp.broadcast_to(own, (XS * ZH, *own.shape)), TENSOR)
    entered = gathered.reshape(features, rows)

    gate_a = dot_tn(entered, gate_w).astype(BF16)
    up_a = dot_tn(entered, up_w).astype(BF16)
    hidden_a = hidden_of(gate_a, up_a)
    partial_a = dot_nn(hidden_a, down_w).astype(BF16)
    swapped = shifted(entered, "segment", 1)
    tokens_t = jnp.where(core == 0, entered, swapped)
    cot_t = jnp.where(core == 0, swapped, entered)
    middle = crossing(partial_a, tokens_t.T, 0, core, x, core_id, x_id)

    d_hidden_a = lax.optimization_barrier(
        lax.dot_general(
            entered, down_w, (((0,), (1,)), ((), ())), preferred_element_type=F32
        ).astype(BF16)
    )
    outgoing = picked([[(gate_a, 1), (up_a, 1)], [(d_hidden_a, 0)]], core_id)
    given = shifted(outgoing, "segment", 1)
    load = packed([(gate_a, 0, 0), (up_a, 0, 1), (d_hidden_a, 1, 0)], given, entered, core_id)
    wide = exchanged(load, DP)

    wide_a = wide
    entered_all = wide[:, 3 * half :]
    entered_other = shifted(entered_all, "segment", 1)

    gate_b = dot_nn(middle, gate_w).astype(BF16)
    up_b = dot_nn(middle, up_w).astype(BF16)
    d_gate_b, d_up_b = gate_grads(d_hidden_a.astype(F32), gate_b, up_b)
    partial_b = (dot_nt(d_gate_b, gate_w) + dot_nt(d_up_b, up_w)).astype(BF16)
    upstream = crossing(partial_b, cot_t.T, 1, core, x, core_id, x_id)

    picks = [(gate_b, 0), (up_b, 0)]
    outgoing = picked([picks, picks], core_id)
    given = one_way(outgoing, 1)
    load = packed([(gate_b, 1, 0), (up_b, 1, 1)], given, middle.T, core_id)
    load, wide_a = lax.optimization_barrier((load, wide_a))
    wide_b = exchanged(load, DP)

    d_hidden_b = dot_nt(upstream, down_w).astype(BF16)
    outgoing = d_hidden_b[:, half:][None]
    given = one_way(outgoing, 0)
    load = packed([(d_hidden_b, 0, 0)], given, upstream.T, core_id)
    load, wide_b = lax.optimization_barrier((load, wide_b))
    wide_c = exchanged(load, DP)

    own_1, low_1 = weight_grads(
        (wide_b, 0),
        (wide_a, 2 * half),
        ("own", wide_b, 2 * half),
        ("pick", 1, wide_a, 3 * half, entered_other),
        core_id,
    )
    got_1 = one_way(low_1, 0)
    own_0, low_0 = weight_grads(
        (wide_a, 0),
        (wide_c, 0),
        ("pick", 0, wide_a, 3 * half, entered_other),
        ("own", wide_c, half),
        core_id,
    )
    got_0 = one_way(low_0, 1)
    grad_gate, grad_up, grad_down = finish(own_0, own_1, got_0, got_1, core_id)
    return (grad_gate[None], grad_up[None], grad_down.T[None])


def solution(mesh):
    fine = Mesh(
        mesh.devices.reshape(CORES, XS, ZH, ZL, YS), ("segment", "x", "zh", "zl", "y")
    )
    in_specs = (
        P(DP, TENSOR),
        P("segment", None, TENSOR),
        P("segment", None, TENSOR),
        P("segment", TENSOR, None),
        P(DP, TENSOR),
    )
    out_specs = (
        P("segment", DP, TENSOR),
        P("segment", DP, TENSOR),
        P("segment", TENSOR, DP),
    )
    return jax.shard_map(
        local, mesh=fine, in_specs=in_specs, out_specs=out_specs, check_vma=False
    )
```

```python
import jax
import jax.numpy as jnp
from jax import lax
from jax.experimental import pallas as pl
from jax.experimental.pallas import tpu as pltpu
from jax.sharding import Mesh, PartitionSpec as P

CORES = 2
XS = 4
ZH = 4
ZL = 2
YS = 4
PEERS = ZL * YS
LANES = 128
TENSOR = ("x", "zh")
DP = ("zl", "y")
BF16 = jnp.bfloat16
F32 = jnp.float32


def shifted(value, axis, distance):
    size = lax.axis_size(axis)
    return lax.ppermute(value, axis, [(i, (i + distance) % size) for i in range(size)])


def shifted_on(value, core, axis, distance):
    size = lax.axis_size(axis)
    first = core * size
    pairs = [(first + i, first + (i + distance) % size) for i in range(size)]
    return lax.ppermute(value, ("segment", axis), pairs)


def one_way(value, source):
    return lax.ppermute(value, "segment", [(source, 1 - source)])


def exchanged(value, axes):
    return lax.all_to_all(value, axes, 0, 0, tiled=True)


def dot_tn(left, right):
    return lax.dot_general(left, right, (((0,), (0,)), ((), ())), preferred_element_type=F32)


def dot_nt(left, right):
    return lax.dot_general(left, right, (((1,), (1,)), ((), ())), preferred_element_type=F32)


def dot_nn(left, right):
    return jnp.dot(left, right, preferred_element_type=F32)


def whole(memory_space=pltpu.VMEM):
    return pl.BlockSpec(memory_space=memory_space)


def hidden_of(gate, up):
    gate = gate.astype(F32)
    return (jax.nn.silu(gate) * up.astype(F32)).astype(BF16)


def gate_grads(d_hidden, gate, up):
    gate = gate.astype(F32)
    up = up.astype(F32)
    sigma = jax.nn.sigmoid(gate)
    d_gate = (d_hidden * up * sigma * (1.0 + gate * (1.0 - sigma))).astype(BF16)
    d_up = (d_hidden * gate * sigma).astype(BF16)
    return d_gate, d_up


def limits(mebibytes):
    return pltpu.CompilerParams(vmem_limit_bytes=mebibytes * 2**20)


def columns_at(value, index, width):
    return lax.dynamic_slice_in_dim(value, index * width, width, 1)


def assemble(blocks, x):
    rows, width = blocks[0].shape

    def body(x_ref, *refs):
        out_ref = refs[-1]
        for k in range(XS):
            start = pl.multiple_of(((x_ref[0] + k) % XS) * width, LANES)
            out_ref[:, pl.ds(start, width)] = refs[k][...]

    return pl.pallas_call(
        body,
        in_specs=[whole(pltpu.SMEM)] + [whole()] * XS,
        out_specs=whole(),
        out_shape=jax.ShapeDtypeStruct((rows, width * XS), BF16),
        compiler_params=limits(2),
        name="assemble",
    )(x, *blocks)


def picked(by_core, core):
    rows, width = by_core[0][0][0].shape
    half = width // CORES
    count = max(len(picks) for picks in by_core)
    values = []
    for picks in by_core:
        for value, _ in picks:
            if not any(value is known for known in values):
                values.append(value)

    def body(core_ref, *refs):
        out_ref = refs[-1]
        for c, picks in enumerate(by_core):

            @pl.when(core_ref[0] == c)
            def _(picks=picks):
                for slot in range(count):
                    value, side = picks[min(slot, len(picks) - 1)]
                    at = [value is known for known in values].index(True)
                    out_ref[slot] = refs[at][:, side * half : (side + 1) * half]

    return pl.pallas_call(
        body,
        in_specs=[whole(pltpu.SMEM)] + [whole()] * len(values),
        out_specs=whole(),
        out_shape=jax.ShapeDtypeStruct((count, rows, half), BF16),
        compiler_params=limits(4),
        name="picked",
    )(core, *values)


def packed(choices, given, acts, core):
    rows = choices[0][0].shape[0]
    half = choices[0][0].shape[1] // (1 if given is None else CORES)
    tiles = half // LANES
    turned = isinstance(acts, tuple)
    features = acts[0].shape[1] if turned else acts.shape[0]
    shard = features // PEERS
    count = len(choices)
    height = count * tiles * rows + shard
    values = [choice[0] for choice in choices]
    specs = [pl.BlockSpec(value.shape, lambda p: (0, 0)) for value in values]
    if given is not None:
        values.append(given)
        specs.append(pl.BlockSpec(given.shape, lambda p: (0, 0, 0)))
    if turned:
        values += acts[:2]
        specs += [pl.BlockSpec(acts[0].shape, lambda p: (0, 0))] * 2
    else:
        values.append(acts)
        specs.append(pl.BlockSpec((shard, rows), lambda p: (p, 0)))

    def body(core_ref, *refs):
        given_ref = None if given is None else refs[count]
        out_ref = refs[len(values)]
        peer = pl.program_id(0)
        for c, (_, source, slot) in enumerate(choices):
            for t in range(tiles):
                base = (c * tiles + t) * rows
                first = (source or 0) * half + t * LANES
                tile = refs[c][:, first : first + LANES]
                if source is not None:
                    other = given_ref[slot, :, t * LANES : (t + 1) * LANES]
                    tile = jnp.where(core_ref[0] == source, tile, other)
                out_ref[0, base : base + rows, :] = tile
        if turned:
            own_ref, received_ref = refs[len(values) - 2 : len(values)]
            turned_ref = refs[-1]

            @pl.when(peer == 0)
            def _():
                for t in range(features // LANES):
                    at = slice(t * LANES, (t + 1) * LANES)
                    tile = jnp.where(core_ref[0] == acts[2], own_ref[:, at], received_ref[:, at])
                    turned_ref[at, :] = tile.T

            start = pl.multiple_of(peer * shard, 64)
            out_ref[0, count * tiles * rows :, :] = turned_ref[pl.ds(start, shard), :]
        else:
            out_ref[0, count * tiles * rows :, :] = refs[len(values) - 1][...]

    return pl.pallas_call(
        body,
        grid=(PEERS,),
        in_specs=[whole(pltpu.SMEM)] + specs,
        out_specs=pl.BlockSpec((1, height, rows), lambda p: (p, 0, 0)),
        out_shape=jax.ShapeDtypeStruct((PEERS, height, rows), BF16),
        scratch_shapes=[pltpu.VMEM((features, rows), BF16)] if turned else [],
        compiler_params=limits(8),
        name="packed",
    )(core, *values)


def weight_grads(stored, d_hidden, acts, upstream, core):
    arrays = []

    def ref_of(array):
        for i, known in enumerate(arrays):
            if known is array:
                return i
        arrays.append(array)
        return len(arrays) - 1

    step = 2
    lanes = stored[0].shape[2]
    half = 3 * lanes
    shard = 192
    stored_at = ref_of(stored[0])
    grad_at = ref_of(d_hidden[0])
    plans = []
    for plan in (acts, upstream):
        if plan[0] == "own":
            plans.append((ref_of(plan[1]), plan[2], None, None))
        else:
            plans.append((ref_of(plan[2]), plan[3], plan[1], ref_of(plan[4])))

    def body(core_ref, *refs):
        ins = refs[: len(arrays)]
        out_ref, low_ref, acc_ref = refs[len(arrays) :]
        index = pl.program_id(0)

        @pl.when(index == 0)
        def _():
            acc_ref[...] = jnp.zeros_like(acc_ref)

        def wide(ref, base):
            rows = [
                jnp.concatenate(
                    [ref[r, base + t * lanes : base + (t + 1) * lanes, :] for t in range(3)],
                    axis=1,
                )
                for r in range(step)
            ]
            return jnp.concatenate(rows, axis=0)

        def features(plan):
            at, base, when, other = plan
            blocks = []
            for r in range(step):
                block = ins[at][r, base : base + shard, :]
                if other is not None:
                    block = jnp.where(core_ref[0] == when, block, ins[other][r])
                blocks.append(block)
            return jnp.concatenate(blocks, axis=1)

        gate = wide(ins[stored_at], stored[1]).astype(F32)
        up = wide(ins[stored_at], stored[1] + half).astype(F32)
        grad = wide(ins[grad_at], d_hidden[1]).astype(F32)
        sigma = jax.nn.sigmoid(gate)
        silu = gate * sigma
        d_gate = (grad * up * sigma * (1.0 + gate * (1.0 - sigma))).astype(BF16)
        d_up = (grad * silu).astype(BF16)
        acts_t = features(plans[0])
        acc_ref[0] += dot_nn(acts_t, d_gate)
        acc_ref[1] += dot_nn(acts_t, d_up)
        acc_ref[2] += dot_nn(features(plans[1]), (silu * up).astype(BF16))

        @pl.when(index == PEERS // step - 1)
        def _():
            out_ref[...] = acc_ref[...]
            low_ref[...] = acc_ref[...].astype(BF16)

    shape = (3, shard, half)
    return pl.pallas_call(
        body,
        grid=(PEERS // step,),
        in_specs=[whole(pltpu.SMEM)]
        + [pl.BlockSpec((step, *a.shape[1:]), lambda p: (p, 0, 0)) for a in arrays],
        out_specs=[
            pl.BlockSpec(shape, lambda p: (0, 0, 0)),
            pl.BlockSpec(shape, lambda p: (0, 0, 0)),
        ],
        out_shape=[jax.ShapeDtypeStruct(shape, F32), jax.ShapeDtypeStruct(shape, BF16)],
        scratch_shapes=[pltpu.VMEM(shape, F32)],
        compiler_params=limits(16),
    )(core, *arrays)


def finish(own_0, own_1, got_0, got_1, core):
    count, shard, half = own_0.shape

    def body(core_ref, own_0_ref, own_1_ref, got_0_ref, got_1_ref, *outs):
        @pl.when(core_ref[0] == 0)
        def _():
            for i in range(count):
                outs[i][:, :half] = own_0_ref[i]
                outs[i][:, half:] = got_0_ref[i].astype(F32)

        @pl.when(core_ref[0] != 0)
        def _():
            for i in range(count):
                outs[i][:, :half] = got_1_ref[i].astype(F32)
                outs[i][:, half:] = own_1_ref[i]

    shape = jax.ShapeDtypeStruct((shard, half * CORES), F32)
    return pl.pallas_call(
        body,
        in_specs=[whole(pltpu.SMEM)] + [whole()] * 4,
        out_specs=[whole()] * count,
        out_shape=[shape] * count,
        compiler_params=limits(8),
        name="finish",
    )(core, own_0, own_1, got_0, got_1)


def crossing(partial, residual, source, x, x_id):
    width = partial.shape[1] // XS
    pieces = [
        shifted_on(columns_at(partial, (x + k) % XS, width), source, "x", k)
        for k in range(1, XS)
    ]
    total = columns_at(partial, x, width).astype(F32)
    for piece in pieces:
        total = total + piece.astype(F32)
    summed = total.astype(BF16)
    pieces = [shifted_on(summed, source, "zh", k) for k in range(1, ZH)]
    total = summed.astype(F32)
    for piece in pieces:
        total = total + piece.astype(F32)
    out = (columns_at(residual, x, width).astype(F32) + total).astype(BF16)
    blocks = [out] + [shifted_on(out, source, "x", XS - k) for k in range(1, XS)]
    own = assemble(blocks, x_id)
    received = one_way(own, source)
    return own, received


def local(tokens, w_gate, w_up, w_down, cotangent):
    return step(tokens, w_gate[0], w_up[0], w_down[0], cotangent)


def step(tokens, gate_w, up_w, down_w, cotangent):
    core = lax.axis_index("segment")
    x = lax.axis_index("x")
    core_id = core.astype(jnp.int32)[None]
    x_id = x.astype(jnp.int32)[None]
    rows = tokens.shape[0]
    features, hidden = gate_w.shape
    half = hidden // CORES

    lent = one_way(down_w[half:], 0)
    down_half = lax.optimization_barrier(jnp.where(core == 0, down_w[:half], lent))
    own = jnp.where(core == 0, tokens.T, cotangent.T)
    gathered = exchanged(jnp.broadcast_to(own, (XS * ZH, *own.shape)), TENSOR)
    entered = gathered.reshape(features, rows)

    gate_a = dot_tn(entered, gate_w).astype(BF16)
    up_a = dot_tn(entered, up_w).astype(BF16)
    hidden_a = hidden_of(gate_a, up_a)
    partial_a = dot_nn(hidden_a, down_w).astype(BF16)
    residual = entered.T
    middle_own, middle = crossing(partial_a, residual, 0, x, x_id)

    d_hidden_a = lax.optimization_barrier(
        lax.dot_general(
            entered, down_w, (((0,), (1,)), ((), ())), preferred_element_type=F32
        ).astype(BF16)
    )
    outgoing = picked([[(gate_a, 1), (up_a, 1)], [(d_hidden_a, 0)]], core_id)
    given = shifted(outgoing, "segment", 1)
    load = packed(
        [(gate_a, 0, 0), (up_a, 0, 1), (d_hidden_a, 1, 0)], given, entered, core_id
    )
    wide = exchanged(load, DP)

    wide_a = wide
    entered_all = wide[:, 3 * half :]
    entered_other = shifted(entered_all, "segment", 1)

    gate_b = dot_nn(middle, gate_w).astype(BF16)
    up_b = dot_nn(middle, up_w).astype(BF16)
    d_gate_b, d_up_b = gate_grads(d_hidden_a.astype(F32), gate_b, up_b)
    partial_b = (dot_nt(d_gate_b, gate_w) + dot_nt(d_up_b, up_w)).astype(BF16)
    up_own, up_received = crossing(partial_b, residual, 1, x, x_id)
    upstream = jnp.where(core == 1, up_own, up_received)

    picks = [(gate_b, 0), (up_b, 0)]
    outgoing = picked([picks, picks], core_id)
    given = one_way(outgoing, 1)
    load = packed([(gate_b, 1, 0), (up_b, 1, 1)], given, (middle_own, middle, 0), core_id)
    load, wide_a = lax.optimization_barrier((load, wide_a))
    wide_b = exchanged(load, DP)

    d_hidden_b = dot_nt(upstream, down_half).astype(BF16)
    load = packed([(d_hidden_b, None, 0)], None, (up_own, up_received, 1), core_id)
    load, wide_b = lax.optimization_barrier((load, wide_b))
    wide_c = exchanged(load, DP)

    own_1, low_1 = weight_grads(
        (wide_b, 0),
        (wide_a, 2 * half),
        ("own", wide_b, 2 * half),
        ("pick", 1, wide_a, 3 * half, entered_other),
        core_id,
    )
    got_1 = one_way(low_1, 0)
    own_0, low_0 = weight_grads(
        (wide_a, 0),
        (wide_c, 0),
        ("pick", 0, wide_a, 3 * half, entered_other),
        ("own", wide_c, half),
        core_id,
    )
    got_0 = one_way(low_0, 1)
    grad_gate, grad_up, grad_down = finish(own_0, own_1, got_0, got_1, core_id)
    return (grad_gate[None], grad_up[None], grad_down.T[None])


def solution(mesh):
    fine = Mesh(
        mesh.devices.reshape(CORES, XS, ZH, ZL, YS), ("segment", "x", "zh", "zl", "y")
    )
    in_specs = (
        P(DP, TENSOR),
        P("segment", None, TENSOR),
        P("segment", None, TENSOR),
        P("segment", TENSOR, None),
        P(DP, TENSOR),
    )
    out_specs = (
        P("segment", DP, TENSOR),
        P("segment", DP, TENSOR),
        P("segment", TENSOR, DP),
    )
    return jax.shard_map(
        local, mesh=fine, in_specs=in_specs, out_specs=out_specs, check_vma=False
    )
```

```python
import jax
import jax.numpy as jnp
from jax import lax
from jax.experimental import pallas as pl
from jax.experimental.pallas import tpu as pltpu
from jax.sharding import Mesh, PartitionSpec as P

CORES = 2
XS = 4
ZH = 4
ZL = 2
YS = 4
PEERS = ZL * YS
LANES = 128
TENSOR = ("x", "zh")
DP = ("zl", "y")
BF16 = jnp.bfloat16
F32 = jnp.float32


def shifted(value, axis, distance):
    size = lax.axis_size(axis)
    return lax.ppermute(value, axis, [(i, (i + distance) % size) for i in range(size)])


def one_way(value, source):
    return lax.ppermute(value, "segment", [(source, 1 - source)])


def exchanged(value, axes):
    return lax.all_to_all(value, axes, 0, 0, tiled=True)


def dot_tn(left, right):
    return lax.dot_general(left, right, (((0,), (0,)), ((), ())), preferred_element_type=F32)


def dot_nt(left, right):
    return lax.dot_general(left, right, (((1,), (1,)), ((), ())), preferred_element_type=F32)


def dot_nn(left, right):
    return jnp.dot(left, right, preferred_element_type=F32)


def whole(memory_space=pltpu.VMEM):
    return pl.BlockSpec(memory_space=memory_space)


def hidden_of(gate, up):
    gate = gate.astype(F32)
    return (jax.nn.silu(gate) * up.astype(F32)).astype(BF16)


def gate_grads(d_hidden, gate, up):
    gate = gate.astype(F32)
    up = up.astype(F32)
    sigma = jax.nn.sigmoid(gate)
    d_gate = (d_hidden * up * sigma * (1.0 + gate * (1.0 - sigma))).astype(BF16)
    d_up = (d_hidden * gate * sigma).astype(BF16)
    return d_gate, d_up


def limits(mebibytes):
    return pltpu.CompilerParams(vmem_limit_bytes=mebibytes * 2**20)


def columns_at(value, index, width):
    return lax.dynamic_slice_in_dim(value, index * width, width, 1)


def assemble(blocks, x):
    rows, width = blocks[0].shape

    def body(x_ref, *refs):
        out_ref = refs[-1]
        for k in range(XS):
            start = pl.multiple_of(((x_ref[0] + k) % XS) * width, LANES)
            out_ref[:, pl.ds(start, width)] = refs[k][...]

    return pl.pallas_call(
        body,
        in_specs=[whole(pltpu.SMEM)] + [whole()] * XS,
        out_specs=whole(),
        out_shape=jax.ShapeDtypeStruct((rows, width * XS), BF16),
        compiler_params=limits(2),
        name="assemble",
    )(x, *blocks)


def merge(own, other, core):
    rows, width = own.shape

    def body(core_ref, own_ref, other_ref, out_ref):
        start = pl.multiple_of(core_ref[0] * rows, 16)
        out_ref[pl.ds(start, rows), :] = own_ref[...]
        start = pl.multiple_of((1 - core_ref[0]) * rows, 16)
        out_ref[pl.ds(start, rows), :] = other_ref[...]

    return pl.pallas_call(
        body,
        in_specs=[whole(pltpu.SMEM), whole(), whole()],
        out_specs=whole(),
        out_shape=jax.ShapeDtypeStruct((rows * CORES, width), BF16),
        compiler_params=limits(2),
        name="merge",
    )(core, own, other)


def picked(by_core, core):
    rows, width = by_core[0][0][0].shape
    half = width // CORES
    count = max(len(picks) for picks in by_core)
    values = []
    for picks in by_core:
        for value, _ in picks:
            if not any(value is known for known in values):
                values.append(value)

    def body(core_ref, *refs):
        out_ref = refs[-1]
        for c, picks in enumerate(by_core):

            @pl.when(core_ref[0] == c)
            def _(picks=picks):
                for slot in range(count):
                    value, side = picks[min(slot, len(picks) - 1)]
                    at = [value is known for known in values].index(True)
                    out_ref[slot] = refs[at][:, side * half : (side + 1) * half]

    return pl.pallas_call(
        body,
        in_specs=[whole(pltpu.SMEM)] + [whole()] * len(values),
        out_specs=whole(),
        out_shape=jax.ShapeDtypeStruct((count, rows, half), BF16),
        compiler_params=limits(4),
        name="picked",
    )(core, *values)


def packed(choices, given, acts, core):
    rows = choices[0][0].shape[0]
    half = choices[0][0].shape[1] // (1 if given is None else CORES)
    tiles = half // LANES
    turned = isinstance(acts, tuple)
    features = acts[0].shape[1] if turned else acts.shape[0]
    shard = features // PEERS
    count = len(choices)
    height = count * tiles * rows + shard
    values = [choice[0] for choice in choices]
    specs = [pl.BlockSpec(value.shape, lambda p: (0, 0)) for value in values]
    if given is not None:
        values.append(given)
        specs.append(pl.BlockSpec(given.shape, lambda p: (0, 0, 0)))
    if turned:
        values.append(acts[0])
        specs.append(pl.BlockSpec(acts[0].shape, lambda p: (0, 0)))
    else:
        values.append(acts)
        specs.append(pl.BlockSpec((shard, rows), lambda p: (p, 0)))

    def body(core_ref, *refs):
        given_ref = None if given is None else refs[count]
        out_ref = refs[len(values)]
        peer = pl.program_id(0)
        for c, (_, source, slot) in enumerate(choices):
            for t in range(tiles):
                base = (c * tiles + t) * rows
                first = (source or 0) * half + t * LANES
                tile = refs[c][:, first : first + LANES]
                if source is not None:
                    other = given_ref[slot, :, t * LANES : (t + 1) * LANES]
                    tile = jnp.where(core_ref[0] == source, tile, other)
                out_ref[0, base : base + rows, :] = tile
        if turned:
            acts_ref = refs[len(values) - 1]
            turned_ref = refs[-1]

            @pl.when(peer == 0)
            def _():
                for t in range(features // LANES):
                    at = slice(t * LANES, (t + 1) * LANES)
                    turned_ref[at, :] = acts_ref[:, at].T

            start = pl.multiple_of(peer * shard, 64)
            out_ref[0, count * tiles * rows :, :] = turned_ref[pl.ds(start, shard), :]
        else:
            out_ref[0, count * tiles * rows :, :] = refs[len(values) - 1][...]

    return pl.pallas_call(
        body,
        grid=(PEERS,),
        in_specs=[whole(pltpu.SMEM)] + specs,
        out_specs=pl.BlockSpec((1, height, rows), lambda p: (p, 0, 0)),
        out_shape=jax.ShapeDtypeStruct((PEERS, height, rows), BF16),
        scratch_shapes=[pltpu.VMEM((features, rows), BF16)] if turned else [],
        compiler_params=limits(8),
        name="packed",
    )(core, *values)


def weight_grads(stored, d_hidden, acts, upstream, core):
    arrays = []

    def ref_of(array):
        for i, known in enumerate(arrays):
            if known is array:
                return i
        arrays.append(array)
        return len(arrays) - 1

    step = 2
    lanes = stored[0].shape[2]
    half = 3 * lanes
    shard = 192
    stored_at = ref_of(stored[0])
    grad_at = ref_of(d_hidden[0])
    plans = []
    for plan in (acts, upstream):
        if plan[0] == "own":
            plans.append((ref_of(plan[1]), plan[2], None, None))
        else:
            plans.append((ref_of(plan[2]), plan[3], plan[1], ref_of(plan[4])))

    def body(core_ref, *refs):
        ins = refs[: len(arrays)]
        out_ref, low_ref, acc_ref = refs[len(arrays) :]
        index = pl.program_id(0)

        @pl.when(index == 0)
        def _():
            acc_ref[...] = jnp.zeros_like(acc_ref)

        def wide(ref, base):
            rows = [
                jnp.concatenate(
                    [ref[r, base + t * lanes : base + (t + 1) * lanes, :] for t in range(3)],
                    axis=1,
                )
                for r in range(step)
            ]
            return jnp.concatenate(rows, axis=0)

        def features(plan):
            at, base, when, other = plan
            blocks = []
            for r in range(step):
                block = ins[at][r, base : base + shard, :]
                if other is not None:
                    block = jnp.where(core_ref[0] == when, block, ins[other][r])
                blocks.append(block)
            return jnp.concatenate(blocks, axis=1)

        gate = wide(ins[stored_at], stored[1]).astype(F32)
        up = wide(ins[stored_at], stored[1] + half).astype(F32)
        grad = wide(ins[grad_at], d_hidden[1]).astype(F32)
        sigma = jax.nn.sigmoid(gate)
        silu = gate * sigma
        d_gate = (grad * up * sigma * (1.0 + gate * (1.0 - sigma))).astype(BF16)
        d_up = (grad * silu).astype(BF16)
        acts_t = features(plans[0])
        acc_ref[0] += dot_nn(acts_t, d_gate)
        acc_ref[1] += dot_nn(acts_t, d_up)
        acc_ref[2] += dot_nn(features(plans[1]), (silu * up).astype(BF16))

        @pl.when(index == PEERS // step - 1)
        def _():
            out_ref[...] = acc_ref[...]
            low_ref[...] = acc_ref[...].astype(BF16)

    shape = (3, shard, half)
    return pl.pallas_call(
        body,
        grid=(PEERS // step,),
        in_specs=[whole(pltpu.SMEM)]
        + [pl.BlockSpec((step, *a.shape[1:]), lambda p: (p, 0, 0)) for a in arrays],
        out_specs=[
            pl.BlockSpec(shape, lambda p: (0, 0, 0)),
            pl.BlockSpec(shape, lambda p: (0, 0, 0)),
        ],
        out_shape=[jax.ShapeDtypeStruct(shape, F32), jax.ShapeDtypeStruct(shape, BF16)],
        scratch_shapes=[pltpu.VMEM(shape, F32)],
        compiler_params=limits(16),
    )(core, *arrays)


def coefficients(stored, other, core):
    peers, height, lanes = stored.shape
    shard = other.shape[1]
    half = 3 * lanes
    base = height - shard

    def body(core_ref, stored_ref, other_ref, first_ref, second_ref, hidden_ref, acts_ref):
        for t in range(3):
            at = slice(t * lanes, (t + 1) * lanes)
            gate = stored_ref[0, t * lanes : (t + 1) * lanes, :].astype(F32)
            up = stored_ref[0, half + t * lanes : half + (t + 1) * lanes, :].astype(F32)
            sigma = jax.nn.sigmoid(gate)
            silu = gate * sigma
            first_ref[0, :, at] = (up * sigma * (1.0 + gate * (1.0 - sigma))).astype(BF16)
            second_ref[0, :, at] = silu.astype(BF16)
            hidden_ref[0, :, at] = (silu * up).astype(BF16)
        acts_ref[0] = jnp.where(core_ref[0] == 0, stored_ref[0, base:, :], other_ref[0])

    def block(rows, width):
        return pl.BlockSpec((1, rows, width), lambda p: (p, 0, 0))

    return pl.pallas_call(
        body,
        grid=(peers,),
        in_specs=[whole(pltpu.SMEM), block(height, lanes), block(shard, lanes)],
        out_specs=[block(lanes, half)] * 3 + [block(shard, lanes)],
        out_shape=[
            jax.ShapeDtypeStruct((peers, lanes, half), BF16),
            jax.ShapeDtypeStruct((peers, lanes, half), BF16),
            jax.ShapeDtypeStruct((peers, lanes, half), BF16),
            jax.ShapeDtypeStruct((peers, shard, lanes), BF16),
        ],
        compiler_params=limits(8),
        name="coefficients",
    )(core, stored, other)


def last_grads(first, second, hidden, acts, late):
    peers, _, lanes = late.shape
    shard = acts.shape[1]
    half = 3 * lanes
    step = 2

    def body(first_ref, second_ref, hidden_ref, acts_ref, late_ref, out_ref, low_ref):
        index = pl.program_id(0)

        @pl.when(index == 0)
        def _():
            out_ref[...] = jnp.zeros_like(out_ref)

        def pair(ref):
            return jnp.concatenate([ref[r] for r in range(step)], axis=0)

        def turned(ref, base):
            return jnp.concatenate(
                [ref[r, base : base + shard, :] for r in range(step)], axis=1
            )

        grad = jnp.concatenate(
            [
                jnp.concatenate(
                    [late_ref[r, t * lanes : (t + 1) * lanes, :] for t in range(3)], axis=1
                )
                for r in range(step)
            ],
            axis=0,
        ).astype(F32)
        acts_t = turned(acts_ref, 0)
        out_ref[0] += dot_nn(acts_t, (grad * pair(first_ref).astype(F32)).astype(BF16))
        out_ref[1] += dot_nn(acts_t, (grad * pair(second_ref).astype(F32)).astype(BF16))
        out_ref[2] += dot_nn(turned(late_ref, half), pair(hidden_ref))

        @pl.when(index == peers // step - 1)
        def _():
            low_ref[...] = out_ref[...].astype(BF16)

    shape = (3, shard, half)
    return pl.pallas_call(
        body,
        grid=(peers // step,),
        in_specs=[
            pl.BlockSpec((step, *a.shape[1:]), lambda p: (p, 0, 0))
            for a in (first, second, hidden, acts, late)
        ],
        out_specs=[pl.BlockSpec(shape, lambda p: (0, 0, 0))] * 2,
        out_shape=[jax.ShapeDtypeStruct(shape, F32), jax.ShapeDtypeStruct(shape, BF16)],
        compiler_params=limits(16),
        name="last_grads",
    )(*[pltpu.with_memory_space_constraint(a, pltpu.HBM) for a in (first, second, hidden, acts, late)])


def early_out(own_0, own_1, got_1, core):
    count, shard, half = own_0.shape

    def body(core_ref, own_0_ref, own_1_ref, got_1_ref, *outs):
        @pl.when(core_ref[0] == 0)
        def _():
            for i in range(count):
                outs[i][:, :half] = own_0_ref[i]

        @pl.when(core_ref[0] != 0)
        def _():
            for i in range(count):
                outs[i][:, :half] = got_1_ref[i].astype(F32)
                outs[i][:, half:] = own_1_ref[i]

    shape = jax.ShapeDtypeStruct((shard, half * CORES), F32)
    return pl.pallas_call(
        body,
        in_specs=[whole(pltpu.SMEM)] + [whole()] * 3,
        out_specs=[whole()] * count,
        out_shape=[shape] * count,
        compiler_params=limits(8),
        name="early_out",
    )(core, own_0, own_1, got_1)


def late_out(outs, got_0, core):
    count, shard, half = got_0.shape

    def body(core_ref, got_ref, *refs):
        wide_ref, sems = refs[-2:]
        targets = refs[count : 2 * count]

        @pl.when(core_ref[0] == 0)
        def _():
            copies = []
            for i in range(count):
                wide_ref[i] = got_ref[i].astype(F32)
                copy = pltpu.make_async_copy(
                    wide_ref.at[i], targets[i].at[:, half:], sems.at[i]
                )
                copy.start()
                copies.append(copy)
            for copy in copies:
                copy.wait()

    return pl.pallas_call(
        body,
        in_specs=[whole(pltpu.SMEM), whole()] + [whole(pl.ANY)] * count,
        out_specs=[whole(pl.ANY)] * count,
        out_shape=[jax.ShapeDtypeStruct(o.shape, o.dtype) for o in outs],
        scratch_shapes=[
            pltpu.VMEM((count, shard, half), F32),
            pltpu.SemaphoreType.DMA((count,)),
        ],
        input_output_aliases={2 + i: i for i in range(count)},
        compiler_params=limits(8),
        name="late_out",
    )(core, got_0, *outs)


def crossing(partial, residual, source, core, x, core_id, x_id):
    width = partial.shape[1] // XS
    split = partial.shape[0] // CORES
    own = columns_at(partial, x, width)
    pieces = [
        shifted(columns_at(partial, (x + k) % XS, width), "x", k) for k in range(1, XS)
    ]

    total = own.astype(F32)
    for piece in pieces:
        total = total + piece.astype(F32)
    summed = lax.optimization_barrier(total.astype(BF16))
    halves = [summed[:split], summed[split:]]
    received = one_way(halves[1 - source], source)
    mine = jnp.where(core == source, halves[source], received)
    pieces = [shifted(mine, "zh", k) for k in range(1, ZH)]
    total = mine.astype(F32)
    for piece in pieces:
        total = total + piece.astype(F32)
    out = (residual.astype(F32) + total).astype(BF16)
    blocks = [out] + [shifted(out, "x", XS - k) for k in range(1, XS)]
    gathered = assemble(blocks, x_id)
    other = shifted(gathered, "segment", 1)
    return merge(gathered, other, core_id)


def local(tokens, w_gate, w_up, w_down, cotangent):
    return step(tokens, w_gate[0], w_up[0], w_down[0], cotangent)


def step(tokens, gate_w, up_w, down_w, cotangent):
    core = lax.axis_index("segment")
    x = lax.axis_index("x")
    core_id = core.astype(jnp.int32)[None]
    x_id = x.astype(jnp.int32)[None]
    rows = tokens.shape[0]
    features, hidden = gate_w.shape
    half = hidden // CORES

    lent = one_way(down_w[half:], 0)
    down_half = lax.optimization_barrier(jnp.where(core == 0, down_w[:half], lent))
    own = jnp.where(core == 0, tokens.T, cotangent.T)
    gathered = exchanged(jnp.broadcast_to(own, (XS * ZH, *own.shape)), TENSOR)
    entered = gathered.reshape(features, rows)

    gate_a = dot_tn(entered, gate_w).astype(BF16)
    up_a = dot_tn(entered, up_w).astype(BF16)
    hidden_a = hidden_of(gate_a, up_a)
    partial_a = dot_nn(hidden_a, down_w).astype(BF16)
    block = lax.dynamic_slice_in_dim(entered, x * (features // XS), features // XS, 0).T
    first, second = block[: rows // CORES], block[rows // CORES :]
    other = shifted(jnp.where(core == 0, second, first), "segment", 1)
    residual_1 = jnp.where(core == 0, first, other)
    residual_2 = jnp.where(core == 0, other, second)
    middle = crossing(partial_a, residual_1, 0, core, x, core_id, x_id)

    d_hidden_a = lax.optimization_barrier(
        lax.dot_general(
            entered, down_w, (((0,), (1,)), ((), ())), preferred_element_type=F32
        ).astype(BF16)
    )
    outgoing = picked([[(gate_a, 1), (up_a, 1)], [(d_hidden_a, 0)]], core_id)
    given = shifted(outgoing, "segment", 1)
    load = packed(
        [(gate_a, 0, 0), (up_a, 0, 1), (d_hidden_a, 1, 0)], given, entered, core_id
    )
    wide = exchanged(load, DP)

    wide_a = wide
    entered_all = wide[:, 3 * half :]
    entered_other = shifted(entered_all, "segment", 1)

    gate_b = dot_nn(middle, gate_w).astype(BF16)
    up_b = dot_nn(middle, up_w).astype(BF16)
    d_gate_b, d_up_b = gate_grads(d_hidden_a.astype(F32), gate_b, up_b)
    partial_b = (dot_nt(d_gate_b, gate_w) + dot_nt(d_up_b, up_w)).astype(BF16)
    upstream = crossing(partial_b, residual_2, 1, core, x, core_id, x_id)

    picks = [(gate_b, 0), (up_b, 0)]
    outgoing = picked([picks, picks], core_id)
    given = one_way(outgoing, 1)
    load = packed([(gate_b, 1, 0), (up_b, 1, 1)], given, (middle,), core_id)
    load, wide_a = lax.optimization_barrier((load, wide_a))
    wide_b = exchanged(load, DP)

    d_hidden_b = dot_nt(upstream, down_half).astype(BF16)
    load = packed([(d_hidden_b, None, 0)], None, (upstream,), core_id)
    load, wide_b = lax.optimization_barrier((load, wide_b))
    wide_c = exchanged(load, DP)

    own_1, low_1 = weight_grads(
        (wide_b, 0),
        (wide_a, 2 * half),
        ("own", wide_b, 2 * half),
        ("pick", 1, wide_a, 3 * half, entered_other),
        core_id,
    )
    got_1 = one_way(low_1, 0)
    first, second, hidden_0, tokens_all = coefficients(wide_a, entered_other, core_id)
    own_0, low_0 = last_grads(first, second, hidden_0, tokens_all, wide_c)
    got_0 = one_way(low_0, 1)
    outs = early_out(own_0, own_1, got_1, core_id)
    grad_gate, grad_up, grad_down = late_out(outs, got_0, core_id)
    return (grad_gate[None], grad_up[None], grad_down.T[None])


def solution(mesh):
    fine = Mesh(
        mesh.devices.reshape(CORES, XS, ZH, ZL, YS), ("segment", "x", "zh", "zl", "y")
    )
    in_specs = (
        P(DP, TENSOR),
        P("segment", None, TENSOR),
        P("segment", None, TENSOR),
        P("segment", TENSOR, None),
        P(DP, TENSOR),
    )
    out_specs = (
        P("segment", DP, TENSOR),
        P("segment", DP, TENSOR),
        P("segment", TENSOR, DP),
    )
    return jax.shard_map(
        local, mesh=fine, in_specs=in_specs, out_specs=out_specs, check_vma=False
    )
```

```python
import jax
import jax.numpy as jnp
from jax import lax
from jax.experimental import pallas as pl
from jax.experimental.pallas import tpu as pltpu
from jax.sharding import Mesh, PartitionSpec as P

CORES = 2
XS = 4
ZH = 4
ZL = 2
YS = 4
PEERS = ZL * YS
LANES = 128
TENSOR = ("x", "zh")
DP = ("zl", "y")
BF16 = jnp.bfloat16
F32 = jnp.float32


def shifted(value, axis, distance):
    size = lax.axis_size(axis)
    return lax.ppermute(value, axis, [(i, (i + distance) % size) for i in range(size)])


def one_way(value, source):
    return lax.ppermute(value, "segment", [(source, 1 - source)])


def exchanged(value, axes):
    return lax.all_to_all(value, axes, 0, 0, tiled=True)


def dot_tn(left, right):
    return lax.dot_general(left, right, (((0,), (0,)), ((), ())), preferred_element_type=F32)


def dot_nt(left, right):
    return lax.dot_general(left, right, (((1,), (1,)), ((), ())), preferred_element_type=F32)


def dot_nn(left, right):
    return jnp.dot(left, right, preferred_element_type=F32)


def whole(memory_space=pltpu.VMEM):
    return pl.BlockSpec(memory_space=memory_space)


def hidden_of(gate, up):
    gate = gate.astype(F32)
    return (jax.nn.silu(gate) * up.astype(F32)).astype(BF16)


def gate_grads(d_hidden, gate, up):
    gate = gate.astype(F32)
    up = up.astype(F32)
    sigma = jax.nn.sigmoid(gate)
    d_gate = (d_hidden * up * sigma * (1.0 + gate * (1.0 - sigma))).astype(BF16)
    d_up = (d_hidden * gate * sigma).astype(BF16)
    return d_gate, d_up


def limits(mebibytes):
    return pltpu.CompilerParams(vmem_limit_bytes=mebibytes * 2**20)


def columns_at(value, index, width):
    return lax.dynamic_slice_in_dim(value, index * width, width, 1)


def assemble(blocks, x):
    rows, width = blocks[0].shape

    def body(x_ref, *refs):
        out_ref = refs[-1]
        for k in range(XS):
            start = pl.multiple_of(((x_ref[0] + k) % XS) * width, LANES)
            out_ref[:, pl.ds(start, width)] = refs[k][...]

    return pl.pallas_call(
        body,
        in_specs=[whole(pltpu.SMEM)] + [whole()] * XS,
        out_specs=whole(),
        out_shape=jax.ShapeDtypeStruct((rows, width * XS), BF16),
        compiler_params=limits(2),
        name="assemble",
    )(x, *blocks)


def merge(own, other, core):
    rows, width = own.shape

    def body(core_ref, own_ref, other_ref, out_ref):
        start = pl.multiple_of(core_ref[0] * rows, 16)
        out_ref[pl.ds(start, rows), :] = own_ref[...]
        start = pl.multiple_of((1 - core_ref[0]) * rows, 16)
        out_ref[pl.ds(start, rows), :] = other_ref[...]

    return pl.pallas_call(
        body,
        in_specs=[whole(pltpu.SMEM), whole(), whole()],
        out_specs=whole(),
        out_shape=jax.ShapeDtypeStruct((rows * CORES, width), BF16),
        compiler_params=limits(2),
        name="merge",
    )(core, own, other)


def picked(by_core, core):
    rows, width = by_core[0][0][0].shape
    half = width // CORES
    count = max(len(picks) for picks in by_core)
    values = []
    for picks in by_core:
        for value, _ in picks:
            if not any(value is known for known in values):
                values.append(value)

    def body(core_ref, *refs):
        out_ref = refs[-1]
        for c, picks in enumerate(by_core):

            @pl.when(core_ref[0] == c)
            def _(picks=picks):
                for slot in range(count):
                    value, side = picks[min(slot, len(picks) - 1)]
                    at = [value is known for known in values].index(True)
                    out_ref[slot] = refs[at][:, side * half : (side + 1) * half]

    return pl.pallas_call(
        body,
        in_specs=[whole(pltpu.SMEM)] + [whole()] * len(values),
        out_specs=whole(),
        out_shape=jax.ShapeDtypeStruct((count, rows, half), BF16),
        compiler_params=limits(4),
        name="picked",
    )(core, *values)


def packed(choices, given, acts, core):
    rows = choices[0][0].shape[0]
    half = choices[0][0].shape[1] // (1 if given is None else CORES)
    tiles = half // LANES
    turned = isinstance(acts, tuple)
    features = acts[0].shape[1] if turned else acts.shape[0]
    shard = features // PEERS
    count = len(choices)
    height = count * tiles * rows + shard
    values = [choice[0] for choice in choices]
    specs = [pl.BlockSpec(value.shape, lambda p: (0, 0)) for value in values]
    if given is not None:
        values.append(given)
        specs.append(pl.BlockSpec(given.shape, lambda p: (0, 0, 0)))
    if turned:
        values.append(acts[0])
        specs.append(pl.BlockSpec(acts[0].shape, lambda p: (0, 0)))
    else:
        values.append(acts)
        specs.append(pl.BlockSpec((shard, rows), lambda p: (p, 0)))

    def body(core_ref, *refs):
        given_ref = None if given is None else refs[count]
        out_ref = refs[len(values)]
        peer = pl.program_id(0)
        for c, (_, source, slot) in enumerate(choices):
            for t in range(tiles):
                base = (c * tiles + t) * rows
                first = (source or 0) * half + t * LANES
                tile = refs[c][:, first : first + LANES]
                if source is not None:
                    other = given_ref[slot, :, t * LANES : (t + 1) * LANES]
                    tile = jnp.where(core_ref[0] == source, tile, other)
                out_ref[0, base : base + rows, :] = tile
        if turned:
            acts_ref = refs[len(values) - 1]
            turned_ref = refs[-1]

            @pl.when(peer == 0)
            def _():
                for t in range(features // LANES):
                    at = slice(t * LANES, (t + 1) * LANES)
                    turned_ref[at, :] = acts_ref[:, at].T

            start = pl.multiple_of(peer * shard, 64)
            out_ref[0, count * tiles * rows :, :] = turned_ref[pl.ds(start, shard), :]
        else:
            out_ref[0, count * tiles * rows :, :] = refs[len(values) - 1][...]

    return pl.pallas_call(
        body,
        grid=(PEERS,),
        in_specs=[whole(pltpu.SMEM)] + specs,
        out_specs=pl.BlockSpec((1, height, rows), lambda p: (p, 0, 0)),
        out_shape=jax.ShapeDtypeStruct((PEERS, height, rows), BF16),
        scratch_shapes=[pltpu.VMEM((features, rows), BF16)] if turned else [],
        compiler_params=limits(8),
        name="packed",
    )(core, *values)


def weight_grads(gate, up, d_hidden, acts, upstream, core):
    step = 2
    lanes = gate[0].shape[2]
    half = 3 * lanes
    shard = 192
    values = []
    specs = []

    def add(value, rows, index):
        values.append(value)
        specs.append(pl.BlockSpec((step, rows, lanes), lambda p: (p, index, 0)))

    for value, index in (gate, up, d_hidden):
        add(value, half, index)
    for operand in (acts, upstream):
        add(operand[0], shard, operand[1])
        if len(operand) > 2:
            add(operand[3], shard, 0)

    def body(core_ref, *refs):
        ins = list(refs[: len(values)])
        out_ref, low_ref = refs[len(values) :]
        index = pl.program_id(0)

        @pl.when(index == 0)
        def _():
            out_ref[...] = jnp.zeros_like(out_ref)

        def wide(ref):
            rows = [
                jnp.concatenate(
                    [ref[r, t * lanes : (t + 1) * lanes, :] for t in range(3)], axis=1
                )
                for r in range(step)
            ]
            return jnp.concatenate(rows, axis=0)

        def features(operand):
            ref = ins.pop(0)
            blocks = [ref[r] for r in range(step)]
            if len(operand) > 2:
                other = ins.pop(0)
                mine = core_ref[0] == operand[2]
                blocks = [jnp.where(mine, blocks[r], other[r]) for r in range(step)]
            return jnp.concatenate(blocks, axis=1)

        gate_v = wide(ins.pop(0)).astype(F32)
        up_v = wide(ins.pop(0)).astype(F32)
        grad = wide(ins.pop(0)).astype(F32)
        sigma = jax.nn.sigmoid(gate_v)
        silu = gate_v * sigma
        d_gate = (grad * up_v * sigma * (1.0 + gate_v * (1.0 - sigma))).astype(BF16)
        d_up = (grad * silu).astype(BF16)
        acts_t = features(acts)
        out_ref[0] += dot_nn(acts_t, d_gate)
        out_ref[1] += dot_nn(acts_t, d_up)
        out_ref[2] += dot_nn(features(upstream), (silu * up_v).astype(BF16))

        @pl.when(index == PEERS // step - 1)
        def _():
            low_ref[...] = out_ref[...].astype(BF16)

    shape = (3, shard, half)
    return pl.pallas_call(
        body,
        grid=(PEERS // step,),
        in_specs=[whole(pltpu.SMEM)] + specs,
        out_specs=[pl.BlockSpec(shape, lambda p: (0, 0, 0))] * 2,
        out_shape=[jax.ShapeDtypeStruct(shape, F32), jax.ShapeDtypeStruct(shape, BF16)],
        compiler_params=limits(16),
    )(core, *[pltpu.with_memory_space_constraint(v, pltpu.HBM) for v in values])


def early_out(own_0, own_1, got_1, core):
    count, shard, half = own_0.shape

    def body(core_ref, own_0_ref, own_1_ref, got_1_ref, *outs):
        @pl.when(core_ref[0] == 0)
        def _():
            for i in range(count):
                outs[i][:, :half] = own_0_ref[i]

        @pl.when(core_ref[0] != 0)
        def _():
            for i in range(count):
                outs[i][:, :half] = got_1_ref[i].astype(F32)
                outs[i][:, half:] = own_1_ref[i]

    shape = jax.ShapeDtypeStruct((shard, half * CORES), F32)
    return pl.pallas_call(
        body,
        in_specs=[whole(pltpu.SMEM)] + [whole()] * 3,
        out_specs=[whole()] * count,
        out_shape=[shape] * count,
        compiler_params=limits(8),
        name="early_out",
    )(core, own_0, own_1, got_1)


def late_out(outs, got_0, core):
    count, shard, half = got_0.shape

    def body(core_ref, got_ref, *refs):
        wide_ref, sems = refs[-2:]
        targets = refs[count : 2 * count]

        @pl.when(core_ref[0] == 0)
        def _():
            copies = []
            for i in range(count):
                wide_ref[i] = got_ref[i].astype(F32)
                copy = pltpu.make_async_copy(
                    wide_ref.at[i], targets[i].at[:, half:], sems.at[i]
                )
                copy.start()
                copies.append(copy)
            for copy in copies:
                copy.wait()

    return pl.pallas_call(
        body,
        in_specs=[whole(pltpu.SMEM), whole()] + [whole(pl.ANY)] * count,
        out_specs=[whole(pl.ANY)] * count,
        out_shape=[jax.ShapeDtypeStruct(o.shape, o.dtype) for o in outs],
        scratch_shapes=[
            pltpu.VMEM((count, shard, half), F32),
            pltpu.SemaphoreType.DMA((count,)),
        ],
        input_output_aliases={2 + i: i for i in range(count)},
        compiler_params=limits(8),
        name="late_out",
    )(core, got_0, *outs)


def crossing(partial, residual, source, core, x, core_id, x_id):
    width = partial.shape[1] // XS
    split = partial.shape[0] // CORES
    own = columns_at(partial, x, width)
    pieces = [
        shifted(columns_at(partial, (x + k) % XS, width), "x", k) for k in range(1, XS)
    ]

    total = own.astype(F32)
    for piece in pieces:
        total = total + piece.astype(F32)
    summed = lax.optimization_barrier(total.astype(BF16))
    halves = [summed[:split], summed[split:]]
    received = one_way(halves[1 - source], source)
    mine = jnp.where(core == source, halves[source], received)
    pieces = [shifted(mine, "zh", k) for k in range(1, ZH)]
    total = mine.astype(F32)
    for piece in pieces:
        total = total + piece.astype(F32)
    out = (residual.astype(F32) + total).astype(BF16)
    blocks = [out] + [shifted(out, "x", XS - k) for k in range(1, XS)]
    gathered = assemble(blocks, x_id)
    other = shifted(gathered, "segment", 1)
    return merge(gathered, other, core_id)


def local(tokens, w_gate, w_up, w_down, cotangent):
    return step(tokens, w_gate[0], w_up[0], w_down[0], cotangent)


def step(tokens, gate_w, up_w, down_w, cotangent):
    core = lax.axis_index("segment")
    x = lax.axis_index("x")
    core_id = core.astype(jnp.int32)[None]
    x_id = x.astype(jnp.int32)[None]
    rows = tokens.shape[0]
    features, hidden = gate_w.shape
    half = hidden // CORES

    lent = one_way(down_w[half:], 0)
    down_half = lax.optimization_barrier(jnp.where(core == 0, down_w[:half], lent))
    own = jnp.where(core == 0, tokens.T, cotangent.T)
    gathered = exchanged(jnp.broadcast_to(own, (XS * ZH, *own.shape)), TENSOR)
    entered = gathered.reshape(features, rows)

    gate_a = dot_tn(entered, gate_w).astype(BF16)
    up_a = dot_tn(entered, up_w).astype(BF16)
    hidden_a = hidden_of(gate_a, up_a)
    partial_a = dot_nn(hidden_a, down_w).astype(BF16)
    block = lax.dynamic_slice_in_dim(entered, x * (features // XS), features // XS, 0).T
    first, second = block[: rows // CORES], block[rows // CORES :]
    other = shifted(jnp.where(core == 0, second, first), "segment", 1)
    residual_1 = jnp.where(core == 0, first, other)
    residual_2 = jnp.where(core == 0, other, second)
    middle = crossing(partial_a, residual_1, 0, core, x, core_id, x_id)

    d_hidden_a = lax.dot_general(
        entered, down_w, (((0,), (1,)), ((), ())), preferred_element_type=F32
    ).astype(BF16)
    d_hidden_a = lax.optimization_barrier(d_hidden_a)
    outgoing = picked([[(gate_a, 1), (up_a, 1)], [(d_hidden_a, 0)]], core_id)
    given = shifted(outgoing, "segment", 1)
    load = packed(
        [(gate_a, 0, 0), (up_a, 0, 1), (d_hidden_a, 1, 0)], given, entered, core_id
    )
    wide = exchanged(load, DP)

    wide_a = wide
    entered_all = wide[:, 3 * half :]
    entered_other = shifted(entered_all, "segment", 1)

    gate_b = dot_nn(middle, gate_w).astype(BF16)
    up_b = dot_nn(middle, up_w).astype(BF16)
    d_gate_b, d_up_b = gate_grads(d_hidden_a.astype(F32), gate_b, up_b)
    partial_b = (dot_nt(d_gate_b, gate_w) + dot_nt(d_up_b, up_w)).astype(BF16)
    upstream = crossing(partial_b, residual_2, 1, core, x, core_id, x_id)

    picks = [(gate_b, 0), (up_b, 0)]
    outgoing = picked([picks, picks], core_id)
    given = one_way(outgoing, 1)
    load = packed([(gate_b, 1, 0), (up_b, 1, 1)], given, (middle,), core_id)
    load, wide_a = lax.optimization_barrier((load, wide_a))
    wide_b = exchanged(load, DP)

    d_hidden_b = dot_nt(upstream, down_half).astype(BF16)
    d_hidden_b, wide_b = lax.optimization_barrier((d_hidden_b, wide_b))
    load = packed([(d_hidden_b, None, 0)], None, (upstream,), core_id)
    wide_c = exchanged(load, DP)

    own_1, low_1 = weight_grads(
        (wide_b, 0),
        (wide_b, 1),
        (wide_a, 2),
        (wide_b, 4),
        (wide_a, 6, 1, entered_other),
        core_id,
    )
    got_1 = one_way(low_1, 0)
    own_0, low_0 = weight_grads(
        (wide_a, 0),
        (wide_a, 1),
        (wide_c, 0),
        (wide_a, 6, 0, entered_other),
        (wide_c, 2),
        core_id,
    )
    got_0 = one_way(low_0, 1)
    outs = early_out(own_0, own_1, got_1, core_id)
    grad_gate, grad_up, grad_down = late_out(outs, got_0, core_id)
    return (grad_gate[None], grad_up[None], grad_down.T[None])


def solution(mesh):
    fine = Mesh(
        mesh.devices.reshape(CORES, XS, ZH, ZL, YS), ("segment", "x", "zh", "zl", "y")
    )
    in_specs = (
        P(DP, TENSOR),
        P("segment", None, TENSOR),
        P("segment", None, TENSOR),
        P("segment", TENSOR, None),
        P(DP, TENSOR),
    )
    out_specs = (
        P("segment", DP, TENSOR),
        P("segment", DP, TENSOR),
        P("segment", TENSOR, DP),
    )
    return jax.shard_map(
        local, mesh=fine, in_specs=in_specs, out_specs=out_specs, check_vma=False
    )
```

```python
import jax
import jax.numpy as jnp
from jax import lax
from jax.experimental import pallas as pl
from jax.experimental.pallas import tpu as pltpu
from jax.sharding import Mesh, PartitionSpec as P

CORES = 2
XS = 4
ZH = 4
ZL = 2
YS = 4
PEERS = ZL * YS
LANES = 128
TENSOR = ("x", "zh")
DP = ("zl", "y")
BF16 = jnp.bfloat16
F32 = jnp.float32


def shifted(value, axis, distance):
    size = lax.axis_size(axis)
    return lax.ppermute(value, axis, [(i, (i + distance) % size) for i in range(size)])


def one_way(value, source):
    return lax.ppermute(value, "segment", [(source, 1 - source)])


def exchanged(value, axes):
    return lax.all_to_all(value, axes, 0, 0, tiled=True)


def dot_tn(left, right):
    return lax.dot_general(left, right, (((0,), (0,)), ((), ())), preferred_element_type=F32)


def dot_nt(left, right):
    return lax.dot_general(left, right, (((1,), (1,)), ((), ())), preferred_element_type=F32)


def dot_nn(left, right):
    return jnp.dot(left, right, preferred_element_type=F32)


def whole(memory_space=pltpu.VMEM):
    return pl.BlockSpec(memory_space=memory_space)


def hidden_of(gate, up):
    gate = gate.astype(F32)
    return (jax.nn.silu(gate) * up.astype(F32)).astype(BF16)


def gate_grads(d_hidden, gate, up):
    gate = gate.astype(F32)
    up = up.astype(F32)
    sigma = jax.nn.sigmoid(gate)
    d_gate = (d_hidden * up * sigma * (1.0 + gate * (1.0 - sigma))).astype(BF16)
    d_up = (d_hidden * gate * sigma).astype(BF16)
    return d_gate, d_up


def limits(mebibytes):
    return pltpu.CompilerParams(vmem_limit_bytes=mebibytes * 2**20)


def columns_at(value, index, width):
    return lax.dynamic_slice_in_dim(value, index * width, width, 1)


def assemble(blocks, x):
    rows, width = blocks[0].shape

    def body(x_ref, *refs):
        out_ref = refs[-1]
        for k in range(XS):
            start = pl.multiple_of(((x_ref[0] + k) % XS) * width, LANES)
            out_ref[:, pl.ds(start, width)] = refs[k][...]

    return pl.pallas_call(
        body,
        in_specs=[whole(pltpu.SMEM)] + [whole()] * XS,
        out_specs=whole(),
        out_shape=jax.ShapeDtypeStruct((rows, width * XS), BF16),
        compiler_params=limits(2),
        name="assemble",
    )(x, *blocks)


def merge(own, other, core):
    rows, width = own.shape

    def body(core_ref, own_ref, other_ref, out_ref):
        start = pl.multiple_of(core_ref[0] * rows, 16)
        out_ref[pl.ds(start, rows), :] = own_ref[...]
        start = pl.multiple_of((1 - core_ref[0]) * rows, 16)
        out_ref[pl.ds(start, rows), :] = other_ref[...]

    return pl.pallas_call(
        body,
        in_specs=[whole(pltpu.SMEM), whole(), whole()],
        out_specs=whole(),
        out_shape=jax.ShapeDtypeStruct((rows * CORES, width), BF16),
        compiler_params=limits(2),
        name="merge",
    )(core, own, other)


def picked(by_core, core):
    rows, width = by_core[0][0][0].shape
    half = width // CORES
    count = max(len(picks) for picks in by_core)
    values = []
    for picks in by_core:
        for value, _ in picks:
            if not any(value is known for known in values):
                values.append(value)

    def body(core_ref, *refs):
        out_ref = refs[-1]
        for c, picks in enumerate(by_core):

            @pl.when(core_ref[0] == c)
            def _(picks=picks):
                for slot in range(count):
                    value, side = picks[min(slot, len(picks) - 1)]
                    at = [value is known for known in values].index(True)
                    out_ref[slot] = refs[at][:, side * half : (side + 1) * half]

    return pl.pallas_call(
        body,
        in_specs=[whole(pltpu.SMEM)] + [whole()] * len(values),
        out_specs=whole(),
        out_shape=jax.ShapeDtypeStruct((count, rows, half), BF16),
        compiler_params=limits(4),
        name="picked",
    )(core, *values)


def packed(choices, given, acts, core):
    rows = choices[0][0].shape[0]
    half = choices[0][0].shape[1] // (1 if given is None else CORES)
    tiles = half // LANES
    group = 4
    turned = isinstance(acts, tuple)
    features = acts[0].shape[1] if turned else acts.shape[0]
    shard = features // PEERS
    count = len(choices)
    height = count * tiles * rows + shard
    values = [choice[0] for choice in choices]
    specs = [pl.BlockSpec(value.shape, lambda p: (0, 0)) for value in values]
    if given is not None:
        values.append(given)
        specs.append(pl.BlockSpec(given.shape, lambda p: (0, 0, 0)))
    if turned:
        values.append(acts[0])
        specs.append(pl.BlockSpec(acts[0].shape, lambda p: (0, 0)))
    else:
        values.append(acts)
        specs.append(pl.BlockSpec((group * shard, rows), lambda p: (p, 0)))

    def body(core_ref, *refs):
        given_ref = None if given is None else refs[count]
        out_ref = refs[len(values)]
        index = pl.program_id(0)
        for c, (_, source, slot) in enumerate(choices):
            for t in range(tiles):
                base = (c * tiles + t) * rows
                first = (source or 0) * half + t * LANES
                tile = refs[c][:, first : first + LANES]
                if source is not None:
                    other = given_ref[slot, :, t * LANES : (t + 1) * LANES]
                    tile = jnp.where(core_ref[0] == source, tile, other)
                for g in range(group):
                    out_ref[g, base : base + rows, :] = tile
        if turned:
            acts_ref = refs[len(values) - 1]
            turned_ref = refs[-1]

            @pl.when(index == 0)
            def _():
                for t in range(features // LANES):
                    at = slice(t * LANES, (t + 1) * LANES)
                    turned_ref[at, :] = acts_ref[:, at].T

            for g in range(group):
                start = pl.multiple_of((index * group + g) * shard, 64)
                out_ref[g, count * tiles * rows :, :] = turned_ref[pl.ds(start, shard), :]
        else:
            acts_ref = refs[len(values) - 1]
            for g in range(group):
                at = slice(g * shard, (g + 1) * shard)
                out_ref[g, count * tiles * rows :, :] = acts_ref[at, :]

    return pl.pallas_call(
        body,
        grid=(PEERS // group,),
        in_specs=[whole(pltpu.SMEM)] + specs,
        out_specs=pl.BlockSpec((group, height, rows), lambda p: (p, 0, 0)),
        out_shape=jax.ShapeDtypeStruct((PEERS, height, rows), BF16),
        scratch_shapes=[pltpu.VMEM((features, rows), BF16)] if turned else [],
        compiler_params=limits(8),
        name="packed",
    )(core, *values)


def weight_grads(gate, up, d_hidden, acts, upstream, core):
    step = 2
    lanes = gate[0].shape[2]
    half = 3 * lanes
    shard = 192
    values = []
    specs = []

    def add(value, rows, index):
        values.append(value)
        specs.append(pl.BlockSpec((step, rows, lanes), lambda p: (p, index, 0)))

    for value, index in (gate, up, d_hidden):
        add(value, half, index)
    for operand in (acts, upstream):
        add(operand[0], shard, operand[1])
        if len(operand) > 2:
            add(operand[3], shard, 0)

    def body(core_ref, *refs):
        ins = list(refs[: len(values)])
        out_ref, low_ref = refs[len(values) :]
        index = pl.program_id(0)

        @pl.when(index == 0)
        def _():
            out_ref[...] = jnp.zeros_like(out_ref)

        def wide(ref):
            rows = [
                jnp.concatenate(
                    [ref[r, t * lanes : (t + 1) * lanes, :] for t in range(3)], axis=1
                )
                for r in range(step)
            ]
            return jnp.concatenate(rows, axis=0)

        def features(operand):
            ref = ins.pop(0)
            blocks = [ref[r] for r in range(step)]
            if len(operand) > 2:
                other = ins.pop(0)
                mine = core_ref[0] == operand[2]
                blocks = [jnp.where(mine, blocks[r], other[r]) for r in range(step)]
            return jnp.concatenate(blocks, axis=1)

        gate_v = wide(ins.pop(0)).astype(F32)
        up_v = wide(ins.pop(0)).astype(F32)
        grad = wide(ins.pop(0)).astype(F32)
        sigma = jax.nn.sigmoid(gate_v)
        silu = gate_v * sigma
        d_gate = (grad * up_v * sigma * (1.0 + gate_v * (1.0 - sigma))).astype(BF16)
        d_up = (grad * silu).astype(BF16)
        acts_t = features(acts)
        out_ref[0] += dot_nn(acts_t, d_gate)
        out_ref[1] += dot_nn(acts_t, d_up)
        out_ref[2] += dot_nn(features(upstream), (silu * up_v).astype(BF16))

        @pl.when(index == PEERS // step - 1)
        def _():
            low_ref[...] = out_ref[...].astype(BF16)

    shape = (3, shard, half)
    return pl.pallas_call(
        body,
        grid=(PEERS // step,),
        in_specs=[whole(pltpu.SMEM)] + specs,
        out_specs=[pl.BlockSpec(shape, lambda p: (0, 0, 0))] * 2,
        out_shape=[jax.ShapeDtypeStruct(shape, F32), jax.ShapeDtypeStruct(shape, BF16)],
        compiler_params=limits(16),
    )(core, *[pltpu.with_memory_space_constraint(v, pltpu.HBM) for v in values])


def early_out(own_0, own_1, got_1, core):
    count, shard, half = own_0.shape

    def body(core_ref, own_0_ref, own_1_ref, got_1_ref, *outs):
        @pl.when(core_ref[0] == 0)
        def _():
            for i in range(count):
                outs[i][:, :half] = own_0_ref[i]

        @pl.when(core_ref[0] != 0)
        def _():
            for i in range(count):
                outs[i][:, :half] = got_1_ref[i].astype(F32)
                outs[i][:, half:] = own_1_ref[i]

    shape = jax.ShapeDtypeStruct((shard, half * CORES), F32)
    return pl.pallas_call(
        body,
        in_specs=[whole(pltpu.SMEM)] + [whole()] * 3,
        out_specs=[whole()] * count,
        out_shape=[shape] * count,
        compiler_params=limits(8),
        name="early_out",
    )(core, own_0, own_1, got_1)


def late_out(outs, got_0, core):
    count, shard, half = got_0.shape

    def body(core_ref, got_ref, *refs):
        wide_ref, sems = refs[-2:]
        targets = refs[count : 2 * count]

        @pl.when(core_ref[0] == 0)
        def _():
            copies = []
            for i in range(count):
                wide_ref[i] = got_ref[i].astype(F32)
                copy = pltpu.make_async_copy(
                    wide_ref.at[i], targets[i].at[:, half:], sems.at[i]
                )
                copy.start()
                copies.append(copy)
            for copy in copies:
                copy.wait()

    return pl.pallas_call(
        body,
        in_specs=[whole(pltpu.SMEM), whole()] + [whole(pl.ANY)] * count,
        out_specs=[whole(pl.ANY)] * count,
        out_shape=[jax.ShapeDtypeStruct(o.shape, o.dtype) for o in outs],
        scratch_shapes=[
            pltpu.VMEM((count, shard, half), F32),
            pltpu.SemaphoreType.DMA((count,)),
        ],
        input_output_aliases={2 + i: i for i in range(count)},
        compiler_params=limits(8),
        name="late_out",
    )(core, got_0, *outs)


def crossing(partial, residual, source, core, x, core_id, x_id):
    width = partial.shape[1] // XS
    split = partial.shape[0] // CORES
    own = columns_at(partial, x, width)
    pieces = [
        shifted(columns_at(partial, (x + k) % XS, width), "x", k) for k in range(1, XS)
    ]

    total = own.astype(F32)
    for piece in pieces:
        total = total + piece.astype(F32)
    summed = lax.optimization_barrier(total.astype(BF16))
    halves = [summed[:split], summed[split:]]
    received = one_way(halves[1 - source], source)
    mine = jnp.where(core == source, halves[source], received)
    pieces = [shifted(mine, "zh", k) for k in range(1, ZH)]
    total = mine.astype(F32)
    for piece in pieces:
        total = total + piece.astype(F32)
    out = (residual.astype(F32) + total).astype(BF16)
    blocks = [out] + [shifted(out, "x", XS - k) for k in range(1, XS)]
    gathered = assemble(blocks, x_id)
    other = shifted(gathered, "segment", 1)
    return merge(gathered, other, core_id)


def local(tokens, w_gate, w_up, w_down, cotangent):
    return step(tokens, w_gate[0], w_up[0], w_down[0], cotangent)


def step(tokens, gate_w, up_w, down_w, cotangent):
    core = lax.axis_index("segment")
    x = lax.axis_index("x")
    core_id = core.astype(jnp.int32)[None]
    x_id = x.astype(jnp.int32)[None]
    rows = tokens.shape[0]
    features, hidden = gate_w.shape
    half = hidden // CORES

    lent = one_way(down_w[half:], 0)
    down_half = lax.optimization_barrier(jnp.where(core == 0, down_w[:half], lent))
    own = jnp.where(core == 0, tokens.T, cotangent.T)
    gathered = exchanged(jnp.broadcast_to(own, (XS * ZH, *own.shape)), TENSOR)
    entered = gathered.reshape(features, rows)

    gate_a = dot_tn(entered, gate_w).astype(BF16)
    up_a = dot_tn(entered, up_w).astype(BF16)
    hidden_a = hidden_of(gate_a, up_a)
    partial_a = dot_nn(hidden_a, down_w).astype(BF16)
    block = lax.dynamic_slice_in_dim(entered, x * (features // XS), features // XS, 0).T
    first, second = block[: rows // CORES], block[rows // CORES :]
    other = shifted(jnp.where(core == 0, second, first), "segment", 1)
    residual_1 = jnp.where(core == 0, first, other)
    residual_2 = jnp.where(core == 0, other, second)
    middle = crossing(partial_a, residual_1, 0, core, x, core_id, x_id)

    d_hidden_a = lax.dot_general(
        entered, down_w, (((0,), (1,)), ((), ())), preferred_element_type=F32
    ).astype(BF16)
    d_hidden_a = lax.optimization_barrier(d_hidden_a)
    outgoing = picked([[(gate_a, 1), (up_a, 1)], [(d_hidden_a, 0)]], core_id)
    given = shifted(outgoing, "segment", 1)
    load = packed(
        [(gate_a, 0, 0), (up_a, 0, 1), (d_hidden_a, 1, 0)], given, entered, core_id
    )
    wide = exchanged(load, DP)

    wide_a = wide
    entered_all = wide[:, 3 * half :]
    entered_other = shifted(entered_all, "segment", 1)

    gate_b = dot_nn(middle, gate_w).astype(BF16)
    up_b = dot_nn(middle, up_w).astype(BF16)
    d_gate_b, d_up_b = gate_grads(d_hidden_a.astype(F32), gate_b, up_b)
    partial_b = (dot_nt(d_gate_b, gate_w) + dot_nt(d_up_b, up_w)).astype(BF16)
    upstream = crossing(partial_b, residual_2, 1, core, x, core_id, x_id)

    picks = [(gate_b, 0), (up_b, 0)]
    outgoing = picked([picks, picks], core_id)
    given = one_way(outgoing, 1)
    load = packed([(gate_b, 1, 0), (up_b, 1, 1)], given, (middle,), core_id)
    load, wide_a = lax.optimization_barrier((load, wide_a))
    wide_b = exchanged(load, DP)

    d_hidden_b = dot_nt(upstream, down_half).astype(BF16)
    d_hidden_b, wide_b = lax.optimization_barrier((d_hidden_b, wide_b))
    load = packed([(d_hidden_b, None, 0)], None, (upstream,), core_id)
    wide_c = exchanged(load, DP)

    own_1, low_1 = weight_grads(
        (wide_b, 0),
        (wide_b, 1),
        (wide_a, 2),
        (wide_b, 4),
        (wide_a, 6, 1, entered_other),
        core_id,
    )
    got_1 = one_way(low_1, 0)
    own_0, low_0 = weight_grads(
        (wide_a, 0),
        (wide_a, 1),
        (wide_c, 0),
        (wide_a, 6, 0, entered_other),
        (wide_c, 2),
        core_id,
    )
    got_0 = one_way(low_0, 1)
    outs = early_out(own_0, own_1, got_1, core_id)
    grad_gate, grad_up, grad_down = late_out(outs, got_0, core_id)
    return (grad_gate[None], grad_up[None], grad_down.T[None])


def solution(mesh):
    fine = Mesh(
        mesh.devices.reshape(CORES, XS, ZH, ZL, YS), ("segment", "x", "zh", "zl", "y")
    )
    in_specs = (
        P(DP, TENSOR),
        P("segment", None, TENSOR),
        P("segment", None, TENSOR),
        P("segment", TENSOR, None),
        P(DP, TENSOR),
    )
    out_specs = (
        P("segment", DP, TENSOR),
        P("segment", DP, TENSOR),
        P("segment", TENSOR, DP),
    )
    return jax.shard_map(
        local, mesh=fine, in_specs=in_specs, out_specs=out_specs, check_vma=False
    )
```

```python
import jax
import jax.numpy as jnp
from jax import lax
from jax.experimental import pallas as pl
from jax.experimental.pallas import tpu as pltpu
from jax.sharding import Mesh, PartitionSpec as P

CORES = 2
XS = 4
ZH = 4
ZL = 2
YS = 4
PEERS = ZL * YS
LANES = 128
TENSOR = ("x", "zh")
DP = ("zl", "y")
BF16 = jnp.bfloat16
F32 = jnp.float32


def shifted(value, axis, distance):
    size = lax.axis_size(axis)
    return lax.ppermute(value, axis, [(i, (i + distance) % size) for i in range(size)])


def one_way(value, source):
    return lax.ppermute(value, "segment", [(source, 1 - source)])


def exchanged(value, axes):
    return lax.all_to_all(value, axes, 0, 0, tiled=True)


def dot_tn(left, right):
    return lax.dot_general(left, right, (((0,), (0,)), ((), ())), preferred_element_type=F32)


def dot_nt(left, right):
    return lax.dot_general(left, right, (((1,), (1,)), ((), ())), preferred_element_type=F32)


def dot_nn(left, right):
    return jnp.dot(left, right, preferred_element_type=F32)


def whole(memory_space=pltpu.VMEM):
    return pl.BlockSpec(memory_space=memory_space)


def hidden_of(gate, up):
    gate = gate.astype(F32)
    return (jax.nn.silu(gate) * up.astype(F32)).astype(BF16)


def gate_grads(d_hidden, gate, up):
    gate = gate.astype(F32)
    up = up.astype(F32)
    sigma = jax.nn.sigmoid(gate)
    d_gate = (d_hidden * up * sigma * (1.0 + gate * (1.0 - sigma))).astype(BF16)
    d_up = (d_hidden * gate * sigma).astype(BF16)
    return d_gate, d_up


def limits(mebibytes):
    return pltpu.CompilerParams(vmem_limit_bytes=mebibytes * 2**20)


def columns_at(value, index, width):
    return lax.dynamic_slice_in_dim(value, index * width, width, 1)


def spread(first, second, core):
    def body(core_ref, first_ref, second_ref, out_ref):
        value = jnp.where(core_ref[0] == 0, first_ref[...], second_ref[...])
        for i in range(XS * ZH):
            out_ref[i] = value

    shape = (XS * ZH, *first.shape)
    values = [pltpu.with_memory_space_constraint(v, pltpu.HBM) for v in (first, second)]
    return pl.pallas_call(
        body,
        grid=(1,),
        in_specs=[whole(pltpu.SMEM)] + [pl.BlockSpec(first.shape, lambda i: (0, 0))] * 2,
        out_specs=pl.BlockSpec(shape, lambda i: (0, 0, 0)),
        out_shape=jax.ShapeDtypeStruct(shape, BF16),
        compiler_params=limits(2),
        name="spread",
    )(core, *values)


def assemble(blocks, x):
    rows, width = blocks[0].shape

    def body(x_ref, *refs):
        out_ref = refs[-1]
        for k in range(XS):
            start = pl.multiple_of(((x_ref[0] + k) % XS) * width, LANES)
            out_ref[:, pl.ds(start, width)] = refs[k][...]

    return pl.pallas_call(
        body,
        in_specs=[whole(pltpu.SMEM)] + [whole()] * XS,
        out_specs=whole(),
        out_shape=jax.ShapeDtypeStruct((rows, width * XS), BF16),
        compiler_params=limits(2),
        name="assemble",
    )(x, *blocks)


def merge(own, other, core):
    rows, width = own.shape

    def body(core_ref, own_ref, other_ref, out_ref):
        start = pl.multiple_of(core_ref[0] * rows, 16)
        out_ref[pl.ds(start, rows), :] = own_ref[...]
        start = pl.multiple_of((1 - core_ref[0]) * rows, 16)
        out_ref[pl.ds(start, rows), :] = other_ref[...]

    return pl.pallas_call(
        body,
        in_specs=[whole(pltpu.SMEM), whole(), whole()],
        out_specs=whole(),
        out_shape=jax.ShapeDtypeStruct((rows * CORES, width), BF16),
        compiler_params=limits(2),
        name="merge",
    )(core, own, other)


def picked(by_core, core):
    rows, width = by_core[0][0][0].shape
    half = width // CORES
    count = max(len(picks) for picks in by_core)
    values = []
    for picks in by_core:
        for value, _ in picks:
            if not any(value is known for known in values):
                values.append(value)

    def body(core_ref, *refs):
        out_ref = refs[-1]
        for c, picks in enumerate(by_core):

            @pl.when(core_ref[0] == c)
            def _(picks=picks):
                for slot in range(count):
                    value, side = picks[min(slot, len(picks) - 1)]
                    at = [value is known for known in values].index(True)
                    out_ref[slot] = refs[at][:, side * half : (side + 1) * half]

    return pl.pallas_call(
        body,
        in_specs=[whole(pltpu.SMEM)] + [whole()] * len(values),
        out_specs=whole(),
        out_shape=jax.ShapeDtypeStruct((count, rows, half), BF16),
        compiler_params=limits(4),
        name="picked",
    )(core, *values)


def packed(choices, given, acts, core, shared=False):
    rows = choices[0][0].shape[0]
    half = choices[0][0].shape[1] // (1 if given is None else CORES)
    tiles = half // LANES
    group = 4
    turned = isinstance(acts, tuple)
    features = acts[0].shape[1] if turned else acts.shape[0]
    shard = features // PEERS
    count = len(choices)
    part = shard // CORES if shared else shard
    height = count * tiles * rows + part
    values = [choice[0] for choice in choices]
    specs = [pl.BlockSpec(value.shape, lambda p: (0, 0)) for value in values]
    if given is not None:
        values.append(given)
        specs.append(pl.BlockSpec(given.shape, lambda p: (0, 0, 0)))
    if turned:
        values.append(acts[0])
        specs.append(pl.BlockSpec(acts[0].shape, lambda p: (0, 0)))
    else:
        values.append(acts)
        specs.append(pl.BlockSpec((group * shard, rows), lambda p: (p, 0)))

    def body(core_ref, *refs):
        given_ref = None if given is None else refs[count]
        out_ref = refs[len(values)]
        index = pl.program_id(0)
        for c, (_, source, slot) in enumerate(choices):
            for t in range(tiles):
                base = (c * tiles + t) * rows
                first = (source or 0) * half + t * LANES
                tile = refs[c][:, first : first + LANES]
                if source is not None:
                    other = given_ref[slot, :, t * LANES : (t + 1) * LANES]
                    tile = jnp.where(core_ref[0] == source, tile, other)
                for g in range(group):
                    out_ref[g, base : base + rows, :] = tile
        if turned:
            acts_ref = refs[len(values) - 1]
            turned_ref = refs[-1]

            @pl.when(index == 0)
            def _():
                for t in range(features // LANES):
                    at = slice(t * LANES, (t + 1) * LANES)
                    turned_ref[at, :] = acts_ref[:, at].T

            for g in range(group):
                start = (index * group + g) * shard
                if shared:
                    start = start + core_ref[0] * part
                start = pl.multiple_of(start, 32)
                out_ref[g, count * tiles * rows :, :] = turned_ref[pl.ds(start, part), :]
        else:
            acts_ref = refs[len(values) - 1]
            for g in range(group):
                at = slice(g * shard, (g + 1) * shard)
                out_ref[g, count * tiles * rows :, :] = acts_ref[at, :]

    return pl.pallas_call(
        body,
        grid=(PEERS // group,),
        in_specs=[whole(pltpu.SMEM)] + specs,
        out_specs=pl.BlockSpec((group, height, rows), lambda p: (p, 0, 0)),
        out_shape=jax.ShapeDtypeStruct((PEERS, height, rows), BF16),
        scratch_shapes=[pltpu.VMEM((features, rows), BF16)] if turned else [],
        compiler_params=limits(8),
        name="packed",
    )(core, *values)


def weight_grads(gate, up, d_hidden, acts, upstream, core):
    step = 2
    lanes = gate[0].shape[2]
    half = 3 * lanes
    shard = 192
    values = []
    specs = []

    def add(value, rows, index):
        values.append(value)
        specs.append(pl.BlockSpec((step, rows, lanes), lambda p: (p, index, 0)))

    for value, index in (gate, up, d_hidden):
        add(value, half, index)
    for operand in (acts, upstream):
        height = shard // CORES if len(operand) > 2 and operand[2] is None else shard
        add(operand[0], height, operand[1])
        if len(operand) > 2:
            add(operand[3], height, 0)

    def body(core_ref, *refs):
        ins = list(refs[: len(values)])
        out_ref, low_ref = refs[len(values) :]
        index = pl.program_id(0)

        @pl.when(index == 0)
        def _():
            out_ref[...] = jnp.zeros_like(out_ref)

        def wide(ref):
            rows = [
                jnp.concatenate(
                    [ref[r, t * lanes : (t + 1) * lanes, :] for t in range(3)], axis=1
                )
                for r in range(step)
            ]
            return jnp.concatenate(rows, axis=0)

        def features(operand):
            ref = ins.pop(0)
            blocks = [ref[r] for r in range(step)]
            if len(operand) > 2:
                other = ins.pop(0)
                first = core_ref[0] == (operand[2] or 0)
                heads = [jnp.where(first, blocks[r], other[r]) for r in range(step)]
                if operand[2] is None:
                    tails = [jnp.where(first, other[r], blocks[r]) for r in range(step)]
                    heads = [jnp.concatenate(pair, axis=0) for pair in zip(heads, tails)]
                blocks = heads
            return jnp.concatenate(blocks, axis=1)

        gate_v = wide(ins.pop(0)).astype(F32)
        up_v = wide(ins.pop(0)).astype(F32)
        grad = wide(ins.pop(0)).astype(F32)
        sigma = jax.nn.sigmoid(gate_v)
        silu = gate_v * sigma
        d_gate = (grad * up_v * sigma * (1.0 + gate_v * (1.0 - sigma))).astype(BF16)
        d_up = (grad * silu).astype(BF16)
        acts_t = features(acts)
        out_ref[0] += dot_nn(acts_t, d_gate)
        out_ref[1] += dot_nn(acts_t, d_up)
        out_ref[2] += dot_nn(features(upstream), (silu * up_v).astype(BF16))

        @pl.when(index == PEERS // step - 1)
        def _():
            low_ref[...] = out_ref[...].astype(BF16)

    shape = (3, shard, half)
    return pl.pallas_call(
        body,
        grid=(PEERS // step,),
        in_specs=[whole(pltpu.SMEM)] + specs,
        out_specs=[pl.BlockSpec(shape, lambda p: (0, 0, 0))] * 2,
        out_shape=[jax.ShapeDtypeStruct(shape, F32), jax.ShapeDtypeStruct(shape, BF16)],
        compiler_params=limits(16),
    )(core, *[pltpu.with_memory_space_constraint(v, pltpu.HBM) for v in values])


def early_out(own_0, own_1, got_1, core):
    count, shard, half = own_0.shape

    def body(core_ref, own_0_ref, own_1_ref, got_1_ref, *outs):
        @pl.when(core_ref[0] == 0)
        def _():
            for i in range(count):
                outs[i][:, :half] = own_0_ref[i]

        @pl.when(core_ref[0] != 0)
        def _():
            for i in range(count):
                outs[i][:, :half] = got_1_ref[i].astype(F32)
                outs[i][:, half:] = own_1_ref[i]

    shape = jax.ShapeDtypeStruct((shard, half * CORES), F32)
    return pl.pallas_call(
        body,
        in_specs=[whole(pltpu.SMEM)] + [whole()] * 3,
        out_specs=[whole()] * count,
        out_shape=[shape] * count,
        compiler_params=limits(8),
        name="early_out",
    )(core, own_0, own_1, got_1)


def late_out(outs, got_0, core):
    count, shard, half = got_0.shape

    def body(core_ref, got_ref, *refs):
        wide_ref, sems = refs[-2:]
        targets = refs[count : 2 * count]

        @pl.when(core_ref[0] == 0)
        def _():
            copies = []
            for i in range(count):
                wide_ref[i] = got_ref[i].astype(F32)
                copy = pltpu.make_async_copy(
                    wide_ref.at[i], targets[i].at[:, half:], sems.at[i]
                )
                copy.start()
                copies.append(copy)
            for copy in copies:
                copy.wait()

    return pl.pallas_call(
        body,
        in_specs=[whole(pltpu.SMEM), whole()] + [whole(pl.ANY)] * count,
        out_specs=[whole(pl.ANY)] * count,
        out_shape=[jax.ShapeDtypeStruct(o.shape, o.dtype) for o in outs],
        scratch_shapes=[
            pltpu.VMEM((count, shard, half), F32),
            pltpu.SemaphoreType.DMA((count,)),
        ],
        input_output_aliases={2 + i: i for i in range(count)},
        compiler_params=limits(8),
        name="late_out",
    )(core, got_0, *outs)


def crossing(partial, residual, source, core, x, core_id, x_id):
    width = partial.shape[1] // XS
    split = partial.shape[0] // CORES
    own = columns_at(partial, x, width)
    pieces = [
        shifted(columns_at(partial, (x + k) % XS, width), "x", k) for k in range(1, XS)
    ]

    total = own.astype(F32)
    for piece in pieces:
        total = total + piece.astype(F32)
    summed = lax.optimization_barrier(total.astype(BF16))
    halves = [summed[:split], summed[split:]]
    received = one_way(halves[1 - source], source)
    mine = jnp.where(core == source, halves[source], received)
    pieces = [shifted(mine, "zh", k) for k in range(1, ZH)]
    total = mine.astype(F32)
    for piece in pieces:
        total = total + piece.astype(F32)
    out = (residual.astype(F32) + total).astype(BF16)
    blocks = [out] + [shifted(out, "x", XS - k) for k in range(1, XS)]
    gathered = assemble(blocks, x_id)
    other = shifted(gathered, "segment", 1)
    return merge(gathered, other, core_id)


def local(tokens, w_gate, w_up, w_down, cotangent):
    return step(tokens, w_gate[0], w_up[0], w_down[0], cotangent)


def step(tokens, gate_w, up_w, down_w, cotangent):
    core = lax.axis_index("segment")
    x = lax.axis_index("x")
    core_id = core.astype(jnp.int32)[None]
    x_id = x.astype(jnp.int32)[None]
    rows = tokens.shape[0]
    features, hidden = gate_w.shape
    half = hidden // CORES

    lent = one_way(down_w[half:], 0)
    down_half = lax.optimization_barrier(jnp.where(core == 0, down_w[:half], lent))
    own = spread(tokens.T, cotangent.T, core_id)
    gathered = exchanged(own, TENSOR)
    entered = gathered.reshape(features, rows)

    gate_a = dot_tn(entered, gate_w).astype(BF16)
    up_a = dot_tn(entered, up_w).astype(BF16)
    hidden_a = hidden_of(gate_a, up_a)
    partial_a = dot_nn(hidden_a, down_w).astype(BF16)
    block = lax.dynamic_slice_in_dim(entered, x * (features // XS), features // XS, 0).T
    first, second = block[: rows // CORES], block[rows // CORES :]
    other = shifted(jnp.where(core == 0, second, first), "segment", 1)
    residual_1 = jnp.where(core == 0, first, other)
    residual_2 = jnp.where(core == 0, other, second)
    middle = crossing(partial_a, residual_1, 0, core, x, core_id, x_id)

    d_hidden_a = lax.dot_general(
        entered, down_w, (((0,), (1,)), ((), ())), preferred_element_type=F32
    ).astype(BF16)
    d_hidden_a = lax.optimization_barrier(d_hidden_a)
    outgoing = picked([[(gate_a, 1), (up_a, 1)], [(d_hidden_a, 0)]], core_id)
    given = shifted(outgoing, "segment", 1)
    load = packed(
        [(gate_a, 0, 0), (up_a, 0, 1), (d_hidden_a, 1, 0)], given, entered, core_id
    )
    wide = exchanged(load, DP)

    wide_a = wide
    entered_all = wide[:, 3 * half :]
    entered_other = shifted(entered_all, "segment", 1)

    gate_b = dot_nn(middle, gate_w).astype(BF16)
    up_b = dot_nn(middle, up_w).astype(BF16)
    d_gate_b, d_up_b = gate_grads(d_hidden_a.astype(F32), gate_b, up_b)
    partial_b = (dot_nt(d_gate_b, gate_w) + dot_nt(d_up_b, up_w)).astype(BF16)
    upstream = crossing(partial_b, residual_2, 1, core, x, core_id, x_id)

    picks = [(gate_b, 0), (up_b, 0)]
    outgoing = picked([picks, picks], core_id)
    given = one_way(outgoing, 1)
    load = packed([(gate_b, 1, 0), (up_b, 1, 1)], given, (middle,), core_id, True)
    load, wide_a = lax.optimization_barrier((load, wide_a))
    wide_b = exchanged(load, DP)

    d_hidden_b = dot_nt(upstream, down_half).astype(BF16)
    load = packed([(d_hidden_b, None, 0)], None, (upstream,), core_id)
    load, wide_b = lax.optimization_barrier((load, wide_b))
    wide_c = exchanged(load, DP)

    middle_other = shifted(wide_b[:, 2 * half :], "segment", 1)
    own_1, low_1 = weight_grads(
        (wide_b, 0),
        (wide_b, 1),
        (wide_a, 2),
        (wide_b, 8, None, middle_other),
        (wide_a, 6, 1, entered_other),
        core_id,
    )
    got_1 = one_way(low_1, 0)
    own_0, low_0 = weight_grads(
        (wide_a, 0),
        (wide_a, 1),
        (wide_c, 0),
        (wide_a, 6, 0, entered_other),
        (wide_c, 2),
        core_id,
    )
    got_0 = one_way(low_0, 1)
    outs = early_out(own_0, own_1, got_1, core_id)
    grad_gate, grad_up, grad_down = late_out(outs, got_0, core_id)
    return (grad_gate[None], grad_up[None], grad_down.T[None])


def solution(mesh):
    fine = Mesh(
        mesh.devices.reshape(CORES, XS, ZH, ZL, YS), ("segment", "x", "zh", "zl", "y")
    )
    in_specs = (
        P(DP, TENSOR),
        P("segment", None, TENSOR),
        P("segment", None, TENSOR),
        P("segment", TENSOR, None),
        P(DP, TENSOR),
    )
    out_specs = (
        P("segment", DP, TENSOR),
        P("segment", DP, TENSOR),
        P("segment", TENSOR, DP),
    )
    return jax.shard_map(
        local, mesh=fine, in_specs=in_specs, out_specs=out_specs, check_vma=False
    )
```

```python
import jax
import jax.numpy as jnp
from jax import lax
from jax.experimental import pallas as pl
from jax.experimental.pallas import tpu as pltpu
from jax.sharding import Mesh, PartitionSpec as P

CORES = 2
XS = 4
ZH = 4
ZL = 2
YS = 4
PEERS = ZL * YS
LANES = 128
TENSOR = ("x", "zh")
DP = ("zl", "y")
BF16 = jnp.bfloat16
F32 = jnp.float32


def shifted(value, axis, distance):
    size = lax.axis_size(axis)
    return lax.ppermute(value, axis, [(i, (i + distance) % size) for i in range(size)])


def fanned(value_of, axis, distance_of):
    out = []
    for k in range(1, lax.axis_size(axis)):
        out.append(shifted(value_of(k), axis, distance_of(k)))
    return out


def one_way(value, source):
    return lax.ppermute(value, "segment", [(source, 1 - source)])


def exchanged(value, axes):
    return lax.all_to_all(value, axes, 0, 0, tiled=True)


def dot_tn(left, right):
    return lax.dot_general(left, right, (((0,), (0,)), ((), ())), preferred_element_type=F32)


def dot_nt(left, right):
    return lax.dot_general(left, right, (((1,), (1,)), ((), ())), preferred_element_type=F32)


def dot_nn(left, right):
    return jnp.dot(left, right, preferred_element_type=F32)


def whole(memory_space=pltpu.VMEM):
    return pl.BlockSpec(memory_space=memory_space)


def hidden_of(gate, up):
    gate = gate.astype(F32)
    return (jax.nn.silu(gate) * up.astype(F32)).astype(BF16)


def gate_grads(d_hidden, gate, up):
    gate = gate.astype(F32)
    up = up.astype(F32)
    sigma = jax.nn.sigmoid(gate)
    d_gate = (d_hidden * up * sigma * (1.0 + gate * (1.0 - sigma))).astype(BF16)
    d_up = (d_hidden * gate * sigma).astype(BF16)
    return d_gate, d_up


def limits(mebibytes):
    return pltpu.CompilerParams(vmem_limit_bytes=mebibytes * 2**20)


def columns_at(value, index, width):
    return lax.dynamic_slice_in_dim(value, index * width, width, 1)


def spread(first, second, core):
    def body(core_ref, first_ref, second_ref, out_ref):
        value = jnp.where(core_ref[0] == 0, first_ref[...], second_ref[...])
        for i in range(XS * ZH):
            out_ref[i] = value

    shape = (XS * ZH, *first.shape)
    values = [pltpu.with_memory_space_constraint(v, pltpu.HBM) for v in (first, second)]
    return pl.pallas_call(
        body,
        grid=(1,),
        in_specs=[whole(pltpu.SMEM)] + [pl.BlockSpec(first.shape, lambda i: (0, 0))] * 2,
        out_specs=pl.BlockSpec(shape, lambda i: (0, 0, 0)),
        out_shape=jax.ShapeDtypeStruct(shape, BF16),
        compiler_params=limits(2),
        name="spread",
    )(core, *values)


def assemble(blocks, x):
    rows, width = blocks[0].shape

    def body(x_ref, *refs):
        out_ref = refs[-1]
        for k in range(XS):
            start = pl.multiple_of(((x_ref[0] + k) % XS) * width, LANES)
            out_ref[:, pl.ds(start, width)] = refs[k][...]

    return pl.pallas_call(
        body,
        in_specs=[whole(pltpu.SMEM)] + [whole()] * XS,
        out_specs=whole(),
        out_shape=jax.ShapeDtypeStruct((rows, width * XS), BF16),
        compiler_params=limits(2),
        name="assemble",
    )(x, *blocks)


def merge(own, other, core):
    rows, width = own.shape

    def body(core_ref, own_ref, other_ref, out_ref):
        start = pl.multiple_of(core_ref[0] * rows, 16)
        out_ref[pl.ds(start, rows), :] = own_ref[...]
        start = pl.multiple_of((1 - core_ref[0]) * rows, 16)
        out_ref[pl.ds(start, rows), :] = other_ref[...]

    return pl.pallas_call(
        body,
        in_specs=[whole(pltpu.SMEM), whole(), whole()],
        out_specs=whole(),
        out_shape=jax.ShapeDtypeStruct((rows * CORES, width), BF16),
        compiler_params=limits(2),
        name="merge",
    )(core, own, other)


def picked(by_core, core):
    rows, width = by_core[0][0][0].shape
    half = width // CORES
    count = max(len(picks) for picks in by_core)
    values = []
    for picks in by_core:
        for value, _ in picks:
            if not any(value is known for known in values):
                values.append(value)

    def body(core_ref, *refs):
        out_ref = refs[-1]
        for c, picks in enumerate(by_core):

            @pl.when(core_ref[0] == c)
            def _(picks=picks):
                for slot in range(count):
                    value, side = picks[min(slot, len(picks) - 1)]
                    at = [value is known for known in values].index(True)
                    out_ref[slot] = refs[at][:, side * half : (side + 1) * half]

    return pl.pallas_call(
        body,
        in_specs=[whole(pltpu.SMEM)] + [whole()] * len(values),
        out_specs=whole(),
        out_shape=jax.ShapeDtypeStruct((count, rows, half), BF16),
        compiler_params=limits(4),
        name="picked",
    )(core, *values)


def packed(choices, given, acts, core, shared=False):
    rows = choices[0][0].shape[0]
    half = choices[0][0].shape[1] // (1 if given is None else CORES)
    tiles = half // LANES
    group = 4
    turned = isinstance(acts, tuple)
    features = acts[0].shape[1] if turned else acts.shape[0]
    shard = features // PEERS
    count = len(choices)
    part = shard // CORES if shared else shard
    height = count * tiles * rows + part
    values = [choice[0] for choice in choices]
    specs = [pl.BlockSpec(value.shape, lambda p: (0, 0)) for value in values]
    if given is not None:
        values.append(given)
        specs.append(pl.BlockSpec(given.shape, lambda p: (0, 0, 0)))
    if turned:
        values.append(acts[0])
        specs.append(pl.BlockSpec(acts[0].shape, lambda p: (0, 0)))
    else:
        values.append(acts)
        specs.append(pl.BlockSpec((group * shard, rows), lambda p: (p, 0)))

    def body(core_ref, *refs):
        given_ref = None if given is None else refs[count]
        out_ref = refs[len(values)]
        index = pl.program_id(0)
        for c, (_, source, slot) in enumerate(choices):
            for t in range(tiles):
                base = (c * tiles + t) * rows
                first = (source or 0) * half + t * LANES
                tile = refs[c][:, first : first + LANES]
                if source is not None:
                    other = given_ref[slot, :, t * LANES : (t + 1) * LANES]
                    tile = jnp.where(core_ref[0] == source, tile, other)
                for g in range(group):
                    out_ref[g, base : base + rows, :] = tile
        if turned:
            acts_ref = refs[len(values) - 1]
            turned_ref = refs[-1]

            @pl.when(index == 0)
            def _():
                for t in range(features // LANES):
                    at = slice(t * LANES, (t + 1) * LANES)
                    turned_ref[at, :] = acts_ref[:, at].T

            for g in range(group):
                start = (index * group + g) * shard
                if shared:
                    start = start + core_ref[0] * part
                start = pl.multiple_of(start, 32)
                out_ref[g, count * tiles * rows :, :] = turned_ref[pl.ds(start, part), :]
        else:
            acts_ref = refs[len(values) - 1]
            for g in range(group):
                at = slice(g * shard, (g + 1) * shard)
                out_ref[g, count * tiles * rows :, :] = acts_ref[at, :]

    return pl.pallas_call(
        body,
        grid=(PEERS // group,),
        in_specs=[whole(pltpu.SMEM)] + specs,
        out_specs=pl.BlockSpec((group, height, rows), lambda p: (p, 0, 0)),
        out_shape=jax.ShapeDtypeStruct((PEERS, height, rows), BF16),
        scratch_shapes=[pltpu.VMEM((features, rows), BF16)] if turned else [],
        compiler_params=limits(8),
        name="packed",
    )(core, *values)


def weight_grads(gate, up, d_hidden, acts, upstream, core):
    step = 2
    lanes = gate[0].shape[2]
    half = 3 * lanes
    shard = 192
    values = []
    specs = []

    def add(value, rows, index):
        values.append(value)
        specs.append(pl.BlockSpec((step, rows, lanes), lambda p: (p, index, 0)))

    for value, index in (gate, up, d_hidden):
        add(value, half, index)
    for operand in (acts, upstream):
        height = shard // CORES if len(operand) > 2 and operand[2] is None else shard
        add(operand[0], height, operand[1])
        if len(operand) > 2:
            add(operand[3], height, 0)

    def body(core_ref, *refs):
        ins = list(refs[: len(values)])
        out_ref, low_ref = refs[len(values) :]
        index = pl.program_id(0)

        @pl.when(index == 0)
        def _():
            out_ref[...] = jnp.zeros_like(out_ref)

        def wide(ref):
            rows = [
                jnp.concatenate(
                    [ref[r, t * lanes : (t + 1) * lanes, :] for t in range(3)], axis=1
                )
                for r in range(step)
            ]
            return jnp.concatenate(rows, axis=0)

        def features(operand):
            ref = ins.pop(0)
            blocks = [ref[r] for r in range(step)]
            if len(operand) > 2:
                other = ins.pop(0)
                first = core_ref[0] == (operand[2] or 0)
                heads = [jnp.where(first, blocks[r], other[r]) for r in range(step)]
                if operand[2] is None:
                    tails = [jnp.where(first, other[r], blocks[r]) for r in range(step)]
                    heads = [jnp.concatenate(pair, axis=0) for pair in zip(heads, tails)]
                blocks = heads
            return jnp.concatenate(blocks, axis=1)

        gate_v = wide(ins.pop(0)).astype(F32)
        up_v = wide(ins.pop(0)).astype(F32)
        grad = wide(ins.pop(0)).astype(F32)
        sigma = jax.nn.sigmoid(gate_v)
        silu = gate_v * sigma
        d_gate = (grad * up_v * sigma * (1.0 + gate_v * (1.0 - sigma))).astype(BF16)
        d_up = (grad * silu).astype(BF16)
        acts_t = features(acts)
        out_ref[0] += dot_nn(acts_t, d_gate)
        out_ref[1] += dot_nn(acts_t, d_up)
        out_ref[2] += dot_nn(features(upstream), (silu * up_v).astype(BF16))

        @pl.when(index == PEERS // step - 1)
        def _():
            low_ref[...] = out_ref[...].astype(BF16)

    shape = (3, shard, half)
    return pl.pallas_call(
        body,
        grid=(PEERS // step,),
        in_specs=[whole(pltpu.SMEM)] + specs,
        out_specs=[pl.BlockSpec(shape, lambda p: (0, 0, 0))] * 2,
        out_shape=[jax.ShapeDtypeStruct(shape, F32), jax.ShapeDtypeStruct(shape, BF16)],
        compiler_params=limits(16),
    )(core, *[pltpu.with_memory_space_constraint(v, pltpu.HBM) for v in values])


def early_out(own_0, own_1, got_1, core):
    count, shard, half = own_0.shape

    def body(core_ref, own_0_ref, own_1_ref, got_1_ref, *outs):
        @pl.when(core_ref[0] == 0)
        def _():
            for i in range(count):
                outs[i][:, :half] = own_0_ref[i]

        @pl.when(core_ref[0] != 0)
        def _():
            for i in range(count):
                outs[i][:, :half] = got_1_ref[i].astype(F32)
                outs[i][:, half:] = own_1_ref[i]

    shape = jax.ShapeDtypeStruct((shard, half * CORES), F32)
    return pl.pallas_call(
        body,
        in_specs=[whole(pltpu.SMEM)] + [whole()] * 3,
        out_specs=[whole()] * count,
        out_shape=[shape] * count,
        compiler_params=limits(8),
        name="early_out",
    )(core, own_0, own_1, got_1)


def late_out(outs, got_0, core):
    count, shard, half = got_0.shape

    def body(core_ref, got_ref, *refs):
        wide_ref, sems = refs[-2:]
        targets = refs[count : 2 * count]

        @pl.when(core_ref[0] == 0)
        def _():
            copies = []
            for i in range(count):
                wide_ref[i] = got_ref[i].astype(F32)
                copy = pltpu.make_async_copy(
                    wide_ref.at[i], targets[i].at[:, half:], sems.at[i]
                )
                copy.start()
                copies.append(copy)
            for copy in copies:
                copy.wait()

    return pl.pallas_call(
        body,
        in_specs=[whole(pltpu.SMEM), whole()] + [whole(pl.ANY)] * count,
        out_specs=[whole(pl.ANY)] * count,
        out_shape=[jax.ShapeDtypeStruct(o.shape, o.dtype) for o in outs],
        scratch_shapes=[
            pltpu.VMEM((count, shard, half), F32),
            pltpu.SemaphoreType.DMA((count,)),
        ],
        input_output_aliases={2 + i: i for i in range(count)},
        compiler_params=limits(8),
        name="late_out",
    )(core, got_0, *outs)


def crossing(partial, residual, source, core, x, core_id, x_id):
    width = partial.shape[1] // XS
    split = partial.shape[0] // CORES
    own = columns_at(partial, x, width)
    pieces = fanned(
        lambda k: columns_at(partial, (x + k) % XS, width), "x", lambda k: k
    )

    total = own.astype(F32)
    for piece in pieces:
        total = total + piece.astype(F32)
    summed = lax.optimization_barrier(total.astype(BF16))
    halves = [summed[:split], summed[split:]]
    received = one_way(halves[1 - source], source)
    mine = jnp.where(core == source, halves[source], received)
    pieces = fanned(lambda k: mine, "zh", lambda k: k)
    total = mine.astype(F32)
    for piece in pieces:
        total = total + piece.astype(F32)
    out = (residual.astype(F32) + total).astype(BF16)
    blocks = [out] + fanned(lambda k: out, "x", lambda k: XS - k)
    gathered = assemble(blocks, x_id)
    other = shifted(gathered, "segment", 1)
    return merge(gathered, other, core_id)


def local(tokens, w_gate, w_up, w_down, cotangent):
    return step(tokens, w_gate[0], w_up[0], w_down[0], cotangent)


def step(tokens, gate_w, up_w, down_w, cotangent):
    core = lax.axis_index("segment")
    x = lax.axis_index("x")
    core_id = core.astype(jnp.int32)[None]
    x_id = x.astype(jnp.int32)[None]
    rows = tokens.shape[0]
    features, hidden = gate_w.shape
    half = hidden // CORES

    lent = one_way(down_w[half:], 0)
    down_half = lax.optimization_barrier(jnp.where(core == 0, down_w[:half], lent))
    own = spread(tokens.T, cotangent.T, core_id)
    gathered = exchanged(own, TENSOR)
    entered = gathered.reshape(features, rows)

    gate_a = dot_tn(entered, gate_w).astype(BF16)
    up_a = dot_tn(entered, up_w).astype(BF16)
    hidden_a = hidden_of(gate_a, up_a)
    partial_a = dot_nn(hidden_a, down_w).astype(BF16)
    block = lax.dynamic_slice_in_dim(entered, x * (features // XS), features // XS, 0).T
    first, second = block[: rows // CORES], block[rows // CORES :]
    other = shifted(jnp.where(core == 0, second, first), "segment", 1)
    residual_1 = jnp.where(core == 0, first, other)
    residual_2 = jnp.where(core == 0, other, second)
    middle = crossing(partial_a, residual_1, 0, core, x, core_id, x_id)

    d_hidden_a = lax.dot_general(
        entered, down_w, (((0,), (1,)), ((), ())), preferred_element_type=F32
    ).astype(BF16)
    d_hidden_a = lax.optimization_barrier(d_hidden_a)
    outgoing = picked([[(gate_a, 1), (up_a, 1)], [(d_hidden_a, 0)]], core_id)
    given = shifted(outgoing, "segment", 1)
    load = packed(
        [(gate_a, 0, 0), (up_a, 0, 1), (d_hidden_a, 1, 0)], given, entered, core_id
    )
    wide = exchanged(load, DP)

    wide_a = wide
    entered_all = wide[:, 3 * half :]
    entered_other = shifted(entered_all, "segment", 1)

    gate_b = dot_nn(middle, gate_w).astype(BF16)
    up_b = dot_nn(middle, up_w).astype(BF16)
    d_gate_b, d_up_b = gate_grads(d_hidden_a.astype(F32), gate_b, up_b)
    partial_b = (dot_nt(d_gate_b, gate_w) + dot_nt(d_up_b, up_w)).astype(BF16)
    upstream = crossing(partial_b, residual_2, 1, core, x, core_id, x_id)

    picks = [(gate_b, 0), (up_b, 0)]
    outgoing = picked([picks, picks], core_id)
    given = one_way(outgoing, 1)
    load = packed([(gate_b, 1, 0), (up_b, 1, 1)], given, (middle,), core_id, True)
    load, wide_a = lax.optimization_barrier((load, wide_a))
    wide_b = exchanged(load, DP)

    d_hidden_b = dot_nt(upstream, down_half).astype(BF16)
    load = packed([(d_hidden_b, None, 0)], None, (upstream,), core_id)
    load, wide_b = lax.optimization_barrier((load, wide_b))
    wide_c = exchanged(load, DP)

    middle_other = shifted(wide_b[:, 2 * half :], "segment", 1)
    own_1, low_1 = weight_grads(
        (wide_b, 0),
        (wide_b, 1),
        (wide_a, 2),
        (wide_b, 8, None, middle_other),
        (wide_a, 6, 1, entered_other),
        core_id,
    )
    got_1 = one_way(low_1, 0)
    own_0, low_0 = weight_grads(
        (wide_a, 0),
        (wide_a, 1),
        (wide_c, 0),
        (wide_a, 6, 0, entered_other),
        (wide_c, 2),
        core_id,
    )
    got_0 = one_way(low_0, 1)
    outs = early_out(own_0, own_1, got_1, core_id)
    grad_gate, grad_up, grad_down = late_out(outs, got_0, core_id)
    return (grad_gate[None], grad_up[None], grad_down.T[None])


def solution(mesh):
    fine = Mesh(
        mesh.devices.reshape(CORES, XS, ZH, ZL, YS), ("segment", "x", "zh", "zl", "y")
    )
    in_specs = (
        P(DP, TENSOR),
        P("segment", None, TENSOR),
        P("segment", None, TENSOR),
        P("segment", TENSOR, None),
        P(DP, TENSOR),
    )
    out_specs = (
        P("segment", DP, TENSOR),
        P("segment", DP, TENSOR),
        P("segment", TENSOR, DP),
    )
    return jax.shard_map(
        local, mesh=fine, in_specs=in_specs, out_specs=out_specs, check_vma=False
    )
```

```python
import jax
import jax.numpy as jnp
from jax import lax
from jax.experimental import pallas as pl
from jax.experimental.pallas import tpu as pltpu
from jax.sharding import Mesh, PartitionSpec as P


CORES = 2
XS = 4
ZH = 4
ZL = 2
YS = 4
PEERS = ZL * YS
LANES = 128
TENSOR = ("x", "zh")
DP = ("zl", "y")
BF16 = jnp.bfloat16
F32 = jnp.float32


def shifted(value, axis, distance):
    size = lax.axis_size(axis)
    return lax.ppermute(value, axis, [(i, (i + distance) % size) for i in range(size)])


def fanned(value_of, axis, distance_of):
    out = []
    for k in range(1, lax.axis_size(axis)):
        out.append(shifted(value_of(k), axis, distance_of(k)))
    return out


def one_way(value, source):
    return lax.ppermute(value, "segment", [(source, 1 - source)])


def exchanged(value, axes):
    return lax.all_to_all(value, axes, 0, 0, tiled=True)


def dot_tn(left, right):
    return lax.dot_general(left, right, (((0,), (0,)), ((), ())), preferred_element_type=F32)


def dot_nt(left, right):
    return lax.dot_general(left, right, (((1,), (1,)), ((), ())), preferred_element_type=F32)


def dot_nn(left, right):
    return jnp.dot(left, right, preferred_element_type=F32)


def whole(memory_space=pltpu.VMEM):
    return pl.BlockSpec(memory_space=memory_space)


def hidden_of(gate, up):
    gate = gate.astype(F32)
    return (jax.nn.silu(gate) * up.astype(F32)).astype(BF16)


def gate_grads(d_hidden, gate, up):
    gate = gate.astype(F32)
    up = up.astype(F32)
    sigma = jax.nn.sigmoid(gate)
    d_gate = (d_hidden * up * sigma * (1.0 + gate * (1.0 - sigma))).astype(BF16)
    d_up = (d_hidden * gate * sigma).astype(BF16)
    return d_gate, d_up


def limits(mebibytes):
    return pltpu.CompilerParams(vmem_limit_bytes=mebibytes * 2**20)


def columns_at(value, index, width):
    return lax.dynamic_slice_in_dim(value, index * width, width, 1)


def spread(first, second, core):
    def body(core_ref, first_ref, second_ref, out_ref):
        value = jnp.where(core_ref[0] == 0, first_ref[...], second_ref[...])
        for i in range(XS * ZH):
            out_ref[i] = value

    shape = (XS * ZH, *first.shape)
    values = [pltpu.with_memory_space_constraint(v, pltpu.HBM) for v in (first, second)]
    return pl.pallas_call(
        body,
        grid=(1,),
        in_specs=[whole(pltpu.SMEM)] + [pl.BlockSpec(first.shape, lambda i: (0, 0))] * 2,
        out_specs=pl.BlockSpec(shape, lambda i: (0, 0, 0)),
        out_shape=jax.ShapeDtypeStruct(shape, BF16),
        compiler_params=limits(2),
        name="spread",
    )(core, *values)


def assemble(blocks, x):
    rows, width = blocks[0].shape

    def body(x_ref, *refs):
        out_ref = refs[-1]
        for k in range(XS):
            start = pl.multiple_of(((x_ref[0] + k) % XS) * width, LANES)
            out_ref[:, pl.ds(start, width)] = refs[k][...]

    return pl.pallas_call(
        body,
        in_specs=[whole(pltpu.SMEM)] + [whole()] * XS,
        out_specs=whole(),
        out_shape=jax.ShapeDtypeStruct((rows, width * XS), BF16),
        compiler_params=limits(2),
        name="assemble",
    )(x, *blocks)


def merge(own, other, core):
    rows, width = own.shape

    def body(core_ref, own_ref, other_ref, out_ref):
        start = pl.multiple_of(core_ref[0] * rows, 16)
        out_ref[pl.ds(start, rows), :] = own_ref[...]
        start = pl.multiple_of((1 - core_ref[0]) * rows, 16)
        out_ref[pl.ds(start, rows), :] = other_ref[...]

    return pl.pallas_call(
        body,
        in_specs=[whole(pltpu.SMEM), whole(), whole()],
        out_specs=whole(),
        out_shape=jax.ShapeDtypeStruct((rows * CORES, width), BF16),
        compiler_params=limits(2),
        name="merge",
    )(core, own, other)


def picked(by_core, core):
    rows, width = by_core[0][0][0].shape
    half = width // CORES
    count = max(len(picks) for picks in by_core)
    values = []
    for picks in by_core:
        for value, _ in picks:
            if not any(value is known for known in values):
                values.append(value)

    def body(core_ref, *refs):
        out_ref = refs[-1]
        for c, picks in enumerate(by_core):

            @pl.when(core_ref[0] == c)
            def _(picks=picks):
                for slot in range(count):
                    value, side = picks[min(slot, len(picks) - 1)]
                    at = [value is known for known in values].index(True)
                    out_ref[slot] = refs[at][:, side * half : (side + 1) * half]

    return pl.pallas_call(
        body,
        in_specs=[whole(pltpu.SMEM)] + [whole()] * len(values),
        out_specs=whole(),
        out_shape=jax.ShapeDtypeStruct((count, rows, half), BF16),
        compiler_params=limits(4),
        name="picked",
    )(core, *values)


def packed(choices, given, acts, core, shared=False):
    rows = choices[0][0].shape[0]
    half = choices[0][0].shape[1] // (1 if given is None else CORES)
    tiles = half // LANES
    group = 4
    turned = isinstance(acts, tuple)
    features = acts[0].shape[1] if turned else acts.shape[0]
    shard = features // PEERS
    count = len(choices)
    part = shard // CORES if shared else shard
    height = count * tiles * rows + part
    values = [choice[0] for choice in choices]
    specs = [pl.BlockSpec(value.shape, lambda p: (0, 0)) for value in values]
    if given is not None:
        values.append(given)
        specs.append(pl.BlockSpec(given.shape, lambda p: (0, 0, 0)))
    if turned:
        values.append(acts[0])
        specs.append(pl.BlockSpec(acts[0].shape, lambda p: (0, 0)))
    else:
        values.append(acts)
        specs.append(pl.BlockSpec((group * shard, rows), lambda p: (p, 0)))

    def body(core_ref, *refs):
        given_ref = None if given is None else refs[count]
        out_ref = refs[len(values)]
        index = pl.program_id(0)
        for c, (_, source, slot) in enumerate(choices):
            for t in range(tiles):
                base = (c * tiles + t) * rows
                first = (source or 0) * half + t * LANES
                tile = refs[c][:, first : first + LANES]
                if source is not None:
                    other = given_ref[slot, :, t * LANES : (t + 1) * LANES]
                    tile = jnp.where(core_ref[0] == source, tile, other)
                for g in range(group):
                    out_ref[g, base : base + rows, :] = tile
        if turned:
            acts_ref = refs[len(values) - 1]
            turned_ref = refs[-1]

            @pl.when(index == 0)
            def _():
                for t in range(features // LANES):
                    at = slice(t * LANES, (t + 1) * LANES)
                    turned_ref[at, :] = acts_ref[:, at].T

            for g in range(group):
                start = (index * group + g) * shard
                if shared:
                    start = start + core_ref[0] * part
                start = pl.multiple_of(start, 32)
                out_ref[g, count * tiles * rows :, :] = turned_ref[pl.ds(start, part), :]
        else:
            acts_ref = refs[len(values) - 1]
            for g in range(group):
                at = slice(g * shard, (g + 1) * shard)
                out_ref[g, count * tiles * rows :, :] = acts_ref[at, :]

    return pl.pallas_call(
        body,
        grid=(PEERS // group,),
        in_specs=[whole(pltpu.SMEM)] + specs,
        out_specs=pl.BlockSpec((group, height, rows), lambda p: (p, 0, 0)),
        out_shape=jax.ShapeDtypeStruct((PEERS, height, rows), BF16),
        scratch_shapes=[pltpu.VMEM((features, rows), BF16)] if turned else [],
        compiler_params=limits(8),
        name="packed",
    )(core, *values)


def weight_grads(gate, up, d_hidden, acts, upstream, core):
    step = 2
    lanes = gate[0].shape[2]
    half = 3 * lanes
    shard = 192
    values = []
    specs = []

    def add(value, rows, index):
        values.append(value)
        specs.append(pl.BlockSpec((step, rows, lanes), lambda p: (p, index, 0)))

    for value, index in (gate, up, d_hidden):
        add(value, half, index)
    for operand in (acts, upstream):
        height = shard // CORES if len(operand) > 2 and operand[2] is None else shard
        add(operand[0], height, operand[1])
        if len(operand) > 2:
            add(operand[3], height, 0)

    def body(core_ref, *refs):
        ins = list(refs[: len(values)])
        out_ref, low_ref = refs[len(values) :]
        index = pl.program_id(0)

        @pl.when(index == 0)
        def _():
            out_ref[...] = jnp.zeros_like(out_ref)

        def wide(ref):
            rows = [
                jnp.concatenate(
                    [ref[r, t * lanes : (t + 1) * lanes, :] for t in range(3)], axis=1
                )
                for r in range(step)
            ]
            return jnp.concatenate(rows, axis=0)

        def features(operand):
            ref = ins.pop(0)
            blocks = [ref[r] for r in range(step)]
            if len(operand) > 2:
                other = ins.pop(0)
                first = core_ref[0] == (operand[2] or 0)
                heads = [jnp.where(first, blocks[r], other[r]) for r in range(step)]
                if operand[2] is None:
                    tails = [jnp.where(first, other[r], blocks[r]) for r in range(step)]
                    heads = [jnp.concatenate(pair, axis=0) for pair in zip(heads, tails)]
                blocks = heads
            return jnp.concatenate(blocks, axis=1)

        gate_v = wide(ins.pop(0)).astype(F32)
        up_v = wide(ins.pop(0)).astype(F32)
        grad = wide(ins.pop(0)).astype(F32)
        sigma = jax.nn.sigmoid(gate_v)
        silu = gate_v * sigma
        d_gate = (grad * up_v * sigma * (1.0 + gate_v * (1.0 - sigma))).astype(BF16)
        d_up = (grad * silu).astype(BF16)
        acts_t = features(acts)
        out_ref[0] += dot_nn(acts_t, d_gate)
        out_ref[1] += dot_nn(acts_t, d_up)
        out_ref[2] += dot_nn(features(upstream), (silu * up_v).astype(BF16))

        @pl.when(index == PEERS // step - 1)
        def _():
            low_ref[...] = out_ref[...].astype(BF16)

    shape = (3, shard, half)
    return pl.pallas_call(
        body,
        grid=(PEERS // step,),
        in_specs=[whole(pltpu.SMEM)] + specs,
        out_specs=[pl.BlockSpec(shape, lambda p: (0, 0, 0))] * 2,
        out_shape=[jax.ShapeDtypeStruct(shape, F32), jax.ShapeDtypeStruct(shape, BF16)],
        compiler_params=limits(16),
    )(core, *[pltpu.with_memory_space_constraint(v, pltpu.HBM) for v in values])


def packed_late(d_hidden, upstream, place):
    rows, half = d_hidden.shape
    features = upstream.shape[1]
    shard = features // PEERS
    tiles = half // LANES

    def body(place_ref, grad_ref, up_ref, *refs):
        outs = refs[:PEERS]
        turned_ref = refs[PEERS]
        for t in range(features // LANES):
            at = slice(t * LANES, (t + 1) * LANES)
            turned_ref[at, :] = up_ref[:, at].T
        for k in range(PEERS):
            for t in range(tiles):
                outs[k][t * rows : (t + 1) * rows, :] = grad_ref[:, t * LANES : (t + 1) * LANES]
            start = pl.multiple_of(((place_ref[1] + k) % PEERS) * shard, 64)
            outs[k][tiles * rows :, :] = turned_ref[pl.ds(start, shard), :]

    shape = jax.ShapeDtypeStruct((tiles * rows + shard, rows), BF16)
    return pl.pallas_call(
        body,
        in_specs=[whole(pltpu.SMEM), whole(), whole()],
        out_specs=[whole()] * PEERS,
        out_shape=[shape] * PEERS,
        scratch_shapes=[pltpu.VMEM((features, rows), BF16)],
        compiler_params=limits(4),
        name="packed_late",
    )(place, d_hidden, upstream)


def last_grads(wide, other, late, place):
    peers, height, lanes = wide.shape
    shard = other.shape[1]
    half = 3 * lanes
    step = 2

    def at_place(index, k):
        return lambda p, place_ref: ((place_ref[1] + 2 * peers - step * p - k) % peers, index, 0)

    specs = []
    values = []
    for k in range(step):
        for index in (0, 1):
            specs.append(pl.BlockSpec((1, half, lanes), at_place(index, k)))
            values.append(wide)
        specs.append(pl.BlockSpec((1, shard, lanes), at_place((height - shard) // shard, k)))
        values.append(wide)
        specs.append(pl.BlockSpec((1, shard, lanes), at_place(0, k)))
        values.append(other)
    early = len(values)

    def body(place_ref, *refs):
        out_ref, low_ref = refs[early + peers :]
        index = pl.program_id(0)

        @pl.when(index == 0)
        def _():
            out_ref[...] = jnp.zeros_like(out_ref)

        def flat(ref):
            return jnp.concatenate(
                [ref[t * lanes : (t + 1) * lanes, :] for t in range(3)], axis=1
            )

        def over(which):
            return jnp.concatenate([flat(refs[4 * k + which].at[0]) for k in range(step)], axis=0)

        gate = over(0).astype(F32)
        up = over(1).astype(F32)
        sigma = jax.nn.sigmoid(gate)
        silu = gate * sigma
        for_gate = up * sigma * (1.0 + gate * (1.0 - sigma))
        hidden = (silu * up).astype(BF16)
        mine = place_ref[0] == 0
        acts = jnp.concatenate(
            [jnp.where(mine, refs[4 * k + 2][0], refs[4 * k + 3][0]) for k in range(step)], axis=1
        )
        for turn in range(peers // step):

            @pl.when(index == turn)
            def _(turn=turn):
                pair = refs[early + step * turn : early + step * (turn + 1)]
                grad = jnp.concatenate([flat(ref) for ref in pair], axis=0).astype(F32)
                upstream = jnp.concatenate([ref[half:, :] for ref in pair], axis=1)
                out_ref[0] += dot_nn(acts, (grad * for_gate).astype(BF16))
                out_ref[1] += dot_nn(acts, (grad * silu).astype(BF16))
                out_ref[2] += dot_nn(upstream, hidden)

        @pl.when(index == peers // step - 1)
        def _():
            low_ref[...] = out_ref[...].astype(BF16)

    shape = (3, shard, half)
    return pl.pallas_call(
        body,
        grid_spec=pltpu.PrefetchScalarGridSpec(
            num_scalar_prefetch=1,
            grid=(peers // step,),
            in_specs=specs + [whole()] * peers,
            out_specs=[pl.BlockSpec(shape, lambda p, place_ref: (0, 0, 0))] * 2,
        ),
        out_shape=[jax.ShapeDtypeStruct(shape, F32), jax.ShapeDtypeStruct(shape, BF16)],
        compiler_params=limits(16),
        name="last_grads",
    )(place, *[pltpu.with_memory_space_constraint(v, pltpu.HBM) for v in values], *late)


def early_out(own_0, own_1, got_1, core):
    count, shard, half = own_0.shape

    def body(core_ref, own_0_ref, own_1_ref, got_1_ref, *outs):
        @pl.when(core_ref[0] == 0)
        def _():
            for i in range(count):
                outs[i][:, :half] = own_0_ref[i]

        @pl.when(core_ref[0] != 0)
        def _():
            for i in range(count):
                outs[i][:, :half] = got_1_ref[i].astype(F32)
                outs[i][:, half:] = own_1_ref[i]

    shape = jax.ShapeDtypeStruct((shard, half * CORES), F32)
    return pl.pallas_call(
        body,
        in_specs=[whole(pltpu.SMEM)] + [whole()] * 3,
        out_specs=[whole()] * count,
        out_shape=[shape] * count,
        compiler_params=limits(8),
        name="early_out",
    )(core, own_0, own_1, got_1)


def late_out(outs, got_0, core):
    count, shard, half = got_0.shape

    def body(core_ref, got_ref, *refs):
        wide_ref, sems = refs[-2:]
        targets = refs[count : 2 * count]

        @pl.when(core_ref[0] == 0)
        def _():
            copies = []
            for i in range(count):
                wide_ref[i] = got_ref[i].astype(F32)
                copy = pltpu.make_async_copy(
                    wide_ref.at[i], targets[i].at[:, half:], sems.at[i]
                )
                copy.start()
                copies.append(copy)
            for copy in copies:
                copy.wait()

    return pl.pallas_call(
        body,
        in_specs=[whole(pltpu.SMEM), whole()] + [whole(pl.ANY)] * count,
        out_specs=[whole(pl.ANY)] * count,
        out_shape=[jax.ShapeDtypeStruct(o.shape, o.dtype) for o in outs],
        scratch_shapes=[
            pltpu.VMEM((count, shard, half), F32),
            pltpu.SemaphoreType.DMA((count,)),
        ],
        input_output_aliases={2 + i: i for i in range(count)},
        compiler_params=limits(8),
        name="late_out",
    )(core, got_0, *outs)


def crossing(partial, residual, source, core, x, core_id, x_id):
    width = partial.shape[1] // XS
    split = partial.shape[0] // CORES
    own = columns_at(partial, x, width)
    pieces = fanned(
        lambda k: columns_at(partial, (x + k) % XS, width), "x", lambda k: k
    )

    total = own.astype(F32)
    for piece in pieces:
        total = total + piece.astype(F32)
    summed = lax.optimization_barrier(total.astype(BF16))
    halves = [summed[:split], summed[split:]]
    received = one_way(halves[1 - source], source)
    mine = jnp.where(core == source, halves[source], received)
    pieces = fanned(lambda k: mine, "zh", lambda k: k)
    total = mine.astype(F32)
    for piece in pieces:
        total = total + piece.astype(F32)
    out = (residual.astype(F32) + total).astype(BF16)
    blocks = [out] + fanned(lambda k: out, "x", lambda k: XS - k)
    gathered = assemble(blocks, x_id)
    other = shifted(gathered, "segment", 1)
    return merge(gathered, other, core_id)


def local(tokens, w_gate, w_up, w_down, cotangent):
    return step(tokens, w_gate[0], w_up[0], w_down[0], cotangent)


def step(tokens, gate_w, up_w, down_w, cotangent):
    core = lax.axis_index("segment")
    x = lax.axis_index("x")
    core_id = core.astype(jnp.int32)[None]
    x_id = x.astype(jnp.int32)[None]
    place = jnp.stack([core, lax.axis_index(DP)]).astype(jnp.int32)
    rows = tokens.shape[0]
    features, hidden = gate_w.shape
    half = hidden // CORES

    lent = one_way(down_w[half:], 0)
    down_half = lax.optimization_barrier(jnp.where(core == 0, down_w[:half], lent))
    own = spread(tokens.T, cotangent.T, core_id)
    gathered = exchanged(own, TENSOR)
    entered = gathered.reshape(features, rows)

    gate_a = dot_tn(entered, gate_w).astype(BF16)
    up_a = dot_tn(entered, up_w).astype(BF16)
    hidden_a = hidden_of(gate_a, up_a)
    partial_a = dot_nn(hidden_a, down_w).astype(BF16)
    block = lax.dynamic_slice_in_dim(entered, x * (features // XS), features // XS, 0).T
    first, second = block[: rows // CORES], block[rows // CORES :]
    other = shifted(jnp.where(core == 0, second, first), "segment", 1)
    residual_1 = jnp.where(core == 0, first, other)
    residual_2 = jnp.where(core == 0, other, second)
    middle = crossing(partial_a, residual_1, 0, core, x, core_id, x_id)

    d_hidden_a = lax.dot_general(
        entered, down_w, (((0,), (1,)), ((), ())), preferred_element_type=F32
    ).astype(BF16)
    d_hidden_a = lax.optimization_barrier(d_hidden_a)
    outgoing = picked([[(gate_a, 1), (up_a, 1)], [(d_hidden_a, 0)]], core_id)
    given = shifted(outgoing, "segment", 1)
    load = packed(
        [(gate_a, 0, 0), (up_a, 0, 1), (d_hidden_a, 1, 0)], given, entered, core_id
    )
    wide = exchanged(load, DP)

    wide_a = wide
    entered_all = wide[:, 3 * half :]
    entered_other = shifted(entered_all, "segment", 1)

    gate_b = dot_nn(middle, gate_w).astype(BF16)
    up_b = dot_nn(middle, up_w).astype(BF16)
    d_gate_b, d_up_b = gate_grads(d_hidden_a.astype(F32), gate_b, up_b)
    partial_b = (dot_nt(d_gate_b, gate_w) + dot_nt(d_up_b, up_w)).astype(BF16)
    upstream = crossing(partial_b, residual_2, 1, core, x, core_id, x_id)

    picks = [(gate_b, 0), (up_b, 0)]
    outgoing = picked([picks, picks], core_id)
    given = one_way(outgoing, 1)
    load = packed([(gate_b, 1, 0), (up_b, 1, 1)], given, (middle,), core_id, True)
    load, wide_a = lax.optimization_barrier((load, wide_a))
    wide_b = exchanged(load, DP)

    d_hidden_b = dot_nt(upstream, down_half).astype(BF16)
    late = list(packed_late(d_hidden_b, upstream, place))
    for k in range(1, PEERS):
        late[k] = shifted(late[k], DP, k)

    middle_other = shifted(wide_b[:, 2 * half :], "segment", 1)
    own_1, low_1 = weight_grads(
        (wide_b, 0),
        (wide_b, 1),
        (wide_a, 2),
        (wide_b, 8, None, middle_other),
        (wide_a, 6, 1, entered_other),
        core_id,
    )
    got_1 = one_way(low_1, 0)
    own_0, low_0 = last_grads(wide_a, entered_other, late, place)
    got_0 = one_way(low_0, 1)
    outs = early_out(own_0, own_1, got_1, core_id)
    grad_gate, grad_up, grad_down = late_out(outs, got_0, core_id)
    return (grad_gate[None], grad_up[None], grad_down.T[None])


def solution(mesh):
    fine = Mesh(
        mesh.devices.reshape(CORES, XS, ZH, ZL, YS), ("segment", "x", "zh", "zl", "y")
    )
    in_specs = (
        P(DP, TENSOR),
        P("segment", None, TENSOR),
        P("segment", None, TENSOR),
        P("segment", TENSOR, None),
        P(DP, TENSOR),
    )
    out_specs = (
        P("segment", DP, TENSOR),
        P("segment", DP, TENSOR),
        P("segment", TENSOR, DP),
    )
    return jax.shard_map(
        local, mesh=fine, in_specs=in_specs, out_specs=out_specs, check_vma=False
    )
```

```python
import jax
import jax.numpy as jnp
from jax import lax
from jax.experimental import pallas as pl
from jax.experimental.pallas import tpu as pltpu
from jax.sharding import Mesh, PartitionSpec as P


CORES = 2
XS = 4
ZH = 4
ZL = 2
YS = 4
PEERS = ZL * YS
LANES = 128
TENSOR = ("x", "zh")
DP = ("zl", "y")
BF16 = jnp.bfloat16
F32 = jnp.float32


def shifted(value, axis, distance):
    size = lax.axis_size(axis)
    return lax.ppermute(value, axis, [(i, (i + distance) % size) for i in range(size)])


def fanned(value_of, axis, distance_of):
    out = []
    for k in range(1, lax.axis_size(axis)):
        out.append(shifted(value_of(k), axis, distance_of(k)))
    return out


def one_way(value, source):
    return lax.ppermute(value, "segment", [(source, 1 - source)])


def exchanged(value, axes):
    return lax.all_to_all(value, axes, 0, 0, tiled=True)


def dot_tn(left, right):
    return lax.dot_general(left, right, (((0,), (0,)), ((), ())), preferred_element_type=F32)


def dot_nt(left, right):
    return lax.dot_general(left, right, (((1,), (1,)), ((), ())), preferred_element_type=F32)


def dot_nn(left, right):
    return jnp.dot(left, right, preferred_element_type=F32)


def whole(memory_space=pltpu.VMEM):
    return pl.BlockSpec(memory_space=memory_space)


def hidden_of(gate, up):
    gate = gate.astype(F32)
    return (jax.nn.silu(gate) * up.astype(F32)).astype(BF16)


def gate_grads(d_hidden, gate, up):
    gate = gate.astype(F32)
    up = up.astype(F32)
    sigma = jax.nn.sigmoid(gate)
    d_gate = (d_hidden * up * sigma * (1.0 + gate * (1.0 - sigma))).astype(BF16)
    d_up = (d_hidden * gate * sigma).astype(BF16)
    return d_gate, d_up


def limits(mebibytes):
    return pltpu.CompilerParams(vmem_limit_bytes=mebibytes * 2**20)


def columns_at(value, index, width):
    return lax.dynamic_slice_in_dim(value, index * width, width, 1)


def spread(first, second, core):
    def body(core_ref, first_ref, second_ref, out_ref):
        value = jnp.where(core_ref[0] == 0, first_ref[...], second_ref[...])
        for i in range(XS * ZH):
            out_ref[i] = value

    shape = (XS * ZH, *first.shape)
    values = [pltpu.with_memory_space_constraint(v, pltpu.HBM) for v in (first, second)]
    return pl.pallas_call(
        body,
        grid=(1,),
        in_specs=[whole(pltpu.SMEM)] + [pl.BlockSpec(first.shape, lambda i: (0, 0))] * 2,
        out_specs=pl.BlockSpec(shape, lambda i: (0, 0, 0)),
        out_shape=jax.ShapeDtypeStruct(shape, BF16),
        compiler_params=limits(2),
        name="spread",
    )(core, *values)


def assemble(blocks, x):
    rows, width = blocks[0].shape

    def body(x_ref, *refs):
        out_ref = refs[-1]
        for k in range(XS):
            start = pl.multiple_of(((x_ref[0] + k) % XS) * width, LANES)
            out_ref[:, pl.ds(start, width)] = refs[k][...]

    return pl.pallas_call(
        body,
        in_specs=[whole(pltpu.SMEM)] + [whole()] * XS,
        out_specs=whole(),
        out_shape=jax.ShapeDtypeStruct((rows, width * XS), BF16),
        compiler_params=limits(2),
        name="assemble",
    )(x, *blocks)


def merge(own, other, core):
    rows, width = own.shape

    def body(core_ref, own_ref, other_ref, out_ref):
        start = pl.multiple_of(core_ref[0] * rows, 16)
        out_ref[pl.ds(start, rows), :] = own_ref[...]
        start = pl.multiple_of((1 - core_ref[0]) * rows, 16)
        out_ref[pl.ds(start, rows), :] = other_ref[...]

    return pl.pallas_call(
        body,
        in_specs=[whole(pltpu.SMEM), whole(), whole()],
        out_specs=whole(),
        out_shape=jax.ShapeDtypeStruct((rows * CORES, width), BF16),
        compiler_params=limits(2),
        name="merge",
    )(core, own, other)


def picked(by_core, core):
    rows, width = by_core[0][0][0].shape
    half = width // CORES
    count = max(len(picks) for picks in by_core)
    values = []
    for picks in by_core:
        for value, _ in picks:
            if not any(value is known for known in values):
                values.append(value)

    def body(core_ref, *refs):
        out_ref = refs[-1]
        for c, picks in enumerate(by_core):

            @pl.when(core_ref[0] == c)
            def _(picks=picks):
                for slot in range(count):
                    value, side = picks[min(slot, len(picks) - 1)]
                    at = [value is known for known in values].index(True)
                    out_ref[slot] = refs[at][:, side * half : (side + 1) * half]

    return pl.pallas_call(
        body,
        in_specs=[whole(pltpu.SMEM)] + [whole()] * len(values),
        out_specs=whole(),
        out_shape=jax.ShapeDtypeStruct((count, rows, half), BF16),
        compiler_params=limits(4),
        name="picked",
    )(core, *values)


def packed(choices, given, acts, core, shared=False):
    rows = choices[0][0].shape[0]
    half = choices[0][0].shape[1] // (1 if given is None else CORES)
    tiles = half // LANES
    group = 4
    turned = isinstance(acts, tuple)
    features = acts[0].shape[1] if turned else acts.shape[0]
    shard = features // PEERS
    count = len(choices)
    part = shard // CORES if shared else shard
    height = count * tiles * rows + part
    values = [choice[0] for choice in choices]
    specs = [pl.BlockSpec(value.shape, lambda p: (0, 0)) for value in values]
    if given is not None:
        values.append(given)
        specs.append(pl.BlockSpec(given.shape, lambda p: (0, 0, 0)))
    if turned:
        values.append(acts[0])
        specs.append(pl.BlockSpec(acts[0].shape, lambda p: (0, 0)))
    else:
        values.append(acts)
        specs.append(pl.BlockSpec((group * shard, rows), lambda p: (p, 0)))

    def body(core_ref, *refs):
        given_ref = None if given is None else refs[count]
        out_ref = refs[len(values)]
        index = pl.program_id(0)
        for c, (_, source, slot) in enumerate(choices):
            for t in range(tiles):
                base = (c * tiles + t) * rows
                first = (source or 0) * half + t * LANES
                tile = refs[c][:, first : first + LANES]
                if source is not None:
                    other = given_ref[slot, :, t * LANES : (t + 1) * LANES]
                    tile = jnp.where(core_ref[0] == source, tile, other)
                for g in range(group):
                    out_ref[g, base : base + rows, :] = tile
        if turned:
            acts_ref = refs[len(values) - 1]
            turned_ref = refs[-1]

            @pl.when(index == 0)
            def _():
                for t in range(features // LANES):
                    at = slice(t * LANES, (t + 1) * LANES)
                    turned_ref[at, :] = acts_ref[:, at].T

            for g in range(group):
                start = (index * group + g) * shard
                if shared:
                    start = start + core_ref[0] * part
                start = pl.multiple_of(start, 32)
                out_ref[g, count * tiles * rows :, :] = turned_ref[pl.ds(start, part), :]
        else:
            acts_ref = refs[len(values) - 1]
            for g in range(group):
                at = slice(g * shard, (g + 1) * shard)
                out_ref[g, count * tiles * rows :, :] = acts_ref[at, :]

    return pl.pallas_call(
        body,
        grid=(PEERS // group,),
        in_specs=[whole(pltpu.SMEM)] + specs,
        out_specs=pl.BlockSpec((group, height, rows), lambda p: (p, 0, 0)),
        out_shape=jax.ShapeDtypeStruct((PEERS, height, rows), BF16),
        scratch_shapes=[pltpu.VMEM((features, rows), BF16)] if turned else [],
        compiler_params=limits(8),
        name="packed",
    )(core, *values)


def tiled(ref, k, base, lanes):
    return jnp.concatenate(
        [ref[k, base + t * lanes : base + (t + 1) * lanes, :] for t in range(3)], axis=1
    )


def add_grads(out_ref, low_ref, turn, turns, gate, up, grad, acts, upstream):
    gate = gate.astype(F32)
    up = up.astype(F32)
    grad = grad.astype(F32)
    sigma = jax.nn.sigmoid(gate)
    silu = gate * sigma
    d_gate = (grad * up * sigma * (1.0 + gate * (1.0 - sigma))).astype(BF16)
    parts = [
        dot_nn(acts, d_gate),
        dot_nn(acts, (grad * silu).astype(BF16)),
        dot_nn(upstream, (silu * up).astype(BF16)),
    ]
    for i, part in enumerate(parts):
        total = part if turn == 0 else out_ref[i] + part
        out_ref[i] = total
        if turn == turns - 1:
            low_ref[i] = total.astype(BF16)


def first_grads(stored, entry, entry_other, acts_other, core):
    peers, height, lanes = stored.shape
    half = 3 * lanes
    shard = entry_other.shape[1]
    tail = half + shard
    step = 2

    def body(core_ref, stored_ref, entry_ref, entry_other_ref, acts_other_ref, *refs):
        out_ref, low_ref, own_ref, late_ref, cot_ref, acts_ref, sems, whole_sems = refs
        wholes = [
            pltpu.make_async_copy(entry_other_ref, cot_ref, whole_sems.at[0]),
            pltpu.make_async_copy(acts_other_ref, acts_ref, whole_sems.at[1]),
        ]
        copies = []
        for k in range(peers):
            copies.append(
                [
                    pltpu.make_async_copy(stored_ref.at[k], own_ref.at[k], sems.at[k, 0]),
                    pltpu.make_async_copy(
                        entry_ref.at[k, pl.ds(2 * half, tail)], late_ref.at[k], sems.at[k, 1]
                    ),
                ]
            )
            for copy in copies[k]:
                copy.start()
            if k == 0:
                for copy in wholes:
                    copy.start()
        for copy in wholes:
            copy.wait()
        first = core_ref[0] == 0
        for turn in range(peers // step):
            ks = range(step * turn, step * (turn + 1))
            for k in ks:
                for copy in copies[k]:
                    copy.wait()

            def over(ref, base):
                return jnp.concatenate([tiled(ref, k, base, lanes) for k in ks], axis=0)

            acts = []
            upstream = []
            for k in ks:
                mine = own_ref[k, 2 * half :, :]
                other = acts_ref[k]
                acts.append(
                    jnp.concatenate(
                        [jnp.where(first, mine, other), jnp.where(first, other, mine)], axis=0
                    )
                )
                upstream.append(jnp.where(first, cot_ref[k], late_ref[k, half:, :]))
            add_grads(
                out_ref,
                low_ref,
                turn,
                peers // step,
                over(own_ref, 0),
                over(own_ref, half),
                over(late_ref, 0),
                jnp.concatenate(acts, axis=1),
                jnp.concatenate(upstream, axis=1),
            )

    shape = (3, shard, half)
    values = [pltpu.with_memory_space_constraint(v, pltpu.HBM) for v in (stored, entry, entry_other)]
    return pl.pallas_call(
        body,
        in_specs=[whole(pltpu.SMEM)] + [whole(pl.ANY)] * 4,
        out_specs=[whole()] * 2,
        out_shape=[jax.ShapeDtypeStruct(shape, F32), jax.ShapeDtypeStruct(shape, BF16)],
        scratch_shapes=[
            pltpu.VMEM((peers, height, lanes), BF16),
            pltpu.VMEM((peers, tail, lanes), BF16),
            pltpu.VMEM(entry_other.shape, BF16),
            pltpu.VMEM(acts_other.shape, BF16),
            pltpu.SemaphoreType.DMA((peers, 2)),
            pltpu.SemaphoreType.DMA((2,)),
        ],
        compiler_params=limits(16),
        name="first_grads",
    )(core, *values, acts_other)


def packed_late(d_hidden, upstream, place):
    rows, half = d_hidden.shape
    features = upstream.shape[1]
    shard = features // PEERS
    tiles = half // LANES

    def body(place_ref, grad_ref, up_ref, *refs):
        outs = refs[:PEERS]
        turned_ref = refs[PEERS]
        for t in range(features // LANES):
            at = slice(t * LANES, (t + 1) * LANES)
            turned_ref[at, :] = up_ref[:, at].T
        for k in range(PEERS):
            for t in range(tiles):
                outs[k][t * rows : (t + 1) * rows, :] = grad_ref[:, t * LANES : (t + 1) * LANES]
            start = pl.multiple_of(((place_ref[1] + k) % PEERS) * shard, 64)
            outs[k][tiles * rows :, :] = turned_ref[pl.ds(start, shard), :]

    shape = jax.ShapeDtypeStruct((tiles * rows + shard, rows), BF16)
    return pl.pallas_call(
        body,
        in_specs=[whole(pltpu.SMEM), whole(), whole()],
        out_specs=[whole()] * PEERS,
        out_shape=[shape] * PEERS,
        scratch_shapes=[pltpu.VMEM((features, rows), BF16)],
        compiler_params=limits(4),
        name="packed_late",
    )(place, d_hidden, upstream)


def last_grads(wide, other, late, place):
    peers, height, lanes = wide.shape
    shard = other.shape[1]
    half = 3 * lanes
    step = 2

    def body(place_ref, wide_ref, other_ref, *refs):
        late_refs = refs[:peers]
        out_ref, low_ref, stored_ref, acts_ref, swapped_ref, sems = refs[peers:]
        copies = []
        for k in range(peers):
            replica = (place_ref[1] + peers - k) % peers
            moves = [
                (wide_ref.at[replica, pl.ds(0, 2 * half)], stored_ref),
                (wide_ref.at[replica, pl.ds(height - shard, shard)], acts_ref),
                (other_ref.at[replica], swapped_ref),
            ]
            copies.append(
                [
                    pltpu.make_async_copy(source, target.at[k], sems.at[k, i])
                    for i, (source, target) in enumerate(moves)
                ]
            )
            for copy in copies[k]:
                copy.start()

        mine = place_ref[0] == 0
        for turn in range(peers // step):
            ks = range(step * turn, step * (turn + 1))
            for k in ks:
                for copy in copies[k]:
                    copy.wait()

            def over(ref, base):
                return jnp.concatenate([tiled(ref, k, base, lanes) for k in ks], axis=0)

            grad = jnp.concatenate(
                [
                    jnp.concatenate(
                        [late_refs[k][t * lanes : (t + 1) * lanes, :] for t in range(3)], axis=1
                    )
                    for k in ks
                ],
                axis=0,
            )
            add_grads(
                out_ref,
                low_ref,
                turn,
                peers // step,
                over(stored_ref, 0),
                over(stored_ref, half),
                grad,
                jnp.concatenate(
                    [jnp.where(mine, acts_ref[k], swapped_ref[k]) for k in ks], axis=1
                ),
                jnp.concatenate([late_refs[k][half:, :] for k in ks], axis=1),
            )

    shape = (3, shard, half)
    return pl.pallas_call(
        body,
        in_specs=[whole(pltpu.SMEM), whole(pl.ANY), whole(pl.ANY)] + [whole()] * peers,
        out_specs=[whole()] * 2,
        out_shape=[jax.ShapeDtypeStruct(shape, F32), jax.ShapeDtypeStruct(shape, BF16)],
        scratch_shapes=[
            pltpu.VMEM((peers, 2 * half, lanes), BF16),
            pltpu.VMEM((peers, shard, lanes), BF16),
            pltpu.VMEM((peers, shard, lanes), BF16),
            pltpu.SemaphoreType.DMA((peers, 3)),
        ],
        compiler_params=limits(16),
        name="last_grads",
    )(place, *[pltpu.with_memory_space_constraint(v, pltpu.HBM) for v in (wide, other)], *late)


def early_out(own_0, own_1, got_1, core):
    count, shard, half = own_0.shape

    def body(core_ref, own_0_ref, own_1_ref, got_1_ref, *outs):
        @pl.when(core_ref[0] == 0)
        def _():
            for i in range(count):
                outs[i][:, :half] = own_0_ref[i]

        @pl.when(core_ref[0] != 0)
        def _():
            for i in range(count):
                outs[i][:, :half] = got_1_ref[i].astype(F32)
                outs[i][:, half:] = own_1_ref[i]

    shape = jax.ShapeDtypeStruct((shard, half * CORES), F32)
    return pl.pallas_call(
        body,
        in_specs=[whole(pltpu.SMEM)] + [whole()] * 3,
        out_specs=[whole()] * count,
        out_shape=[shape] * count,
        compiler_params=limits(8),
        name="early_out",
    )(core, own_0, own_1, got_1)


def late_out(outs, got_0, core):
    count, shard, half = got_0.shape

    def body(core_ref, got_ref, *refs):
        wide_ref, sems = refs[-2:]
        targets = refs[count : 2 * count]

        @pl.when(core_ref[0] == 0)
        def _():
            copies = []
            for i in range(count):
                wide_ref[i] = got_ref[i].astype(F32)
                copy = pltpu.make_async_copy(
                    wide_ref.at[i], targets[i].at[:, half:], sems.at[i]
                )
                copy.start()
                copies.append(copy)
            for copy in copies:
                copy.wait()

    return pl.pallas_call(
        body,
        in_specs=[whole(pltpu.SMEM), whole()] + [whole(pl.ANY)] * count,
        out_specs=[whole(pl.ANY)] * count,
        out_shape=[jax.ShapeDtypeStruct(o.shape, o.dtype) for o in outs],
        scratch_shapes=[
            pltpu.VMEM((count, shard, half), F32),
            pltpu.SemaphoreType.DMA((count,)),
        ],
        input_output_aliases={2 + i: i for i in range(count)},
        compiler_params=limits(8),
        name="late_out",
    )(core, got_0, *outs)


def crossing(partial, residual, source, core, x, core_id, x_id):
    width = partial.shape[1] // XS
    split = partial.shape[0] // CORES
    own = columns_at(partial, x, width)
    pieces = fanned(lambda k: columns_at(partial, (x + k) % XS, width), "x", lambda k: k)

    total = own.astype(F32)
    for piece in pieces:
        total = total + piece.astype(F32)
    summed = lax.optimization_barrier(total.astype(BF16))
    halves = [summed[:split], summed[split:]]
    received = one_way(halves[1 - source], source)
    mine = jnp.where(core == source, halves[source], received)
    pieces = fanned(lambda k: mine, "zh", lambda k: k)
    total = mine.astype(F32)
    for piece in pieces:
        total = total + piece.astype(F32)
    out = (residual.astype(F32) + total).astype(BF16)
    blocks = [out] + fanned(lambda k: out, "x", lambda k: XS - k)
    gathered = assemble(blocks, x_id)
    other = shifted(gathered, "segment", 1)
    return merge(gathered, other, core_id)


def local(tokens, w_gate, w_up, w_down, cotangent):
    return step(tokens, w_gate[0], w_up[0], w_down[0], cotangent)


def step(tokens, gate_w, up_w, down_w, cotangent):
    core = lax.axis_index("segment")
    x = lax.axis_index("x")
    core_id = core.astype(jnp.int32)[None]
    x_id = x.astype(jnp.int32)[None]
    place = jnp.stack([core, lax.axis_index(DP)]).astype(jnp.int32)
    rows = tokens.shape[0]
    features, hidden = gate_w.shape
    half = hidden // CORES

    lent = one_way(down_w[half:], 0)
    down_half = lax.optimization_barrier(jnp.where(core == 0, down_w[:half], lent))
    own = spread(tokens.T, cotangent.T, core_id)
    gathered = exchanged(own, TENSOR)
    entered = gathered.reshape(features, rows)

    gate_a = dot_tn(entered, gate_w).astype(BF16)
    up_a = dot_tn(entered, up_w).astype(BF16)
    hidden_a = hidden_of(gate_a, up_a)
    partial_a = dot_nn(hidden_a, down_w).astype(BF16)
    block = lax.dynamic_slice_in_dim(entered, x * (features // XS), features // XS, 0).T
    first, second = block[: rows // CORES], block[rows // CORES :]
    other = shifted(jnp.where(core == 0, second, first), "segment", 1)
    residual_1 = jnp.where(core == 0, first, other)
    residual_2 = jnp.where(core == 0, other, second)
    middle = crossing(partial_a, residual_1, 0, core, x, core_id, x_id)

    d_hidden_a = lax.dot_general(
        entered, down_w, (((0,), (1,)), ((), ())), preferred_element_type=F32
    ).astype(BF16)
    d_hidden_a = lax.optimization_barrier(d_hidden_a)
    outgoing = picked([[(gate_a, 1), (up_a, 1)], [(d_hidden_a, 0)]], core_id)
    given = shifted(outgoing, "segment", 1)
    load = packed(
        [(gate_a, 0, 0), (up_a, 0, 1), (d_hidden_a, 1, 0)], given, entered, core_id
    )
    wide = exchanged(load, DP)

    wide_a = wide
    entered_other = shifted(wide[:, 3 * half :], "segment", 1)

    gate_b = dot_nn(middle, gate_w).astype(BF16)
    up_b = dot_nn(middle, up_w).astype(BF16)
    d_gate_b, d_up_b = gate_grads(d_hidden_a.astype(F32), gate_b, up_b)
    partial_b = (dot_nt(d_gate_b, gate_w) + dot_nt(d_up_b, up_w)).astype(BF16)
    upstream = crossing(partial_b, residual_2, 1, core, x, core_id, x_id)

    picks = [(gate_b, 0), (up_b, 0)]
    outgoing = picked([picks, picks], core_id)
    given = one_way(outgoing, 1)
    load = packed([(gate_b, 1, 0), (up_b, 1, 1)], given, (middle,), core_id, True)
    load, wide_a = lax.optimization_barrier((load, wide_a))
    wide_b = exchanged(load, DP)

    d_hidden_b = dot_nt(upstream, down_half).astype(BF16)
    late = list(packed_late(d_hidden_b, upstream, place))
    for k in range(1, PEERS):
        late[k] = shifted(late[k], DP, k)

    middle_other = shifted(wide_b[:, 2 * half :], "segment", 1)
    own_1, low_1 = first_grads(wide_b, wide_a, entered_other, middle_other, core_id)
    got_1 = one_way(low_1, 0)
    own_0, low_0 = last_grads(wide_a, entered_other, late, place)
    got_0 = one_way(low_0, 1)
    outs = early_out(own_0, own_1, got_1, core_id)
    grad_gate, grad_up, grad_down = late_out(outs, got_0, core_id)
    return (grad_gate[None], grad_up[None], grad_down.T[None])


def solution(mesh):
    fine = Mesh(
        mesh.devices.reshape(CORES, XS, ZH, ZL, YS), ("segment", "x", "zh", "zl", "y")
    )
    in_specs = (
        P(DP, TENSOR),
        P("segment", None, TENSOR),
        P("segment", None, TENSOR),
        P("segment", TENSOR, None),
        P(DP, TENSOR),
    )
    out_specs = (
        P("segment", DP, TENSOR),
        P("segment", DP, TENSOR),
        P("segment", TENSOR, DP),
    )
    return jax.shard_map(local, mesh=fine, in_specs=in_specs, out_specs=out_specs, check_vma=False)
```

```python
import jax
import jax.numpy as jnp
from jax import lax
from jax.experimental import pallas as pl
from jax.experimental.pallas import tpu as pltpu
from jax.sharding import Mesh, PartitionSpec as P


CORES = 2
XS = 4
ZH = 4
ZL = 2
YS = 4
PEERS = ZL * YS
LANES = 128
TENSOR = ("x", "zh")
DP = ("zl", "y")
BF16 = jnp.bfloat16
F32 = jnp.float32


def shifted(value, axis, distance):
    size = lax.axis_size(axis)
    return lax.ppermute(value, axis, [(i, (i + distance) % size) for i in range(size)])


def traded(value, axis, mask):
    return lax.ppermute(value, axis, [(i, i ^ mask) for i in range(lax.axis_size(axis))])


def fanned(value_of, axis):
    out = []
    for k in range(1, lax.axis_size(axis)):
        out.append(traded(value_of(k), axis, k))
    return out


def one_way(value, source):
    return lax.ppermute(value, "segment", [(source, 1 - source)])


def exchanged(value, axes):
    return lax.all_to_all(value, axes, 0, 0, tiled=True)


def dot_tn(left, right):
    return lax.dot_general(left, right, (((0,), (0,)), ((), ())), preferred_element_type=F32)


def dot_nt(left, right):
    return lax.dot_general(left, right, (((1,), (1,)), ((), ())), preferred_element_type=F32)


def dot_nn(left, right):
    return jnp.dot(left, right, preferred_element_type=F32)


def whole(memory_space=pltpu.VMEM):
    return pl.BlockSpec(memory_space=memory_space)


def hidden_of(gate, up):
    gate = gate.astype(F32)
    return (jax.nn.silu(gate) * up.astype(F32)).astype(BF16)


def gate_grads(d_hidden, gate, up):
    gate = gate.astype(F32)
    up = up.astype(F32)
    sigma = jax.nn.sigmoid(gate)
    d_gate = (d_hidden * up * sigma * (1.0 + gate * (1.0 - sigma))).astype(BF16)
    d_up = (d_hidden * gate * sigma).astype(BF16)
    return d_gate, d_up


def limits(mebibytes):
    return pltpu.CompilerParams(vmem_limit_bytes=mebibytes * 2**20)


def columns_at(value, index, width):
    return lax.dynamic_slice_in_dim(value, index * width, width, 1)


def spread(first, second, core):
    def body(core_ref, first_ref, second_ref, out_ref):
        value = jnp.where(core_ref[0] == 0, first_ref[...], second_ref[...])
        for i in range(XS * ZH):
            out_ref[i] = value

    shape = (XS * ZH, *first.shape)
    values = [pltpu.with_memory_space_constraint(v, pltpu.HBM) for v in (first, second)]
    return pl.pallas_call(
        body,
        grid=(1,),
        in_specs=[whole(pltpu.SMEM)] + [pl.BlockSpec(first.shape, lambda i: (0, 0))] * 2,
        out_specs=pl.BlockSpec(shape, lambda i: (0, 0, 0)),
        out_shape=jax.ShapeDtypeStruct(shape, BF16),
        compiler_params=limits(2),
        name="spread",
    )(core, *values)


def assemble(blocks, x):
    rows, width = blocks[0].shape

    def body(x_ref, *refs):
        out_ref = refs[-1]
        for k in range(XS):
            start = pl.multiple_of((x_ref[0] ^ k) * width, LANES)
            out_ref[:, pl.ds(start, width)] = refs[k][...]

    return pl.pallas_call(
        body,
        in_specs=[whole(pltpu.SMEM)] + [whole()] * XS,
        out_specs=whole(),
        out_shape=jax.ShapeDtypeStruct((rows, width * XS), BF16),
        compiler_params=limits(2),
        name="assemble",
    )(x, *blocks)


def merge(own, other, core):
    rows, width = own.shape

    def body(core_ref, own_ref, other_ref, out_ref):
        start = pl.multiple_of(core_ref[0] * rows, 16)
        out_ref[pl.ds(start, rows), :] = own_ref[...]
        start = pl.multiple_of((1 - core_ref[0]) * rows, 16)
        out_ref[pl.ds(start, rows), :] = other_ref[...]

    return pl.pallas_call(
        body,
        in_specs=[whole(pltpu.SMEM), whole(), whole()],
        out_specs=whole(),
        out_shape=jax.ShapeDtypeStruct((rows * CORES, width), BF16),
        compiler_params=limits(2),
        name="merge",
    )(core, own, other)


def picked(by_core, core):
    rows, width = by_core[0][0][0].shape
    half = width // CORES
    count = max(len(picks) for picks in by_core)
    values = []
    for picks in by_core:
        for value, _ in picks:
            if not any(value is known for known in values):
                values.append(value)

    def body(core_ref, *refs):
        out_ref = refs[-1]
        for c, picks in enumerate(by_core):

            @pl.when(core_ref[0] == c)
            def _(picks=picks):
                for slot in range(count):
                    value, side = picks[min(slot, len(picks) - 1)]
                    at = [value is known for known in values].index(True)
                    out_ref[slot] = refs[at][:, side * half : (side + 1) * half]

    return pl.pallas_call(
        body,
        in_specs=[whole(pltpu.SMEM)] + [whole()] * len(values),
        out_specs=whole(),
        out_shape=jax.ShapeDtypeStruct((count, rows, half), BF16),
        compiler_params=limits(4),
        name="picked",
    )(core, *values)


def packed(choices, given, acts, core, shared=False):
    rows = choices[0][0].shape[0]
    half = choices[0][0].shape[1] // (1 if given is None else CORES)
    tiles = half // LANES
    group = 4
    turned = isinstance(acts, tuple)
    features = acts[0].shape[1] if turned else acts.shape[0]
    shard = features // PEERS
    count = len(choices)
    part = shard // CORES if shared else shard
    height = count * tiles * rows + part
    values = [choice[0] for choice in choices]
    specs = [pl.BlockSpec(value.shape, lambda p: (0, 0)) for value in values]
    if given is not None:
        values.append(given)
        specs.append(pl.BlockSpec(given.shape, lambda p: (0, 0, 0)))
    if turned:
        values.append(acts[0])
        specs.append(pl.BlockSpec(acts[0].shape, lambda p: (0, 0)))
    else:
        values.append(acts)
        specs.append(pl.BlockSpec((group * shard, rows), lambda p: (p, 0)))

    def body(core_ref, *refs):
        given_ref = None if given is None else refs[count]
        out_ref = refs[len(values)]
        index = pl.program_id(0)
        for c, (_, source, slot) in enumerate(choices):
            for t in range(tiles):
                base = (c * tiles + t) * rows
                first = (source or 0) * half + t * LANES
                tile = refs[c][:, first : first + LANES]
                if source is not None:
                    other = given_ref[slot, :, t * LANES : (t + 1) * LANES]
                    tile = jnp.where(core_ref[0] == source, tile, other)
                for g in range(group):
                    out_ref[g, base : base + rows, :] = tile
        if turned:
            acts_ref = refs[len(values) - 1]
            turned_ref = refs[-1]

            @pl.when(index == 0)
            def _():
                for t in range(features // LANES):
                    at = slice(t * LANES, (t + 1) * LANES)
                    turned_ref[at, :] = acts_ref[:, at].T

            for g in range(group):
                start = (index * group + g) * shard
                if shared:
                    start = start + core_ref[0] * part
                start = pl.multiple_of(start, 32)
                out_ref[g, count * tiles * rows :, :] = turned_ref[pl.ds(start, part), :]
        else:
            acts_ref = refs[len(values) - 1]
            for g in range(group):
                at = slice(g * shard, (g + 1) * shard)
                out_ref[g, count * tiles * rows :, :] = acts_ref[at, :]

    return pl.pallas_call(
        body,
        grid=(PEERS // group,),
        in_specs=[whole(pltpu.SMEM)] + specs,
        out_specs=pl.BlockSpec((group, height, rows), lambda p: (p, 0, 0)),
        out_shape=jax.ShapeDtypeStruct((PEERS, height, rows), BF16),
        scratch_shapes=[pltpu.VMEM((features, rows), BF16)] if turned else [],
        compiler_params=limits(8),
        name="packed",
    )(core, *values)


def tiled(ref, k, base, lanes):
    return jnp.concatenate(
        [ref[k, base + t * lanes : base + (t + 1) * lanes, :] for t in range(3)], axis=1
    )


def add_grads(out_ref, low_ref, turn, turns, gate, up, grad, acts, upstream):
    gate = gate.astype(F32)
    up = up.astype(F32)
    grad = grad.astype(F32)
    sigma = jax.nn.sigmoid(gate)
    silu = gate * sigma
    d_gate = (grad * up * sigma * (1.0 + gate * (1.0 - sigma))).astype(BF16)
    parts = [
        dot_nn(acts, d_gate),
        dot_nn(acts, (grad * silu).astype(BF16)),
        dot_nn(upstream, (silu * up).astype(BF16)),
    ]
    for i, part in enumerate(parts):
        total = part if turn == 0 else out_ref[i] + part
        out_ref[i] = total
        if turn == turns - 1:
            low_ref[i] = total.astype(BF16)


def first_grads(stored, entry, entry_other, acts_other, core):
    peers, height, lanes = stored.shape
    half = 3 * lanes
    shard = entry_other.shape[1]
    tail = half + shard
    step = 2

    def body(core_ref, stored_ref, entry_ref, entry_other_ref, acts_other_ref, *refs):
        out_ref, low_ref, own_ref, late_ref, cot_ref, acts_ref, sems, whole_sems = refs
        wholes = [
            pltpu.make_async_copy(entry_other_ref, cot_ref, whole_sems.at[0]),
            pltpu.make_async_copy(acts_other_ref, acts_ref, whole_sems.at[1]),
        ]
        copies = []
        for k in range(peers):
            copies.append(
                [
                    pltpu.make_async_copy(stored_ref.at[k], own_ref.at[k], sems.at[k, 0]),
                    pltpu.make_async_copy(
                        entry_ref.at[k, pl.ds(2 * half, tail)], late_ref.at[k], sems.at[k, 1]
                    ),
                ]
            )
            for copy in copies[k]:
                copy.start()
            if k == 0:
                for copy in wholes:
                    copy.start()
        for copy in wholes:
            copy.wait()
        first = core_ref[0] == 0
        for turn in range(peers // step):
            ks = range(step * turn, step * (turn + 1))
            for k in ks:
                for copy in copies[k]:
                    copy.wait()

            def over(ref, base):
                return jnp.concatenate([tiled(ref, k, base, lanes) for k in ks], axis=0)

            acts = []
            upstream = []
            for k in ks:
                mine = own_ref[k, 2 * half :, :]
                other = acts_ref[k]
                acts.append(
                    jnp.concatenate(
                        [jnp.where(first, mine, other), jnp.where(first, other, mine)], axis=0
                    )
                )
                upstream.append(jnp.where(first, cot_ref[k], late_ref[k, half:, :]))
            add_grads(
                out_ref,
                low_ref,
                turn,
                peers // step,
                over(own_ref, 0),
                over(own_ref, half),
                over(late_ref, 0),
                jnp.concatenate(acts, axis=1),
                jnp.concatenate(upstream, axis=1),
            )

    shape = (3, shard, half)
    values = [pltpu.with_memory_space_constraint(v, pltpu.HBM) for v in (stored, entry, entry_other)]
    return pl.pallas_call(
        body,
        in_specs=[whole(pltpu.SMEM)] + [whole(pl.ANY)] * 4,
        out_specs=[whole()] * 2,
        out_shape=[jax.ShapeDtypeStruct(shape, F32), jax.ShapeDtypeStruct(shape, BF16)],
        scratch_shapes=[
            pltpu.VMEM((peers, height, lanes), BF16),
            pltpu.VMEM((peers, tail, lanes), BF16),
            pltpu.VMEM(entry_other.shape, BF16),
            pltpu.VMEM(acts_other.shape, BF16),
            pltpu.SemaphoreType.DMA((peers, 2)),
            pltpu.SemaphoreType.DMA((2,)),
        ],
        compiler_params=limits(16),
        name="first_grads",
    )(core, *values, acts_other)


def packed_late(d_hidden, upstream, place):
    rows, half = d_hidden.shape
    features = upstream.shape[1]
    shard = features // PEERS
    tiles = half // LANES

    def body(place_ref, grad_ref, up_ref, *refs):
        outs = refs[:PEERS]
        turned_ref = refs[PEERS]
        for t in range(features // LANES):
            at = slice(t * LANES, (t + 1) * LANES)
            turned_ref[at, :] = up_ref[:, at].T
        for k in range(PEERS):
            for t in range(tiles):
                outs[k][t * rows : (t + 1) * rows, :] = grad_ref[:, t * LANES : (t + 1) * LANES]
            start = pl.multiple_of((place_ref[1] ^ k) * shard, 64)
            outs[k][tiles * rows :, :] = turned_ref[pl.ds(start, shard), :]

    shape = jax.ShapeDtypeStruct((tiles * rows + shard, rows), BF16)
    return pl.pallas_call(
        body,
        in_specs=[whole(pltpu.SMEM), whole(), whole()],
        out_specs=[whole()] * PEERS,
        out_shape=[shape] * PEERS,
        scratch_shapes=[pltpu.VMEM((features, rows), BF16)],
        compiler_params=limits(4),
        name="packed_late",
    )(place, d_hidden, upstream)


def last_grads(wide, other, late, place):
    peers, height, lanes = wide.shape
    shard = other.shape[1]
    half = 3 * lanes
    step = 2

    def body(place_ref, wide_ref, other_ref, *refs):
        late_refs = refs[:peers]
        out_ref, low_ref, stored_ref, acts_ref, swapped_ref, sems = refs[peers:]
        copies = []
        for k in range(peers):
            replica = place_ref[1] ^ k
            moves = [
                (wide_ref.at[replica, pl.ds(0, 2 * half)], stored_ref),
                (wide_ref.at[replica, pl.ds(height - shard, shard)], acts_ref),
                (other_ref.at[replica], swapped_ref),
            ]
            copies.append(
                [
                    pltpu.make_async_copy(source, target.at[k], sems.at[k, i])
                    for i, (source, target) in enumerate(moves)
                ]
            )
            for copy in copies[k]:
                copy.start()

        mine = place_ref[0] == 0
        for turn in range(peers // step):
            ks = range(step * turn, step * (turn + 1))
            for k in ks:
                for copy in copies[k]:
                    copy.wait()

            def over(ref, base):
                return jnp.concatenate([tiled(ref, k, base, lanes) for k in ks], axis=0)

            grad = jnp.concatenate(
                [
                    jnp.concatenate(
                        [late_refs[k][t * lanes : (t + 1) * lanes, :] for t in range(3)], axis=1
                    )
                    for k in ks
                ],
                axis=0,
            )
            add_grads(
                out_ref,
                low_ref,
                turn,
                peers // step,
                over(stored_ref, 0),
                over(stored_ref, half),
                grad,
                jnp.concatenate(
                    [jnp.where(mine, acts_ref[k], swapped_ref[k]) for k in ks], axis=1
                ),
                jnp.concatenate([late_refs[k][half:, :] for k in ks], axis=1),
            )

    shape = (3, shard, half)
    return pl.pallas_call(
        body,
        in_specs=[whole(pltpu.SMEM), whole(pl.ANY), whole(pl.ANY)] + [whole()] * peers,
        out_specs=[whole()] * 2,
        out_shape=[jax.ShapeDtypeStruct(shape, F32), jax.ShapeDtypeStruct(shape, BF16)],
        scratch_shapes=[
            pltpu.VMEM((peers, 2 * half, lanes), BF16),
            pltpu.VMEM((peers, shard, lanes), BF16),
            pltpu.VMEM((peers, shard, lanes), BF16),
            pltpu.SemaphoreType.DMA((peers, 3)),
        ],
        compiler_params=limits(16),
        name="last_grads",
    )(place, *[pltpu.with_memory_space_constraint(v, pltpu.HBM) for v in (wide, other)], *late)


def early_out(own_0, own_1, got_1, core):
    count, shard, half = own_0.shape

    def body(core_ref, own_0_ref, own_1_ref, got_1_ref, *outs):
        @pl.when(core_ref[0] == 0)
        def _():
            for i in range(count):
                outs[i][:, :half] = own_0_ref[i]

        @pl.when(core_ref[0] != 0)
        def _():
            for i in range(count):
                outs[i][:, :half] = got_1_ref[i].astype(F32)
                outs[i][:, half:] = own_1_ref[i]

    shape = jax.ShapeDtypeStruct((shard, half * CORES), F32)
    return pl.pallas_call(
        body,
        in_specs=[whole(pltpu.SMEM)] + [whole()] * 3,
        out_specs=[whole()] * count,
        out_shape=[shape] * count,
        compiler_params=limits(8),
        name="early_out",
    )(core, own_0, own_1, got_1)


def late_out(outs, got_0, core):
    count, shard, half = got_0.shape

    def body(core_ref, got_ref, *refs):
        wide_ref, sems = refs[-2:]
        targets = refs[count : 2 * count]

        @pl.when(core_ref[0] == 0)
        def _():
            copies = []
            for i in range(count):
                wide_ref[i] = got_ref[i].astype(F32)
                copy = pltpu.make_async_copy(
                    wide_ref.at[i], targets[i].at[:, half:], sems.at[i]
                )
                copy.start()
                copies.append(copy)
            for copy in copies:
                copy.wait()

    return pl.pallas_call(
        body,
        in_specs=[whole(pltpu.SMEM), whole()] + [whole(pl.ANY)] * count,
        out_specs=[whole(pl.ANY)] * count,
        out_shape=[jax.ShapeDtypeStruct(o.shape, o.dtype) for o in outs],
        scratch_shapes=[
            pltpu.VMEM((count, shard, half), F32),
            pltpu.SemaphoreType.DMA((count,)),
        ],
        input_output_aliases={2 + i: i for i in range(count)},
        compiler_params=limits(8),
        name="late_out",
    )(core, got_0, *outs)


def crossing(partial, residual, source, core, x, core_id, x_id):
    width = partial.shape[1] // XS
    split = partial.shape[0] // CORES
    own = columns_at(partial, x, width)
    pieces = fanned(lambda k: columns_at(partial, x ^ k, width), "x")

    total = own.astype(F32)
    for piece in pieces:
        total = total + piece.astype(F32)
    summed = lax.optimization_barrier(total.astype(BF16))
    halves = [summed[:split], summed[split:]]
    received = one_way(halves[1 - source], source)
    mine = jnp.where(core == source, halves[source], received)
    pieces = fanned(lambda k: mine, "zh")
    total = mine.astype(F32)
    for piece in pieces:
        total = total + piece.astype(F32)
    out = (residual.astype(F32) + total).astype(BF16)
    blocks = [out] + fanned(lambda k: out, "x")
    gathered = assemble(blocks, x_id)
    other = shifted(gathered, "segment", 1)
    return merge(gathered, other, core_id)


def local(tokens, w_gate, w_up, w_down, cotangent):
    return step(tokens, w_gate[0], w_up[0], w_down[0], cotangent)


def step(tokens, gate_w, up_w, down_w, cotangent):
    core = lax.axis_index("segment")
    x = lax.axis_index("x")
    core_id = core.astype(jnp.int32)[None]
    x_id = x.astype(jnp.int32)[None]
    place = jnp.stack([core, lax.axis_index(DP)]).astype(jnp.int32)
    rows = tokens.shape[0]
    features, hidden = gate_w.shape
    half = hidden // CORES

    lent = one_way(down_w[half:], 0)
    down_half = lax.optimization_barrier(jnp.where(core == 0, down_w[:half], lent))
    own = spread(tokens.T, cotangent.T, core_id)
    gathered = exchanged(own, TENSOR)
    entered = gathered.reshape(features, rows)

    gate_a = dot_tn(entered, gate_w).astype(BF16)
    up_a = dot_tn(entered, up_w).astype(BF16)
    hidden_a = hidden_of(gate_a, up_a)
    partial_a = dot_nn(hidden_a, down_w).astype(BF16)
    block = lax.dynamic_slice_in_dim(entered, x * (features // XS), features // XS, 0).T
    first, second = block[: rows // CORES], block[rows // CORES :]
    other = shifted(jnp.where(core == 0, second, first), "segment", 1)
    residual_1 = jnp.where(core == 0, first, other)
    residual_2 = jnp.where(core == 0, other, second)
    middle = crossing(partial_a, residual_1, 0, core, x, core_id, x_id)

    d_hidden_a = lax.dot_general(
        entered, down_w, (((0,), (1,)), ((), ())), preferred_element_type=F32
    ).astype(BF16)
    d_hidden_a = lax.optimization_barrier(d_hidden_a)
    outgoing = picked([[(gate_a, 1), (up_a, 1)], [(d_hidden_a, 0)]], core_id)
    given = shifted(outgoing, "segment", 1)
    load = packed(
        [(gate_a, 0, 0), (up_a, 0, 1), (d_hidden_a, 1, 0)], given, entered, core_id
    )
    wide = exchanged(load, DP)

    wide_a = wide
    entered_other = shifted(wide[:, 3 * half :], "segment", 1)

    gate_b = dot_nn(middle, gate_w).astype(BF16)
    up_b = dot_nn(middle, up_w).astype(BF16)
    d_gate_b, d_up_b = gate_grads(d_hidden_a.astype(F32), gate_b, up_b)
    partial_b = (dot_nt(d_gate_b, gate_w) + dot_nt(d_up_b, up_w)).astype(BF16)
    upstream = crossing(partial_b, residual_2, 1, core, x, core_id, x_id)

    picks = [(gate_b, 0), (up_b, 0)]
    outgoing = picked([picks, picks], core_id)
    given = one_way(outgoing, 1)
    load = packed([(gate_b, 1, 0), (up_b, 1, 1)], given, (middle,), core_id, True)
    load, wide_a = lax.optimization_barrier((load, wide_a))
    wide_b = exchanged(load, DP)

    d_hidden_b = dot_nt(upstream, down_half).astype(BF16)
    late = list(packed_late(d_hidden_b, upstream, place))
    for k in range(1, PEERS):
        late[k] = traded(late[k], DP, k)

    middle_other = shifted(wide_b[:, 2 * half :], "segment", 1)
    own_1, low_1 = first_grads(wide_b, wide_a, entered_other, middle_other, core_id)
    got_1 = one_way(low_1, 0)
    own_0, low_0 = last_grads(wide_a, entered_other, late, place)
    got_0 = one_way(low_0, 1)
    outs = early_out(own_0, own_1, got_1, core_id)
    grad_gate, grad_up, grad_down = late_out(outs, got_0, core_id)
    return (grad_gate[None], grad_up[None], grad_down.T[None])


def solution(mesh):
    fine = Mesh(
        mesh.devices.reshape(CORES, XS, ZH, ZL, YS), ("segment", "x", "zh", "zl", "y")
    )
    in_specs = (
        P(DP, TENSOR),
        P("segment", None, TENSOR),
        P("segment", None, TENSOR),
        P("segment", TENSOR, None),
        P(DP, TENSOR),
    )
    out_specs = (
        P("segment", DP, TENSOR),
        P("segment", DP, TENSOR),
        P("segment", TENSOR, DP),
    )
    return jax.shard_map(
        local, mesh=fine, in_specs=in_specs, out_specs=out_specs, check_vma=False
    )
```
